256 devices in a mesh: ent: 64 (over z, x, core), basis: 4 (over y).
Axes of the slice: x: 4, y: 4, z: 8, core: 2. Of those that a mesh axis runs over, the one named last changes fastest.
Arguments:
- entity_rows: bfloat16 [32768, 256], P('ent'), may hold values from -6 to 6
- self_weight: bfloat16 [256, 256], replicated, may hold values from -0.375 to 0.375
- bases: bfloat16 [32, 256, 256], P('basis'), may hold values from -0.375 to 0.375
- coefficients: float32 [1315, 32], P(None, 'basis'), may hold values from -1 to 1
- send_block: int32 [64, 64, 2], P('ent'), may hold values from 0 to 3
- edge_rel: int32 [64, 64, 2], P('ent'), may hold values from 0 to 1314
- edge_dst: int32 [64, 64, 2], P(None, 'ent'), may hold values from 0 to 3
- edge_count: int32 [64, 64, 2], P(None, 'ent'), may hold values from 0 to 128, as said below
- cotangent: bfloat16 [32768, 256], P('ent'), may hold values from -0.75 to 0.75
Outputs:
- activation: bfloat16 [32768, 256], P('ent', 'basis')
- basis_grad: float32 [32, 256, 256], P('basis', 'ent')
- coef_grad: float32 [1315, 32], P(None, 'basis')
- entity_grad: bfloat16 [32768, 256], P('ent', 'basis')
The draws below stay inside these ranges and needn't reach their ends.
Inputs may be any that keep to these rules, and one draw needn't show every extreme that they name: `edge_count`: 0 marks an empty slot; every draw has slots with all 128 rows live.
All inputs are finite; a program needn't handle non-finite values.
Results may differ from the reference program's by a relative error of at most 0.015.
Values may be sent and summed in bfloat16 or wider, within the bound.
No kernel may reach another device: no remote copies, remote signals or barrier semaphores. Data moves between devices by JAX's collectives and lax.ppermute only.
A program may use at most 128 MiB of HBM per device.

```python
import math
import jax
import jax.numpy as jnp
import numpy as np
from jax import lax

D = 256
B = 32
R = 1315
BLK = 128
CAP = 2
ENT_DEV = 512
NBLK = 4
PEERS = 64
ENTITIES = 32768


def draw_edge_count(key, part):
    key_chosen = jax.random.fold_in(key, 11)
    key_counts = jax.random.fold_in(key, 12)
    shape_slots = (PEERS, PEERS, CAP)
    chosen = jax.random.randint(key_chosen, shape_slots, 0, 10) < 7
    counts = jax.random.randint(key_counts, shape_slots, 1, BLK + 1)
    sender = lax.broadcasted_iota(jnp.int32, shape_slots, 0)
    receiver = lax.broadcasted_iota(jnp.int32, shape_slots, 1)
    slot_index = lax.broadcasted_iota(jnp.int32, shape_slots, 2)
    forced = (receiver == (sender + 1) % PEERS) & (slot_index == 0)
    return jnp.where(forced, BLK, jnp.where(chosen, counts, 0)).astype(jnp.int32)


def place_ends(drawn, own_key, low, largest):
    longest = drawn.shape.index(max(drawn.shape))
    spots = []
    for shift in (0, 1):
        where = [jax.random.randint(jax.random.fold_in(own_key, axis), (), 0, length) for axis, length in enumerate(drawn.shape)]
        where[longest] = (where[longest] + shift) % drawn.shape[longest]
        spots.append(tuple(where))
    return drawn.at[spots[0]].set(low).at[spots[1]].set(largest)


def level_of(stream_key, shape, pieces, smallest, high):
    loudness, own = 1.0, jax.random.fold_in(stream_key, 6)
    for axis_at, blocks in pieces:
        steps = jnp.exp(jax.random.uniform(jax.random.fold_in(own, axis_at), (blocks,), jnp.float32, smallest / len(pieces), high / len(pieces)))
        loudness = loudness * jnp.repeat(steps, shape[axis_at] // blocks).reshape([-1 if axis == axis_at else 1 for axis in range(len(shape))])
    return loudness


def rank_table(number_of, slope):
    weights = [(1 << 20) // math.isqrt(rank ** slope) + 1 for rank in range(1, number_of + 1)]
    deviation = 1 + sum(weights) // (1 << 30)
    return np.cumsum(np.array([max(1, weight // deviation) for weight in weights]))


def skewed_ids(key, dims, amount, slope):
    table = rank_table(amount, slope)
    ticket = jax.random.randint(jax.random.fold_in(key, 1), dims, 0, int(table[amount - 1]))
    grade = jnp.searchsorted(jnp.asarray(table, jnp.int32), ticket, side="right")
    return jax.random.permutation(jax.random.fold_in(key, 2), amount)[grade].astype(jnp.int32)


def gaussian(stream_key, extent, scale, bound, cuts=(), kind=jnp.bfloat16):
    result = scale * jax.random.normal(stream_key, extent, jnp.float32)
    if cuts:
        result = result * level_of(stream_key, extent, cuts, -0.22, 0.18)
    return jnp.clip(result, -bound, bound).astype(kind)


def setup_inputs(seed: int = 0) -> dict:
    key_list = jax.random.split(jax.random.key(seed), 10)
    entity_rows = gaussian(key_list[0], (ENTITIES, D), 1.0, 6.0, ((0, 64),))
    self_weight = gaussian(key_list[1], (D, D), D ** -0.5, 0.375)
    bases = gaussian(key_list[2], (B, D, D), D ** -0.5, 0.375, ((0, 4),))
    coefficients = gaussian(key_list[3], (R, B), B ** -0.5, 1.0, ((1, 4),), jnp.float32)
    send_block = place_ends(jax.random.randint(key_list[4], (PEERS, PEERS, CAP), 0, NBLK), jax.random.fold_in(key_list[4], 1), 0, NBLK - 1).astype(jnp.int32)
    edge_rel = place_ends(jax.random.randint(key_list[5], (PEERS, PEERS, CAP), 0, R), jax.random.fold_in(key_list[5], 1), 0, R - 1).astype(jnp.int32)
    edge_dst = place_ends(skewed_ids(key_list[6], (PEERS, PEERS, CAP), NBLK, 2), jax.random.fold_in(key_list[6], 3), 0, NBLK - 1).astype(jnp.int32)
    edge_count = draw_edge_count(jax.random.fold_in(key_list[9], 71), 0)
    cotangent = gaussian(key_list[8], (ENTITIES, D), 0.125, 0.75, ((0, 64),))
    return {"entity_rows": entity_rows, "self_weight": self_weight, "bases": bases, "coefficients": coefficients, "send_block": send_block, "edge_rel": edge_rel, "edge_dst": edge_dst, "edge_count": edge_count, "cotangent": cotangent}


def silu_parts(values):
    logistic = jax.nn.sigmoid(values)
    return values * logistic, logistic * (1.0 + values * (1.0 - logistic))


def reference(entity_rows, self_weight, bases, coefficients, send_block, edge_rel, edge_dst, edge_count, cotangent):
    coef_bf = lax.optimization_barrier(coefficients.astype(jnp.bfloat16)).astype(jnp.float32)
    all_blocks = entity_rows.reshape(PEERS * NBLK, BLK, D)
    basis_full = bases.astype(jnp.float32)
    row_iota = jnp.arange(BLK, dtype=jnp.int32)
    peer_ids = jnp.arange(PEERS, dtype=jnp.int32)
    block_ids = jnp.arange(NBLK, dtype=jnp.int32)
    relation_ids = jnp.arange(R, dtype=jnp.int32)

    def forward_step(running, target_peer):
        sources = peer_ids[:, None] * NBLK + send_block[:, target_peer, :]
        received = all_blocks[sources.reshape(-1)].astype(jnp.float32)
        live_rows = (row_iota[None, None, :] < edge_count[:, target_peer, :][:, :, None]).reshape(-1, BLK)
        received = received * live_rows[:, :, None].astype(jnp.float32)
        weights = coef_bf[edge_rel[:, target_peer, :].reshape(-1)]
        target_hot = (edge_dst[:, target_peer, :].reshape(-1)[:, None] == block_ids[None, :]).astype(jnp.float32)
        messages = jnp.einsum('sk,sb,srd->kbrd', target_hot, weights, received).astype(jnp.bfloat16)
        message_full = messages.astype(jnp.float32)
        aggregate = jnp.einsum('kbrd,bde->kre', message_full, basis_full).reshape(ENT_DEV, D)
        own_rows = lax.dynamic_slice_in_dim(entity_rows, target_peer * ENT_DEV, ENT_DEV, 0)
        pre_act = jnp.dot(own_rows, self_weight, preferred_element_type=jnp.float32) + aggregate
        activated, slope_value = silu_parts(pre_act)
        own_cot = lax.dynamic_slice_in_dim(cotangent, target_peer * ENT_DEV, ENT_DEV, 0).astype(jnp.float32)
        pre_grad = (own_cot * slope_value).astype(jnp.bfloat16)
        grad_blocks = pre_grad.astype(jnp.float32).reshape(NBLK, BLK, D)
        basis_term = jnp.einsum('kbrd,kre->bde', message_full, grad_blocks)
        return running + basis_term, (activated.astype(jnp.bfloat16), pre_grad)

    basis_grad, (activations, gradients) = lax.scan(forward_step, jnp.zeros((B, D, D), jnp.float32), peer_ids)
    activation = activations.reshape(ENTITIES, D)
    pre_grad_all = gradients.reshape(ENTITIES, D)
    gradient_blocks = pre_grad_all.reshape(PEERS * NBLK, BLK, D)
    weight_full = self_weight.astype(jnp.float32)

    def backward_step(running, source_peer):
        targets = peer_ids[:, None] * NBLK + edge_dst[source_peer]
        back_blocks = gradient_blocks[targets.reshape(-1)].astype(jnp.float32)
        live_rows = (row_iota[None, None, :] < edge_count[source_peer][:, :, None]).reshape(-1, BLK)
        back_blocks = back_blocks * live_rows[:, :, None].astype(jnp.float32)
        relations = edge_rel[source_peer].reshape(-1)
        weights = coef_bf[relations]
        source_hot = (send_block[source_peer].reshape(-1)[:, None] == block_ids[None, :]).astype(jnp.float32)
        returned = jnp.einsum('sk,sb,sre->kbre', source_hot, weights, back_blocks).astype(jnp.bfloat16)
        own_rows = lax.dynamic_slice_in_dim(entity_rows, source_peer * ENT_DEV, ENT_DEV, 0).astype(jnp.float32)
        projected = jnp.einsum('nd,bde->bne', own_rows, basis_full).astype(jnp.bfloat16)
        proj_blocks = projected.astype(jnp.float32).reshape(B, NBLK, BLK, D)
        scores = jnp.einsum('sre,bkre->sbk', back_blocks, proj_blocks)
        per_slot = jnp.einsum('sbk,sk->sb', scores, source_hot)
        relation_hot = (relations[:, None] == relation_ids[None, :]).astype(jnp.float32)
        coef_term = jnp.dot(relation_hot.T, per_slot, precision=lax.Precision.HIGHEST)
        own_grad = lax.dynamic_slice_in_dim(pre_grad_all, source_peer * ENT_DEV, ENT_DEV, 0).astype(jnp.float32)
        back_part = jnp.einsum('kbre,bde->krd', returned.astype(jnp.float32), basis_full).reshape(ENT_DEV, D)
        entity_grad = jnp.dot(own_grad, weight_full.T) + back_part
        return running + coef_term, entity_grad.astype(jnp.bfloat16)

    coef_grad, entity_grads = lax.scan(backward_step, jnp.zeros((R, B), jnp.float32), peer_ids)
    return activation, basis_grad, coef_grad, entity_grads.reshape(ENTITIES, D)
```

```python
import functools

import jax
import jax.numpy as jnp
from jax import lax
from jax.experimental import pallas as pl
from jax.experimental.pallas import tpu as pltpu
from jax.sharding import PartitionSpec as P

BLK = 128
BF = jnp.bfloat16
F32 = jnp.float32
NT = (((1,), (1,)), ((), ()))
TN = (((0,), (0,)), ((), ()))
LIMIT = 56 * 1024 * 1024
VM = pl.BlockSpec(memory_space=pltpu.VMEM)
SM = pl.BlockSpec(memory_space=pltpu.SMEM)


def call(body, outs, ins, scratch=()):
    return pl.pallas_call(
        body,
        out_shape=outs,
        in_specs=ins,
        out_specs=jax.tree.map(lambda _: VM, outs),
        scratch_shapes=list(scratch),
        compiler_params=pltpu.CompilerParams(vmem_limit_bytes=LIMIT),
    )


def take_body(share, idx_ref, g_ref, ent_ref, out_ref):
    first = g_ref[0] * share
    for s in range(out_ref.shape[0]):
        row = pl.multiple_of(idx_ref[s] * BLK + first, share)
        out_ref[s] = ent_ref[pl.ds(row, share), :]


def get(ref, at):
    return jnp.concatenate([ref[h, at, :] for h in range(ref.shape[0])], axis=1)


def put(ref, at, value):
    for h in range(ref.shape[0]):
        ref[h, at, :] = value[:, h * 128 : (h + 1) * 128]


def rows_scratch(rows, width):
    return pltpu.VMEM((width // 128, rows, 128), F32)


def slot_weights(table_ref, rel_ref, block_ref, nblk, base_rows, pad):
    chunks = (table_ref.shape[1] - base_rows) // pad
    width = table_ref.shape[2]
    slots = rel_ref.shape[1]
    groups = table_ref.shape[0]
    rel = rel_ref[...]
    parts = [jnp.zeros((pad, slots), F32) for _ in range(groups)]
    for j in range(chunks):
        ids = lax.broadcasted_iota(jnp.int32, (width, slots), 0) + j * width
        hot = jnp.where(ids == rel, 1.0, 0.0).astype(BF)
        for g in range(groups):
            rows = table_ref[g, pl.ds(base_rows + j * pad, pad), :]
            parts[g] += jnp.dot(rows, hot, preferred_element_type=F32)
    coef = jnp.concatenate([p[:8] for p in parts], axis=0)
    blk = block_ref[...]
    return jnp.concatenate([jnp.where(blk == n, coef, 0.0) for n in range(nblk)], axis=0)


def spread(x_ref, w, cnt_ref, first, xf, mf, xr_ref):
    slots = cnt_ref.shape[1]
    share = x_ref.shape[0] // slots
    step = 512

    def widen(i, c):
        at = pl.ds(pl.multiple_of(i * step, step), step)
        put(xf, at, x_ref[at, :].astype(F32))
        return c

    lax.fori_loop(0, x_ref.shape[0] // step, widen, 0)
    cnt = cnt_ref[...]

    def one(k, c):
        at = pl.ds(k, slots, stride=share)
        xk = get(xf, at).astype(BF)
        if xr_ref is not None:
            xr_ref[k] = xk
        wk = jnp.where(cnt > first + k, w, 0.0).astype(BF)
        put(mf, pl.ds(k, w.shape[0], stride=share), jnp.dot(wk, xk, preferred_element_type=F32))
        return c

    lax.fori_loop(0, share, one, 0, unroll=4)


def rows_of(mf, base, nbase, nblk, share):
    return jnp.concatenate(
        [get(mf, pl.ds((n * nbase + base) * share, share)) for n in range(nblk)], axis=0
    )


def own_rows(ref, first, nblk, share):
    return jnp.concatenate(
        [ref[pl.ds(pl.multiple_of(n * BLK + first, share), share), :] for n in range(nblk)], axis=0
    )


def fwd_body(
    nbase, nblk, pad, g_ref, dst_ref, x_ref, rel_ref, dstv_ref, cnt_ref, table_ref, ent_ref, sw_ref,
    cot_ref, y_ref, back_ref, xr_ref, pg_ref, xf, mf,
):
    groups = y_ref.shape[0]
    own = nbase // groups
    width = table_ref.shape[2]
    share = BLK // groups
    first = g_ref[0] * share
    w = slot_weights(table_ref, rel_ref, dstv_ref, nblk, own * width, pad)
    spread(x_ref, w, cnt_ref, first, xf, mf, xr_ref)
    acc = jnp.dot(own_rows(ent_ref, first, nblk, share), sw_ref[...], preferred_element_type=F32)
    for b in range(nbase):
        mb = rows_of(mf, b, nbase, nblk, share).astype(BF)
        y_ref[b // own, b % own] = mb
        acc += jnp.dot(mb, table_ref[b // own, pl.ds((b % own) * width, width), :], preferred_element_type=F32)
    s = jax.nn.sigmoid(acc)
    act = (acc * s).astype(BF)
    cot = own_rows(cot_ref, first, nblk, share).astype(F32)
    pg = (cot * (s * (1.0 + acc * (1.0 - s)))).astype(BF)
    pg_ref[...] = pg
    for g in range(groups):
        y_ref[g, own] = pg
        y_ref[g, own + 1] = act
    for i in range(back_ref.shape[0]):
        back_ref[i] = pg_ref[pl.ds(pl.multiple_of(dst_ref[i] * share, share), share), :]


def score_body(
    nbase, nblk, g_ref, xr_ref, pg_ref, dstv_ref, cnt_ref, relf_ref, table_ref, out_ref, pf
):
    groups = table_ref.shape[0]
    own = nbase // groups
    width = table_ref.shape[2]
    share = xr_ref.shape[0]
    slots = xr_ref.shape[1]
    first = g_ref[0] * share
    pg = pg_ref[...]
    for b in range(nbase):
        base = table_ref[b // own, pl.ds((b % own) * width, width), :]
        p = lax.dot_general(pg, base, NT, preferred_element_type=F32)
        for n in range(nblk):
            put(pf, pl.ds((n * nbase + b) * share, share), p[n * share : (n + 1) * share])
    cnt = cnt_ref[...]

    def one(k, acc):
        pk = get(pf, pl.ds(k, nblk * nbase, stride=share)).astype(BF)
        t = lax.dot_general(pk, xr_ref[k], NT, preferred_element_type=F32)
        return acc + jnp.where(cnt > first + k, t, 0.0)

    acc = lax.fori_loop(0, share, one, jnp.zeros((nblk * nbase, slots), F32), unroll=4)
    blk = dstv_ref[...]
    total = jnp.zeros((nbase, slots), F32)
    for n in range(nblk):
        total += jnp.where(blk == n, acc[n * nbase : (n + 1) * nbase], 0.0)
    for g in range(groups):
        out_ref[g] = total[g * own : (g + 1) * own]


def bwd_body(
    nbase, nblk, pad, g_ref, x_ref, rel_ref, srcv_ref, cnt_ref, table_ref, pg_ref, sw_ref, out_ref, xf, mf
):
    groups = table_ref.shape[0]
    own = nbase // groups
    width = table_ref.shape[2]
    share = BLK // groups
    first = g_ref[0] * share
    w = slot_weights(table_ref, rel_ref, srcv_ref, nblk, own * width, pad)
    spread(x_ref, w, cnt_ref, first, xf, mf, None)
    acc = lax.dot_general(pg_ref[...], sw_ref[...], NT, preferred_element_type=F32)
    for b in range(nbase):
        mb = rows_of(mf, b, nbase, nblk, share).astype(BF)
        base = table_ref[b // own, pl.ds((b % own) * width, width), :]
        acc += lax.dot_general(mb, base, NT, preferred_element_type=F32)
    cols = width // groups
    for g in range(groups):
        out_ref[g] = acc[:, g * cols : (g + 1) * cols].astype(BF)


def basis_body(peers, y_ref, out_ref, tmp, outf):
    groups = y_ref.shape[0]
    own = y_ref.shape[1] - 2
    width = y_ref.shape[3]
    deep = width // peers
    pg = jnp.concatenate([y_ref[g, own] for g in range(groups)], axis=0)
    for b in range(own):
        m = jnp.concatenate([y_ref[g, b] for g in range(groups)], axis=0)
        put(tmp, pl.ds(0, width), lax.dot_general(m, pg, TN, preferred_element_type=F32))
        for d in range(deep):
            put(outf, pl.ds(b * deep + d, peers, stride=own * deep), get(tmp, pl.ds(d, peers, stride=deep)))
    out_ref[...] = get(outf, pl.ds(0, out_ref.shape[0])).astype(BF)


def coef_body(own, in_ref, out_ref):
    peers, _, slots = in_ref.shape
    wide = out_ref.shape[1]

    def one(p, acc):
        blk = in_ref[p]
        score = blk[:own]
        rel = blk[own : own + 1].astype(jnp.int32)
        high = score.astype(BF)
        low = (score - high.astype(F32)).astype(BF)
        ids = lax.broadcasted_iota(jnp.int32, (wide, slots), 0)
        hot = jnp.where(ids == rel, 1.0, 0.0).astype(BF)
        both = jnp.concatenate([high.astype(F32), low.astype(F32)], axis=0).astype(BF)
        return acc + lax.dot_general(both, hot, NT, preferred_element_type=F32)

    acc = lax.fori_loop(0, peers, one, jnp.zeros((2 * own, wide), F32))
    out_ref[...] = acc[:own] + acc[own:]


def local(
    entity_rows,
    self_weight,
    bases,
    coefficients,
    send_block,
    edge_rel,
    edge_dst,
    edge_count,
    cotangent,
):
    peers = lax.axis_size("ent")
    groups = lax.axis_size("basis")
    ent_dev, width = entity_rows.shape
    nblk = ent_dev // BLK
    own = bases.shape[0]
    nbase = own * groups
    relations = coefficients.shape[0]
    cap = send_block.shape[2]
    slots = peers * cap
    share = BLK // groups
    pad = 16
    group = lax.axis_index("basis")
    g = group.reshape(1).astype(jnp.int32)

    src = send_block[0].reshape(slots)
    dst = edge_dst[:, 0, :].reshape(slots)
    rel_out = edge_rel[0].reshape(1, slots)
    cnt_in = edge_count[:, 0, :].reshape(1, slots)

    outgoing = call(
        functools.partial(take_body, share),
        jax.ShapeDtypeStruct((slots, share, width), BF),
        [SM, SM, VM],
    )(src, g, entity_rows)
    incoming = lax.all_to_all(
        outgoing.reshape(peers, cap * share, width), "ent", split_axis=0, concat_axis=0, tiled=True
    )
    notes = jnp.concatenate([edge_rel[0], edge_count[:, 0, :]], axis=1)
    notes = lax.all_to_all(notes, "ent", split_axis=0, concat_axis=0, tiled=True)
    rel_in = notes[:, :cap].reshape(1, slots)
    cnt_out = notes[:, cap:].reshape(1, slots)

    chunks = -(-relations // width)
    coef = jnp.pad(coefficients.astype(BF).T, ((0, pad - own), (0, chunks * width - relations)))
    coef = coef.reshape(pad, chunks, width).transpose(1, 0, 2).reshape(chunks * pad, width)
    table = lax.all_gather(
        jnp.concatenate([bases.reshape(own * width, width), coef], axis=0), "basis"
    )

    dstv, srcv = dst.reshape(1, slots), src.reshape(1, slots)
    y, back, xr, pg = call(
        functools.partial(fwd_body, nbase, nblk, pad),
        (
            jax.ShapeDtypeStruct((groups, own + 2, nblk * share, width), BF),
            jax.ShapeDtypeStruct((slots, share, width), BF),
            jax.ShapeDtypeStruct((share, slots, width), BF),
            jax.ShapeDtypeStruct((nblk * share, width), BF),
        ),
        [SM, SM] + [VM] * 8,
        [rows_scratch(slots * share, width), rows_scratch(nblk * nbase * share, width)],
    )(
        g, dst, incoming.reshape(slots * share, width), rel_in, dstv, cnt_in, table,
        entity_rows, self_weight, cotangent,
    )

    returned = lax.all_to_all(
        back.reshape(peers, cap * share, width), "ent", split_axis=0, concat_axis=0, tiled=True
    )
    shared = lax.all_to_all(y, "basis", split_axis=0, concat_axis=0, tiled=True)

    score = call(
        functools.partial(score_body, nbase, nblk),
        jax.ShapeDtypeStruct((groups, own, slots), F32),
        [SM] + [VM] * 6,
        [rows_scratch(nblk * nbase * share, width)],
    )(g, xr, pg, dstv, cnt_in, rel_in, table)
    score = lax.all_to_all(score, "basis", split_axis=0, concat_axis=0, tiled=True)
    score = jnp.concatenate(
        [jnp.sum(score, axis=0), jnp.broadcast_to(rel_in.astype(F32), (8, slots))], axis=0
    )
    scores = lax.all_to_all(
        jnp.broadcast_to(score[None], (peers,) + score.shape), "ent", split_axis=0, concat_axis=0, tiled=True
    )
    wide = -(-relations // 128) * 128
    coef_grad = call(
        functools.partial(coef_body, own), jax.ShapeDtypeStruct((own, wide), F32), [VM]
    )(scores)[:, :relations].T

    activation = lax.dynamic_slice_in_dim(shared[:, own + 1], group * (width // groups), width // groups, 2)
    activation = activation.reshape(groups, nblk, share, width // groups).transpose(1, 0, 2, 3)
    activation = activation.reshape(ent_dev, width // groups)

    deep = width // peers
    term = call(
        functools.partial(basis_body, peers),
        jax.ShapeDtypeStruct((peers * own * deep, width), BF),
        [VM],
        [rows_scratch(width, width), rows_scratch(peers * own * deep, width)],
    )(shared)
    term = lax.all_to_all(
        term.reshape(peers, own * deep, width), "ent", split_axis=0, concat_axis=0, tiled=True
    )
    basis_grad = jnp.sum(term.astype(F32), axis=0).reshape(own, deep, width)

    grad = call(
        functools.partial(bwd_body, nbase, nblk, pad),
        jax.ShapeDtypeStruct((groups, nblk * share, width // groups), BF),
        [SM] + [VM] * 7,
        [rows_scratch(slots * share, width), rows_scratch(nblk * nbase * share, width)],
    )(g, returned.reshape(slots * share, width), rel_out, srcv, cnt_out, table, pg, self_weight)
    grad = lax.all_to_all(grad, "basis", split_axis=0, concat_axis=0, tiled=True)
    grad = grad.reshape(groups, nblk, share, width // groups).transpose(1, 0, 2, 3)
    entity_grad = grad.reshape(ent_dev, width // groups)
    return (activation, basis_grad, coef_grad, entity_grad)


def solution(mesh):
    placed = (
        P("ent", None),
        P(),
        P("basis", None, None),
        P(None, "basis"),
        P("ent", None, None),
        P("ent", None, None),
        P(None, "ent", None),
        P(None, "ent", None),
        P("ent", None),
    )
    return jax.shard_map(
        local,
        mesh=mesh,
        in_specs=placed,
        out_specs=(P("ent", "basis"), P("basis", "ent", None), P(None, "basis"), P("ent", "basis")),
        check_vma=False,
    )
```

```python
import functools

import jax
import jax.numpy as jnp
from jax import lax
from jax.experimental import pallas as pl
from jax.experimental.pallas import tpu as pltpu
from jax.sharding import PartitionSpec as P

BLK = 128
LANES = 128
NX = 4
NC = 2
BF = jnp.bfloat16
F32 = jnp.float32
NT = (((1,), (1,)), ((), ()))
TN = (((0,), (0,)), ((), ()))
MIB = 1024 * 1024
VM = pl.BlockSpec(memory_space=pltpu.VMEM)
SM = pl.BlockSpec(memory_space=pltpu.SMEM)


def call(body, outs, ins, scratch=(), limit=16):
    return pl.pallas_call(
        body,
        out_shape=outs,
        in_specs=ins,
        out_specs=jax.tree.map(lambda _: VM, outs),
        scratch_shapes=list(scratch),
        compiler_params=pltpu.CompilerParams(vmem_limit_bytes=limit * MIB),
    )


def bf(*shape):
    return jax.ShapeDtypeStruct(shape, BF)


def get(ref, at):
    return jnp.concatenate([ref[h, at, :] for h in range(ref.shape[0])], axis=1)


def put(ref, at, value):
    for h in range(ref.shape[0]):
        ref[h, at, :] = value[:, h * LANES : (h + 1) * LANES]


def rows_scratch(rows, width):
    return pltpu.VMEM((width // LANES, rows, LANES), F32)


def turn(i, r, n):
    return lax.rem(i + r + n, n)


def aligned(i, size):
    return pl.ds(pl.multiple_of(i * size, size), size)


def digits(value):
    high = value.astype(BF)
    return high, (value - high.astype(F32)).astype(BF)


def take_body(share, pos_ref, idx_ref, rel_ref, ent_ref, out_ref):
    first = pos_ref[0] * share
    cap = idx_ref.shape[2]
    halves = ent_ref.shape[1] // LANES
    lane = lax.broadcasted_iota(jnp.int32, (8, LANES), 1)
    for q in range(out_ref.shape[0]):
        note = jnp.zeros((8, LANES), jnp.int32)
        for c in range(cap):
            row = pl.multiple_of(idx_ref[0, q, c] * BLK + first, share)
            block = ent_ref[pl.ds(row, share), :]
            for h in range(halves):
                out_ref[q, pl.ds((c * halves + h) * share, share), :] = block[:, h * LANES : (h + 1) * LANES]
            rel = rel_ref[0, q, c]
            note = jnp.where(lane == 2 * c, rel >> 8, note)
            note = jnp.where(lane == 2 * c + 1, rel & 255, note)
        out_ref[q, pl.ds(cap * halves * share, 8), :] = note.astype(F32).astype(BF)


def slot_weights(own, pos_ref, coef_refs, rel, blk, nblk, cs):
    groups = len(coef_refs)
    rows, width = coef_refs[0].shape
    chunks = rows // 16
    slots = rel.shape[1]
    parts = [jnp.zeros((16, slots), F32) for _ in coef_refs]
    for j in range(chunks):
        ids = lax.broadcasted_iota(jnp.int32, (width, slots), 0) + j * width
        hot = jnp.where(ids == rel, 1.0, 0.0).astype(BF)
        for r, ref in enumerate(coef_refs):
            parts[r] += jnp.dot(ref[pl.ds(j * 16, 16), :], hot, preferred_element_type=F32)
    for r in range(groups):
        cs[turn(pos_ref[0], -r, groups)] = parts[r][:own]
    coef = cs[...].reshape(groups * own, slots)
    return jnp.concatenate([jnp.where(blk == n, coef, 0.0) for n in range(nblk)], axis=0)


def widen(x_ref, xf):
    step = 512

    def some(i, c):
        at = aligned(i, step)
        xf[at, :] = x_ref[at, :].astype(F32)
        return c

    lax.fori_loop(0, x_ref.shape[0] // step, some, 0, unroll=2 if x_ref.shape[0] % 1024 == 0 else 1)


def slot_rows(xf, peers, cap, halves, share, k):
    per = xf.shape[0] // peers
    return jnp.concatenate(
        [
            jnp.concatenate(
                [xf[pl.ds((c * halves + h) * share + k, peers, stride=per), :] for h in range(halves)], axis=1
            )
            for c in range(cap)
        ],
        axis=0,
    )


def rows_of(mf, base, nbase, nblk, share):
    return jnp.concatenate([get(mf, aligned(n * nbase + base, share)) for n in range(nblk)], axis=0)


def own_rows(ref, first, nblk, share):
    return jnp.concatenate(
        [ref[pl.ds(pl.multiple_of(n * BLK + first, share), share), :] for n in range(nblk)], axis=0
    )


def fwd_body(
    cap, nblk, own, pos_ref, dst_ref, count_ref, x_ref, dstv_ref, cnt_ref, c0, c1, c2, c3, table_ref, ent_ref,
    sw_ref, cot_ref, y0, y1, y2, y3, back_ref, xr_ref, pg_ref, rel_ref, xf, mf, cs, at_ref,
):
    groups = table_ref.shape[0]
    nbase = groups * own
    width = table_ref.shape[2]
    halves = width // LANES
    share = BLK // groups
    peers = back_ref.shape[0]
    per = xf.shape[0] // peers
    first = pos_ref[0] * share
    widen(x_ref, xf)
    notes = xf[pl.ds(cap * halves * share, peers, stride=per), :].astype(BF)
    lane = lax.broadcasted_iota(jnp.int32, (8, LANES), 1)
    line = lax.broadcasted_iota(jnp.int32, (8, LANES), 0)
    pick = jnp.where(lane == 2 * line, 256.0, jnp.where(lane == 2 * line + 1, 1.0, 0.0)).astype(BF)
    rels = lax.dot_general(pick, notes, NT, preferred_element_type=F32).astype(jnp.int32)
    rel = jnp.concatenate([rels[c : c + 1] for c in range(cap)], axis=1)
    rel_ref[...] = rel
    w = slot_weights(own, pos_ref, (c0, c1, c2, c3), rel, dstv_ref[...], nblk, cs)
    cnt = cnt_ref[...]

    def one(k, c):
        xk = slot_rows(xf, peers, cap, halves, share, k).astype(BF)
        xr_ref[k] = xk
        wk = jnp.where(cnt > first + k, w, 0.0).astype(BF)
        put(mf, pl.ds(k, w.shape[0], stride=share), jnp.dot(wk, xk, preferred_element_type=F32))
        return c

    lax.fori_loop(0, share, one, 0, unroll=4)
    acc = jnp.dot(own_rows(ent_ref, first, nblk, share), sw_ref[...], preferred_element_type=F32)
    ys = (y0, y1, y2, y3)
    rows = nblk * share
    for r, y in enumerate(ys):
        group = turn(pos_ref[0], r, groups)
        for b in range(own):
            mb = rows_of(mf, group * own + b, nbase, nblk, share).astype(BF)
            y[pl.ds(b * rows, rows), :] = mb
            acc += jnp.dot(mb, table_ref[group, pl.ds(b * width, width), :], preferred_element_type=F32)
    s = jax.nn.sigmoid(acc)
    at_ref[...] = (acc * s).T
    cot = own_rows(cot_ref, first, nblk, share).astype(F32)
    pg = (cot * (s * (1.0 + acc * (1.0 - s)))).astype(BF)
    pg_ref[...] = pg
    cols = width // groups
    for r, y in enumerate(ys):
        y[pl.ds(own * rows, rows), :] = pg
        group = turn(pos_ref[0], r, groups)
        act = at_ref[aligned(group, cols), :].astype(BF)
        half = cols // halves
        for h in range(halves):
            y[pl.ds((own + 1) * rows, half), h * LANES : (h + 1) * LANES] = act[h * half : (h + 1) * half]
    k_of = lax.broadcasted_iota(jnp.int32, (share, width), 0) + first
    for q in range(peers):
        for c in range(cap):
            block = pg_ref[aligned(dst_ref[q, 0, c], share), :]
            block = jnp.where(k_of < count_ref[q, 0, c], block.astype(F32), 0.0).astype(BF)
            for h in range(halves):
                back_ref[q, pl.ds((c * halves + h) * share, share), :] = block[:, h * LANES : (h + 1) * LANES]


def score_body(nblk, own, pos_ref, xr_ref, pg_ref, dstv_ref, cnt_ref, table_ref, s0, s1, s2, s3, pf, ts):
    groups = table_ref.shape[0]
    nbase = groups * own
    width = table_ref.shape[2]
    share, slots = xr_ref.shape[:2]
    first = pos_ref[0] * share
    pg = pg_ref[...]
    for b in range(nbase):
        base = table_ref[b // own, pl.ds((b % own) * width, width), :]
        p = lax.dot_general(pg, base, NT, preferred_element_type=F32)
        for n in range(nblk):
            put(pf, pl.ds((n * nbase + b) * share, share), p[n * share : (n + 1) * share])
    cnt = cnt_ref[...]

    def one(k, acc):
        pk = get(pf, pl.ds(k, nblk * nbase, stride=share)).astype(BF)
        t = lax.dot_general(pk, xr_ref[k], NT, preferred_element_type=F32)
        return acc + jnp.where(cnt > first + k, t, 0.0)

    acc = lax.fori_loop(0, share, one, jnp.zeros((nblk * nbase, slots), F32), unroll=4)
    blk = dstv_ref[...]
    total = jnp.zeros((nbase, slots), F32)
    for n in range(nblk):
        total += jnp.where(blk == n, acc[n * nbase : (n + 1) * nbase], 0.0)
    ts[...] = total
    for r, out in enumerate((s0, s1, s2, s3)):
        out[...] = ts[aligned(turn(pos_ref[0], r, groups), own), :]


def coef_body(rel_ref, s0, s1, s2, s3, out_ref):
    own, slots = s0.shape
    width = out_ref.shape[1]
    chunks = out_ref.shape[0] // (2 * own)
    high, low = digits((s0[...] + s1[...]) + (s2[...] + s3[...]))
    both = jnp.concatenate([high.astype(F32), low.astype(F32)], axis=0).astype(BF)
    rel = rel_ref[...]
    parts = []
    for j in range(chunks):
        ids = lax.broadcasted_iota(jnp.int32, (width, slots), 0) + j * width
        hot = jnp.where(ids == rel, 1.0, 0.0).astype(BF)
        t = lax.dot_general(both, hot, NT, preferred_element_type=F32)
        parts.append(t[:own] + t[own:])
    pack(out_ref, 0, jnp.concatenate(parts, axis=0))


def pack(ref, at, value):
    high, low = digits(value)
    n = value.shape[0]
    ref[pl.ds(at, n), :] = high
    ref[pl.ds(at + n, n), :] = low


def unpack(ref, at, n):
    return ref[pl.ds(at, n), :].astype(F32) + ref[pl.ds(at + n, n), :].astype(F32)


def basis_body(own, rows, peers, pos_ref, y0, y1, y2, y3, coef_ref, keep_ref, send_ref, tmp, outf):
    ys = (y0, y1, y2, y3)
    width = y0.shape[1]
    part = keep_ref.shape[0]
    each = part // NX
    deep = part * NC // (own * peers)
    nz = each // (own * deep)
    pg = jnp.concatenate([y[pl.ds(own * rows, rows), :] for y in ys], axis=0)
    for b in range(own):
        m = jnp.concatenate([y[pl.ds(b * rows, rows), :] for y in ys], axis=0)
        put(tmp, pl.ds(0, width), lax.dot_general(m, pg, TN, preferred_element_type=F32))
        for c in range(NC):
            for x in range(NX):
                for d in range(deep):
                    put(
                        outf,
                        pl.ds((c * NX + x) * each + b * deep + d, nz, stride=own * deep),
                        get(tmp, pl.ds((x * NC + c) * deep + d, nz, stride=NX * NC * deep)),
                    )
    keep_ref[...] = get(outf, aligned(pos_ref[1], part)).astype(BF)
    send_ref[pl.ds(0, part), :] = get(outf, aligned(1 - pos_ref[1], part)).astype(BF)
    send_ref[pl.ds(part, coef_ref.shape[0]), :] = coef_ref[...]


def core_body(pos_ref, keep_ref, got_ref, coef_ref, o0, o1, o2, o3, sums):
    part = keep_ref.shape[0]
    each = part // NX
    n = coef_ref.shape[0] // 2
    sums[...] = keep_ref[...].astype(F32) + got_ref[pl.ds(0, part), :].astype(F32)
    coef = unpack(coef_ref, 0, n) + unpack(got_ref, part, n)
    for r, out in enumerate((o0, o1, o2, o3)):
        out[pl.ds(0, each), :] = sums[aligned(turn(pos_ref[2], r, NX), each), :].astype(BF)
        pack(out, each, coef)


def x_body(nz, *refs):
    pos_ref, i0, i1, i2, i3 = refs[:5]
    outs = refs[5 : 5 + nz]
    sums, order = refs[5 + nz :]
    n = order.shape[1]
    each = i0.shape[0] - 2 * n
    last = each // nz
    sums[...] = sum(i[pl.ds(0, each), :].astype(F32) for i in (i0, i1, i2, i3))
    for r, i in enumerate((i0, i1, i2, i3)):
        order[turn(pos_ref[2], -r, NX)] = unpack(i, each, n)
    coef = (order[0] + order[1]) + (order[2] + order[3])
    for r, out in enumerate(outs):
        out[pl.ds(0, last), :] = sums[aligned(turn(pos_ref[3], r, nz), last), :].astype(BF)
        pack(out, last, coef)


def z_body(nz, own, *refs):
    pos_ref = refs[0]
    ins = refs[1 : 1 + nz]
    basis_ref, coef_ref, order = refs[1 + nz :]
    n = order.shape[1]
    last = basis_ref.shape[0]
    width = basis_ref.shape[1]
    basis_ref[...] = sum(i[pl.ds(0, last), :].astype(F32) for i in ins)
    for r, i in enumerate(ins):
        order[turn(pos_ref[3], -r, nz)] = unpack(i, last, n)
    coef = order[0]
    for r in range(1, nz):
        coef = coef + order[r]
    relations = coef_ref.shape[1]
    for j in range(n // own):
        size = min(width, relations - j * width)
        coef_ref[:, pl.ds(j * width, size)] = coef[j * own : (j + 1) * own, :size]


def bwd_body(
    cap, nblk, own, pos_ref, x_ref, rel_ref, srcv_ref, c0, c1, c2, c3, table_ref, pg_ref, sw_ref,
    o0, o1, o2, o3, xf, mf, cs, at_ref,
):
    groups = table_ref.shape[0]
    nbase = groups * own
    width = table_ref.shape[2]
    halves = width // LANES
    share = BLK // groups
    peers = rel_ref.shape[1] // cap
    w = slot_weights(own, pos_ref, (c0, c1, c2, c3), rel_ref[...], srcv_ref[...], nblk, cs).astype(BF)
    widen(x_ref, xf)

    def one(k, c):
        xk = slot_rows(xf, peers, cap, halves, share, k).astype(BF)
        put(mf, pl.ds(k, w.shape[0], stride=share), jnp.dot(w, xk, preferred_element_type=F32))
        return c

    lax.fori_loop(0, share, one, 0, unroll=4)
    acc = lax.dot_general(pg_ref[...], sw_ref[...], NT, preferred_element_type=F32)
    for b in range(nbase):
        mb = rows_of(mf, b, nbase, nblk, share).astype(BF)
        base = table_ref[b // own, pl.ds((b % own) * width, width), :]
        acc += lax.dot_general(mb, base, NT, preferred_element_type=F32)
    at_ref[...] = acc.T
    cols = width // groups
    for r, out in enumerate((o0, o1, o2, o3)):
        out[...] = at_ref[aligned(turn(pos_ref[0], r, groups), cols), :].astype(BF)


def join_body(nblk, row, pos_ref, i0, i1, i2, i3, out_ref, order):
    cols = out_ref.shape[0]
    share = BLK // 4
    for r, i in enumerate((i0, i1, i2, i3)):
        if row is None:
            piece = i[...]
        else:
            half = cols * LANES // i.shape[1]
            piece = jnp.concatenate(
                [i[pl.ds(row, half), h * LANES : (h + 1) * LANES] for h in range(i.shape[1] // LANES)], axis=0
            )
        order[turn(pos_ref[0], -r, 4)] = piece.astype(F32)
    for n in range(nblk):
        whole = jnp.concatenate([order[g][:, n * share : (n + 1) * share] for g in range(4)], axis=1)
        out_ref[:, n * BLK : (n + 1) * BLK] = whole.astype(BF)


def local(
    entity_rows,
    self_weight,
    bases,
    coefficients,
    send_block,
    edge_rel,
    edge_dst,
    edge_count,
    cotangent,
):
    peers = lax.axis_size("ent")
    groups = lax.axis_size("basis")
    ent_dev, width = entity_rows.shape
    nblk = ent_dev // BLK
    own = bases.shape[0]
    nbase = own * groups
    relations = coefficients.shape[0]
    cap = send_block.shape[2]
    slots = peers * cap
    share = BLK // groups
    halves = width // LANES
    nz = peers // (NX * NC)
    rows = nblk * share
    me = lax.axis_index("ent")
    pos = jnp.stack([lax.axis_index("basis"), me % NC, (me // NC) % NX, me // (NC * NX)]).astype(jnp.int32)

    def over_y(r, value):
        return lax.ppermute(value, "basis", [(i, (i + r) % groups) for i in range(groups)])

    def over_c(value):
        return lax.ppermute(value, "ent", [(i, i ^ 1) for i in range(peers)])

    def over_x(r, value):
        pairs = [(i, i - NC * ((i // NC) % NX) + NC * (((i // NC) + r) % NX)) for i in range(peers)]
        return lax.ppermute(value, "ent", pairs)

    def over_z(r, value):
        return lax.ppermute(value, "ent", [(i, (i + r * NC * NX) % peers) for i in range(peers)])

    def lines(value):
        return value.reshape(peers, cap).T.reshape(1, slots)

    dstv, srcv = lines(edge_dst), lines(send_block)
    cnt_in, rel_out = lines(edge_count), lines(edge_rel)

    per = cap * halves * share
    outgoing = call(functools.partial(take_body, share), bf(peers, per + 8, LANES), [SM, SM, SM, VM])(
        pos, send_block, edge_rel, entity_rows
    )
    incoming = lax.all_to_all(outgoing, "ent", split_axis=0, concat_axis=0, tiled=True)

    table = lax.all_gather(bases.reshape(own * width, width), "basis")
    chunks = -(-relations // width)
    coef = jnp.pad(coefficients.astype(BF).T, ((0, 16 - own), (0, chunks * width - relations)))
    coef = coef.reshape(16, chunks, width).transpose(1, 0, 2).reshape(chunks * 16, width)
    coefs = [coef] + [over_y(r, coef) for r in range(1, groups)]

    sides = [
        rows_scratch(nblk * nbase * share, width),
        pltpu.VMEM((groups, own, slots), F32),
        pltpu.VMEM((width, rows), F32),
    ]
    *ys, back, xr, pg, rel_in = call(
        functools.partial(fwd_body, cap, nblk, own),
        (
            *[bf((own + 1) * rows + share, width) for _ in range(groups)],
            bf(peers, per, LANES),
            bf(share, slots, width),
            bf(rows, width),
            jax.ShapeDtypeStruct((1, slots), jnp.int32),
        ),
        [SM] * 3 + [VM] * 11,
        [pltpu.VMEM((peers * (per + 8), LANES), F32), *sides],
        limit=28,
    )(
        pos, edge_dst, edge_count, incoming.reshape(peers * (per + 8), LANES), dstv, cnt_in, *coefs, table,
        entity_rows, self_weight, cotangent,
    )

    returned = lax.all_to_all(back, "ent", split_axis=0, concat_axis=0, tiled=True)
    ys = [ys[0]] + [over_y(r, ys[r]) for r in range(1, groups)]

    scores = call(
        functools.partial(score_body, nblk, own),
        tuple(jax.ShapeDtypeStruct((own, slots), F32) for _ in range(groups)),
        [SM] + [VM] * 5,
        [rows_scratch(nblk * nbase * share, width), pltpu.VMEM((nbase, slots), F32)],
    )(pos, xr, pg, dstv, cnt_in, table)
    scores = [scores[0]] + [over_y(r, scores[r]) for r in range(1, groups)]
    lot = chunks * own
    coef_part = call(coef_body, bf(2 * lot, width), [VM] * 5)(rel_in, *scores)

    part = peers * (own * width // peers) // NC
    keep, send = call(
        functools.partial(basis_body, own, rows, peers),
        (bf(part, width), bf(part + 2 * lot, width)),
        [SM] + [VM] * 5,
        [rows_scratch(width, width), rows_scratch(NC * part, width)],
    )(pos, *ys, coef_part)
    got = over_c(send)
    each = part // NX
    outs = call(
        core_body,
        tuple(bf(each + 2 * lot, width) for _ in range(NX)),
        [SM] + [VM] * 3,
        [pltpu.VMEM((part, width), F32)],
    )(pos, keep, got, coef_part)
    ins = [outs[0]] + [over_x(r, outs[r]) for r in range(1, NX)]
    last = each // nz
    outs = call(
        functools.partial(x_body, nz),
        tuple(bf(last + 2 * lot, width) for _ in range(nz)),
        [SM] + [VM] * NX,
        [pltpu.VMEM((each, width), F32), pltpu.VMEM((NX, lot, width), F32)],
    )(pos, *ins)
    ins = [outs[0]] + [over_z(r, outs[r]) for r in range(1, nz)]
    basis_grad, coef_grad = call(
        functools.partial(z_body, nz, own),
        (jax.ShapeDtypeStruct((last, width), F32), jax.ShapeDtypeStruct((own, relations), F32)),
        [SM] + [VM] * nz,
        [pltpu.VMEM((nz, lot, width), F32)],
    )(pos, *ins)

    cols = width // groups

    def join(row, pieces):
        return call(
            functools.partial(join_body, nblk, row),
            bf(cols, ent_dev),
            [SM] + [VM] * groups,
            [pltpu.VMEM((groups, cols, rows), F32)],
        )(pos, *pieces).T

    activation = join((own + 1) * rows, ys)

    grads = call(
        functools.partial(bwd_body, cap, nblk, own),
        tuple(bf(cols, rows) for _ in range(groups)),
        [SM] + [VM] * 10,
        [pltpu.VMEM((peers * per, LANES), F32), *sides],
        limit=20,
    )(pos, returned.reshape(peers * per, LANES), rel_out, srcv, *coefs, table, pg, self_weight)
    grads = [grads[0]] + [over_y(r, grads[r]) for r in range(1, groups)]
    entity_grad = join(None, grads)
    return (activation, basis_grad.reshape(own, width // peers, width), coef_grad.T, entity_grad)


def solution(mesh):
    placed = (
        P("ent", None),
        P(),
        P("basis", None, None),
        P(None, "basis"),
        P("ent", None, None),
        P("ent", None, None),
        P(None, "ent", None),
        P(None, "ent", None),
        P("ent", None),
    )
    return jax.shard_map(
        local,
        mesh=mesh,
        in_specs=placed,
        out_specs=(P("ent", "basis"), P("basis", "ent", None), P(None, "basis"), P("ent", "basis")),
        check_vma=False,
    )
```

```python
import functools

import jax
import jax.numpy as jnp
from jax import lax
from jax.experimental import pallas as pl
from jax.experimental.pallas import tpu as pltpu
from jax.sharding import Mesh
from jax.sharding import PartitionSpec as P

BLK = 128
LANES = 128
NX = 4
NC = 2
ENT = ("z", "x", "c")
BF = jnp.bfloat16
F32 = jnp.float32
NT = (((1,), (1,)), ((), ()))
TN = (((0,), (0,)), ((), ()))
MIB = 1024 * 1024
VM = pl.BlockSpec(memory_space=pltpu.VMEM)
SM = pl.BlockSpec(memory_space=pltpu.SMEM)
HB = pl.BlockSpec(memory_space=pltpu.HBM)


def call(body, outs, ins, scratch=(), limit=16, outs_in=None):
    return pl.pallas_call(
        body,
        out_shape=outs,
        in_specs=ins,
        out_specs=outs_in or jax.tree.map(lambda _: VM, outs),
        scratch_shapes=list(scratch),
        compiler_params=pltpu.CompilerParams(vmem_limit_bytes=limit * MIB),
    )


def bf(*shape):
    return jax.ShapeDtypeStruct(shape, BF)


def get(ref, at):
    return jnp.concatenate([ref[h, at, :] for h in range(ref.shape[0])], axis=1)


def put(ref, at, value):
    for h in range(ref.shape[0]):
        ref[h, at, :] = value[:, h * LANES : (h + 1) * LANES]


def rows_scratch(rows, width):
    return pltpu.VMEM((width // LANES, rows, LANES), F32)


def turn(i, r, n):
    return lax.rem(i + r + n, n)


def aligned(i, size):
    return pl.ds(pl.multiple_of(i * size, size), size)


def digits(value):
    high = value.astype(BF)
    return high, (value - high.astype(F32)).astype(BF)


def start_all(copies):
    for copy in copies:
        copy.start()
    return copies


def wait_all(copies):
    for copy in copies:
        copy.wait()


def own_row_copies(ref, scr, sem, share):
    first = lax.axis_index("basis") * share
    return [
        pltpu.make_async_copy(
            ref.at[pl.ds(pl.multiple_of(n * BLK + first, share), share), :],
            scr.at[pl.ds(n * share, share), :],
            sem.at[n],
        )
        for n in range(scr.shape[0] // share)
    ]


def line(ref):
    return jnp.concatenate([ref[c : c + 1, :] for c in range(ref.shape[0])], axis=1)


def take_body(share, idx_ref, rel_ref, ent_ref, out_ref, own, outs, sem, osem):
    wait_all(start_all(own_row_copies(ent_ref, own, sem, share)))
    cap, peers = idx_ref.shape
    halves = own.shape[1] // LANES
    lane = lax.broadcasted_iota(jnp.int32, (8, LANES), 1)
    lots = osem.shape[0]
    lot = peers // lots
    copies = []
    for q in range(peers):
        note = jnp.zeros((8, LANES), jnp.int32)
        for c in range(cap):
            block = own[aligned(idx_ref[c, q], share), :]
            for h in range(halves):
                outs[q, pl.ds((c * halves + h) * share, share), :] = block[:, h * LANES : (h + 1) * LANES]
            rel = rel_ref[c, q]
            note = jnp.where(lane == 2 * c, rel >> 8, note)
            note = jnp.where(lane == 2 * c + 1, rel & 255, note)
        outs[q, pl.ds(cap * halves * share, 8), :] = note.astype(F32).astype(BF)
        if (q + 1) % lot == 0:
            i = q // lot
            at = pl.ds(i * lot, lot)
            copies += start_all([pltpu.make_async_copy(outs.at[at], out_ref.at[at], osem.at[i])])
    wait_all(copies)


def slot_weights(own, coef_refs, rel, blk, nblk, cs):
    groups = len(coef_refs)
    rows, width = coef_refs[0].shape
    chunks = rows // 16
    slots = rel.shape[1]
    parts = [jnp.zeros((16, slots), F32) for _ in coef_refs]
    for j in range(chunks):
        ids = lax.broadcasted_iota(jnp.int32, (width, slots), 0) + j * width
        hot = jnp.where(ids == rel, 1.0, 0.0).astype(BF)
        for r, ref in enumerate(coef_refs):
            parts[r] += jnp.dot(ref[pl.ds(j * 16, 16), :], hot, preferred_element_type=F32)
    for r in range(groups):
        cs[turn(lax.axis_index("basis"), -r, groups)] = parts[r][:own]
    coef = cs[...].reshape(groups * own, slots)
    return jnp.concatenate([jnp.where(blk == n, coef, 0.0) for n in range(nblk)], axis=0)


def weights_body(nblk, own, rel_ref, src_ref, c0, c1, c2, c3, out_ref, cs):
    out_ref[...] = slot_weights(own, (c0, c1, c2, c3), line(rel_ref), line(src_ref), nblk, cs).astype(BF)


def widen(x_ref, xf):
    step = 512

    def some(i, c):
        at = aligned(i, step)
        xf[at, :] = x_ref[at, :].astype(F32)
        return c

    lax.fori_loop(0, x_ref.shape[0] // step, some, 0)


def slot_rows(xf, peers, cap, halves, share, k):
    per = xf.shape[0] // peers
    return jnp.concatenate(
        [
            jnp.concatenate(
                [xf[pl.ds((c * halves + h) * share + k, peers, stride=per), :] for h in range(halves)], axis=1
            )
            for c in range(cap)
        ],
        axis=0,
    )


def rows_of(mf, base, nbase, nblk, share):
    return jnp.concatenate([get(mf, aligned(n * nbase + base, share)) for n in range(nblk)], axis=0)


def table_copies(table_ref, tab, sem):
    return [pltpu.make_async_copy(table_ref.at[g], tab.at[g], sem.at[g]) for g in range(tab.shape[0])]


def fwd_body(
    cap, nblk, own, dst_ref, count_ref, x_ref, dstv_ref, cnt_ref, c0, c1, c2, c3, sw_ref, table_ref, ent_ref,
    cot_ref, y0, y1, y2, y3, back_ref, xr_ref, pg_ref, rel_ref, act_ref,
    xf, mf, cs, at_ref, tab, ent, cot, ysc, back, xr, tsem, esem, csem, ysem, bsem, xsem,
):
    groups = tab.shape[0]
    nbase = groups * own
    width = tab.shape[2]
    halves = width // LANES
    share = BLK // groups
    peers = back.shape[0]
    per = xf.shape[0] // peers
    group0 = lax.axis_index("basis")
    first = group0 * share
    ecopies = start_all(own_row_copies(ent_ref, ent, esem, share))
    tcopies = start_all(table_copies(table_ref, tab, tsem))
    ccopies = start_all(own_row_copies(cot_ref, cot, csem, share))
    widen(x_ref, xf)
    notes = xf[pl.ds(cap * halves * share, peers, stride=per), :].astype(BF)
    lane = lax.broadcasted_iota(jnp.int32, (8, LANES), 1)
    row = lax.broadcasted_iota(jnp.int32, (8, LANES), 0)
    pick = jnp.where(lane == 2 * row, 256.0, jnp.where(lane == 2 * row + 1, 1.0, 0.0)).astype(BF)
    rels = lax.dot_general(pick, notes, NT, preferred_element_type=F32).astype(jnp.int32)
    rel = jnp.concatenate([rels[c : c + 1] for c in range(cap)], axis=1)
    rel_ref[...] = rel
    w = slot_weights(own, (c0, c1, c2, c3), rel, line(dstv_ref), nblk, cs)
    cnt = line(cnt_ref)

    def one(k, c):
        xk = slot_rows(xf, peers, cap, halves, share, k).astype(BF)
        xr[k] = xk
        wk = jnp.where(cnt > first + k, w, 0.0).astype(BF)
        put(mf, pl.ds(k, w.shape[0], stride=share), jnp.dot(wk, xk, preferred_element_type=F32))
        return c

    lax.fori_loop(0, share, one, 0, unroll=4)
    copies = start_all([pltpu.make_async_copy(xr, xr_ref, xsem)])
    wait_all(ecopies)
    acc = jnp.dot(ent[...], sw_ref[...], preferred_element_type=F32)
    rows = nblk * share
    wait_all(tcopies)
    for r in range(groups):
        group = turn(group0, r, groups)
        for b in range(own):
            mb = rows_of(mf, group * own + b, nbase, nblk, share).astype(BF)
            ysc[r, pl.ds(b * rows, rows), :] = mb
            acc += jnp.dot(mb, tab[group, pl.ds(b * width, width), :], preferred_element_type=F32)
    s = jax.nn.sigmoid(acc)
    at_ref[...] = (acc * s).T
    wait_all(ccopies)
    pg = (cot[...].astype(F32) * (s * (1.0 + acc * (1.0 - s)))).astype(BF)
    pg_ref[...] = pg
    k_of = lax.broadcasted_iota(jnp.int32, (share, width), 0) + first
    lots = bsem.shape[0]
    lot = peers // lots
    for q in range(peers):
        for c in range(cap):
            block = pg_ref[aligned(dst_ref[c, q], share), :]
            block = jnp.where(k_of < count_ref[c, q], block.astype(F32), 0.0).astype(BF)
            for h in range(halves):
                back[q, pl.ds((c * halves + h) * share, share), :] = block[:, h * LANES : (h + 1) * LANES]
        if (q + 1) % lot == 0:
            i = q // lot
            at = pl.ds(i * lot, lot)
            copies += start_all([pltpu.make_async_copy(back.at[at], back_ref.at[at], bsem.at[i])])
    cols = width // groups
    for r, y in enumerate((y0, y1, y2, y3)):
        ysc[r, pl.ds(own * rows, rows), :] = pg
        copies += start_all([pltpu.make_async_copy(ysc.at[r], y, ysem.at[r])])
        act_ref[r] = at_ref[aligned(turn(group0, r, groups), cols), :].astype(BF)
    wait_all(copies)


def score_body(nblk, own, pg_ref, dstv_ref, cnt_ref, xr_ref, table_ref, s0, s1, s2, s3, pf, ts, tab, xr, tsem, xsem):
    groups = tab.shape[0]
    nbase = groups * own
    width = tab.shape[2]
    share, slots = xr.shape[:2]
    group0 = lax.axis_index("basis")
    first = group0 * share
    tcopies = start_all(table_copies(table_ref, tab, tsem))
    xcopies = start_all([pltpu.make_async_copy(xr_ref, xr, xsem)])
    pg = pg_ref[...]
    for b in range(nbase):
        if b % own == 0:
            tcopies[b // own].wait()
        base = tab[b // own, pl.ds((b % own) * width, width), :]
        p = lax.dot_general(pg, base, NT, preferred_element_type=F32)
        for n in range(nblk):
            put(pf, pl.ds((n * nbase + b) * share, share), p[n * share : (n + 1) * share])
    cnt = line(cnt_ref)
    wait_all(xcopies)

    def one(k, acc):
        pk = get(pf, pl.ds(k, nblk * nbase, stride=share)).astype(BF)
        t = lax.dot_general(pk, xr[k], NT, preferred_element_type=F32)
        return acc + jnp.where(cnt > first + k, t, 0.0)

    acc = lax.fori_loop(0, share, one, jnp.zeros((nblk * nbase, slots), F32), unroll=4)
    blk = line(dstv_ref)
    total = jnp.zeros((nbase, slots), F32)
    for n in range(nblk):
        total += jnp.where(blk == n, acc[n * nbase : (n + 1) * nbase], 0.0)
    ts[...] = total
    for r, out in enumerate((s0, s1, s2, s3)):
        out[...] = ts[aligned(turn(group0, r, groups), own), :]


def coef_body(rel_ref, s0, s1, s2, s3, out_ref):
    own, slots = s0.shape
    width = out_ref.shape[1]
    chunks = out_ref.shape[0] // (2 * own)
    high, low = digits((s0[...] + s1[...]) + (s2[...] + s3[...]))
    both = jnp.concatenate([high.astype(F32), low.astype(F32)], axis=0).astype(BF)
    rel = rel_ref[...]
    parts = []
    for j in range(chunks):
        ids = lax.broadcasted_iota(jnp.int32, (width, slots), 0) + j * width
        hot = jnp.where(ids == rel, 1.0, 0.0).astype(BF)
        t = lax.dot_general(both, hot, NT, preferred_element_type=F32)
        parts.append(t[:own] + t[own:])
    pack(out_ref, 0, jnp.concatenate(parts, axis=0))


def pack(ref, at, value):
    high, low = digits(value)
    n = value.shape[0]
    ref[pl.ds(at, n), :] = high
    ref[pl.ds(at + n, n), :] = low


def unpack(value, at, n):
    return value[at : at + n].astype(F32) + value[at + n : at + 2 * n].astype(F32)


def basis_body(own, rows, peers, y0, y1, y2, y3, coef_ref, keep_ref, send_ref, tmp, outf):
    ys = (y0, y1, y2, y3)
    width = y0.shape[1]
    part = keep_ref.shape[0]
    each = part // NX
    deep = part * NC // (own * peers)
    nz = each // (own * deep)
    pg = jnp.concatenate([y[pl.ds(own * rows, rows), :] for y in ys], axis=0)
    for b in range(own):
        m = jnp.concatenate([y[pl.ds(b * rows, rows), :] for y in ys], axis=0)
        put(tmp, pl.ds(0, width), lax.dot_general(m, pg, TN, preferred_element_type=F32))
        for c in range(NC):
            for x in range(NX):
                for d in range(deep):
                    put(
                        outf,
                        pl.ds((c * NX + x) * each + b * deep + d, nz, stride=own * deep),
                        get(tmp, pl.ds((x * NC + c) * deep + d, nz, stride=NX * NC * deep)),
                    )
    core = lax.axis_index("c")
    keep_ref[...] = get(outf, aligned(core, part)).astype(BF)
    send_ref[pl.ds(0, part), :] = get(outf, aligned(1 - core, part)).astype(BF)
    send_ref[pl.ds(part, coef_ref.shape[0]), :] = coef_ref[...]


def core_body(keep_ref, got_ref, coef_ref, o0, o1, o2, o3, sums):
    part = keep_ref.shape[0]
    each = part // NX
    n = coef_ref.shape[0] // 2
    sums[...] = keep_ref[...].astype(F32) + got_ref[pl.ds(0, part), :].astype(F32)
    coef = unpack(coef_ref[...], 0, n) + unpack(got_ref[pl.ds(part, 2 * n), :], 0, n)
    for r, out in enumerate((o0, o1, o2, o3)):
        out[pl.ds(0, each), :] = sums[aligned(turn(lax.axis_index("x"), r, NX), each), :].astype(BF)
        pack(out, each, coef)


def x_body(i0, i1, i2, i3, out_ref, order):
    n = order.shape[1]
    each = i0.shape[0] - 2 * n
    nz = out_ref.shape[0]
    last = each // nz
    sums = sum(i[pl.ds(0, each), :].astype(F32) for i in (i0, i1, i2, i3))
    for r, i in enumerate((i0, i1, i2, i3)):
        order[turn(lax.axis_index("x"), -r, NX)] = unpack(i[pl.ds(each, 2 * n), :], 0, n)
    high, low = digits((order[0] + order[1]) + (order[2] + order[3]))
    for z in range(nz):
        out_ref[z, pl.ds(0, last), :] = sums[z * last : (z + 1) * last].astype(BF)
        out_ref[z, pl.ds(last, n), :] = high
        out_ref[z, pl.ds(last + n, n), :] = low


def z_body(own, in_ref, basis_ref, coef_ref):
    nz, rows, width = in_ref.shape
    last = basis_ref.shape[0]
    n = (rows - last) // 2
    basis = jnp.zeros((last, width), F32)
    coef = jnp.zeros((n, width), F32)
    for z in range(nz):
        basis += in_ref[z, pl.ds(0, last), :].astype(F32)
        coef += unpack(in_ref[z, pl.ds(last, 2 * n), :], 0, n)
    basis_ref[...] = basis
    relations = coef_ref.shape[1]
    for j in range(n // own):
        size = min(width, relations - j * width)
        coef_ref[:, pl.ds(j * width, size)] = coef[j * own : (j + 1) * own, :size]


def bwd_body(
    cap, own, x_ref, w_ref, act_ref, pg_ref, sw_ref, table_ref, o0, o1, o2, o3, xf, mf, at_ref, tab, tsem
):
    groups = tab.shape[0]
    nbase = groups * own
    width = tab.shape[2]
    halves = width // LANES
    share = BLK // groups
    slots = w_ref.shape[1]
    peers = slots // cap
    nblk = w_ref.shape[0] // nbase
    tcopies = start_all(table_copies(table_ref, tab, tsem))
    widen(x_ref, xf)
    w = w_ref[...]

    def one(k, c):
        xk = slot_rows(xf, peers, cap, halves, share, k).astype(BF)
        put(mf, pl.ds(k, w.shape[0], stride=share), jnp.dot(w, xk, preferred_element_type=F32))
        return c

    lax.fori_loop(0, share, one, 0, unroll=4)
    acc = lax.dot_general(pg_ref[...], sw_ref[...], NT, preferred_element_type=F32)
    wait_all(tcopies)
    for b in range(nbase):
        mb = rows_of(mf, b, nbase, nblk, share).astype(BF)
        base = tab[b // own, pl.ds((b % own) * width, width), :]
        acc += lax.dot_general(mb, base, NT, preferred_element_type=F32)
    at_ref[...] = acc.T
    cols = width // groups
    for r, out in enumerate((o0, o1, o2, o3)):
        out[0] = at_ref[aligned(turn(lax.axis_index("basis"), r, groups), cols), :].astype(BF)
        out[1] = act_ref[r]


def join_body(nblk, i0, i1, i2, i3, grad_ref, act_ref, order):
    groups = order.shape[0]
    share = BLK // groups
    for r, i in enumerate((i0, i1, i2, i3)):
        order[turn(lax.axis_index("basis"), -r, groups)] = i[...].astype(F32)
    for j, out in enumerate((grad_ref, act_ref)):
        for n in range(nblk):
            whole = jnp.concatenate([order[g, j, :, n * share : (n + 1) * share] for g in range(groups)], axis=1)
            out[:, n * BLK : (n + 1) * BLK] = whole.astype(BF)


def local(
    entity_rows,
    self_weight,
    bases,
    coefficients,
    send_block,
    edge_rel,
    edge_dst,
    edge_count,
    cotangent,
):
    peers = lax.axis_size(ENT)
    groups = lax.axis_size("basis")
    ent_dev, width = entity_rows.shape
    nblk = ent_dev // BLK
    own = bases.shape[0]
    nbase = own * groups
    relations = coefficients.shape[0]
    cap = send_block.shape[2]
    slots = peers * cap
    share = BLK // groups
    halves = width // LANES
    nz = lax.axis_size("z")
    rows = nblk * share
    dma = pltpu.SemaphoreType.DMA

    def over(axis, r, value):
        n = lax.axis_size(axis)
        return lax.ppermute(value, axis, [(i, (i + r) % n) for i in range(n)])

    src, rel_out = send_block[0].T, edge_rel[0].T
    dst, cnt = edge_dst[:, 0, :].T, edge_count[:, 0, :].T

    per = cap * halves * share
    outgoing = call(
        functools.partial(take_body, share),
        bf(peers, per + 8, LANES),
        [SM, SM, HB],
        [
            pltpu.VMEM((rows, width), BF),
            pltpu.VMEM((peers, per + 8, LANES), BF),
            dma((nblk,)),
            dma((4,)),
        ],
        outs_in=HB,
    )(src, rel_out, entity_rows)
    incoming = lax.all_to_all(outgoing, ENT, split_axis=0, concat_axis=0, tiled=True)

    table = lax.all_gather(bases.reshape(own * width, width), "basis")
    chunks = -(-relations // width)
    coef = jnp.pad(coefficients.astype(BF).T, ((0, 16 - own), (0, chunks * width - relations)))
    coef = coef.reshape(16, chunks, width).transpose(1, 0, 2).reshape(chunks * 16, width)
    coefs = [coef] + [over("basis", r, coef) for r in range(1, groups)]
    w_out = call(
        functools.partial(weights_body, nblk, own),
        bf(nblk * nbase, slots),
        [VM] * 6,
        [pltpu.VMEM((groups, own, slots), F32)],
        limit=4,
    )(rel_out, src, *coefs)

    tables = pltpu.VMEM((groups, own * width, width), BF)
    *ys, back, xr, pg, rel_in, act = call(
        functools.partial(fwd_body, cap, nblk, own),
        (
            *[bf((own + 1) * rows, width) for _ in range(groups)],
            bf(peers, per, LANES),
            bf(share, slots, width),
            bf(rows, width),
            jax.ShapeDtypeStruct((1, slots), jnp.int32),
            bf(groups, width // groups, rows),
        ),
        [SM] * 2 + [VM] * 8 + [HB] * 3,
        [
            pltpu.VMEM((peers * (per + 8), LANES), F32),
            rows_scratch(nbase * rows, width),
            pltpu.VMEM((groups, own, slots), F32),
            pltpu.VMEM((width, rows), F32),
            tables,
            pltpu.VMEM((rows, width), BF),
            pltpu.VMEM((rows, width), BF),
            pltpu.VMEM((groups, (own + 1) * rows, width), BF),
            pltpu.VMEM((peers, per, LANES), BF),
            pltpu.VMEM((share, slots, width), BF),
            dma((groups,)),
            dma((nblk,)),
            dma((nblk,)),
            dma((groups,)),
            dma((4,)),
            dma,
        ],
        limit=28,
        outs_in=(HB,) * (groups + 2) + (VM,) * 3,
    )(
        dst, cnt, incoming.reshape(peers * (per + 8), LANES), dst, cnt, *coefs, self_weight, table,
        entity_rows, cotangent,
    )

    returned = lax.all_to_all(back, ENT, split_axis=0, concat_axis=0, tiled=True)
    ys = [ys[0]] + [over("basis", r, ys[r]) for r in range(1, groups)]

    scores = call(
        functools.partial(score_body, nblk, own),
        tuple(jax.ShapeDtypeStruct((own, slots), F32) for _ in range(groups)),
        [VM] * 3 + [HB] * 2,
        [
            rows_scratch(nbase * rows, width),
            pltpu.VMEM((nbase, slots), F32),
            tables,
            pltpu.VMEM((share, slots, width), BF),
            dma((groups,)),
            dma,
        ],
    )(pg, dst, cnt, xr, table)
    scores = [scores[0]] + [over("basis", r, scores[r]) for r in range(1, groups)]
    lot = chunks * own
    coef_part = call(coef_body, bf(2 * lot, width), [VM] * 5, limit=4)(rel_in, *scores)

    part = own * width // NC
    keep, send = call(
        functools.partial(basis_body, own, rows, peers),
        (bf(part, width), bf(part + 2 * lot, width)),
        [VM] * 5,
        [rows_scratch(width, width), rows_scratch(NC * part, width)],
        limit=8,
    )(*ys, coef_part)
    got = over("c", 1, send)
    each = part // NX
    outs = call(
        core_body,
        tuple(bf(each + 2 * lot, width) for _ in range(NX)),
        [VM] * 3,
        [pltpu.VMEM((part, width), F32)],
        limit=8,
    )(keep, got, coef_part)
    ins = [outs[0]] + [over("x", r, outs[r]) for r in range(1, NX)]

    grads = call(
        functools.partial(bwd_body, cap, own),
        tuple(bf(2, width // groups, rows) for _ in range(groups)),
        [VM] * 5 + [HB],
        [
            pltpu.VMEM((peers * per, LANES), F32),
            rows_scratch(nbase * rows, width),
            pltpu.VMEM((width, rows), F32),
            tables,
            dma((groups,)),
        ],
        limit=18,
    )(returned.reshape(peers * per, LANES), w_out, act, pg, self_weight, table)

    ins = lax.optimization_barrier((*ins, grads[0]))[:NX]
    last = each // nz
    out = call(
        x_body,
        bf(nz, last + 2 * lot, width),
        [VM] * NX,
        [pltpu.VMEM((NX, lot, width), F32)],
        limit=4,
    )(*ins)
    out = lax.all_to_all(out, "z", split_axis=0, concat_axis=0, tiled=True)
    basis_grad, coef_grad = call(
        functools.partial(z_body, own),
        (jax.ShapeDtypeStruct((last, width), F32), jax.ShapeDtypeStruct((own, relations), F32)),
        [VM],
        limit=4,
    )(out)

    grads = [grads[0]] + [over("basis", r, grads[r]) for r in range(1, groups)]
    cols = width // groups
    entity_grad, activation = call(
        functools.partial(join_body, nblk),
        (bf(cols, ent_dev), bf(cols, ent_dev)),
        [VM] * groups,
        [pltpu.VMEM((groups, 2, cols, rows), F32)],
        limit=4,
    )(*grads)
    return (activation.T, basis_grad.reshape(own, width // peers, width), coef_grad.T, entity_grad.T)


def solution(mesh):
    nz = mesh.devices.shape[0] // (NX * NC)
    fine = Mesh(mesh.devices.reshape(nz, NX, NC, mesh.devices.shape[1]), (*ENT, "basis"))
    placed = (
        P(ENT, None),
        P(),
        P("basis", None, None),
        P(None, "basis"),
        P(ENT, None, None),
        P(ENT, None, None),
        P(None, ENT, None),
        P(None, ENT, None),
        P(ENT, None),
    )
    return jax.shard_map(
        local,
        mesh=fine,
        in_specs=placed,
        out_specs=(P(ENT, "basis"), P("basis", ENT, None), P(None, "basis"), P(ENT, "basis")),
        check_vma=False,
    )
```

```python
import functools

import jax
import jax.numpy as jnp
from jax import lax
from jax.experimental import pallas as pl
from jax.experimental.pallas import tpu as pltpu
from jax.sharding import Mesh
from jax.sharding import PartitionSpec as P

BLK = 128
LANES = 128
NX = 4
NC = 2
ENT = ("z", "x", "c")
BF = jnp.bfloat16
F32 = jnp.float32
NT = (((1,), (1,)), ((), ()))
TN = (((0,), (0,)), ((), ()))
MIB = 1024 * 1024
VM = pl.BlockSpec(memory_space=pltpu.VMEM)
SM = pl.BlockSpec(memory_space=pltpu.SMEM)
HB = pl.BlockSpec(memory_space=pltpu.HBM)


def call(body, outs, ins, scratch=(), limit=16, outs_in=None):
    return pl.pallas_call(
        body,
        out_shape=outs,
        in_specs=ins,
        out_specs=outs_in or jax.tree.map(lambda _: VM, outs),
        scratch_shapes=list(scratch),
        compiler_params=pltpu.CompilerParams(vmem_limit_bytes=limit * MIB),
    )


def bf(*shape):
    return jax.ShapeDtypeStruct(shape, BF)


def hbm(*shape):
    return pltpu.HBM(shape, BF)


def far(value):
    return pltpu.with_memory_space_constraint(value, pltpu.HBM)


def get(ref, at):
    return jnp.concatenate([ref[h, at, :] for h in range(ref.shape[0])], axis=1)


def put(ref, at, value):
    for h in range(ref.shape[0]):
        ref[h, at, :] = value[:, h * LANES : (h + 1) * LANES]


def rows_scratch(rows, width):
    return pltpu.VMEM((width // LANES, rows, LANES), F32)


def turn(i, r, n):
    return lax.rem(i + r + n, n)


def aligned(i, size):
    return pl.ds(pl.multiple_of(i * size, size), size)


def digits(value):
    high = value.astype(BF)
    return high, (value - high.astype(F32)).astype(BF)


def start_all(copies):
    for copy in copies:
        copy.start()
    return copies


def wait_all(copies):
    for copy in copies:
        copy.wait()


def own_row_copies(ref, scr, sem, share):
    first = lax.axis_index("basis") * share
    return [
        pltpu.make_async_copy(
            ref.at[pl.ds(pl.multiple_of(n * BLK + first, share), share), :],
            scr.at[pl.ds(n * share, share), :],
            sem.at[n],
        )
        for n in range(scr.shape[0] // share)
    ]


def line(ref):
    return jnp.concatenate([ref[c : c + 1, :] for c in range(ref.shape[0])], axis=1)


def take_body(share, idx_ref, rel_ref, ent_ref, out_ref, own, outs, sem, osem):
    wait_all(start_all(own_row_copies(ent_ref, own, sem, share)))
    cap, peers = idx_ref.shape
    halves = own.shape[1] // LANES
    lane = lax.broadcasted_iota(jnp.int32, (8, LANES), 1)
    lots = osem.shape[0]
    lot = peers // lots
    copies = []
    for q in range(peers):
        note = jnp.zeros((8, LANES), jnp.int32)
        for c in range(cap):
            block = own[aligned(idx_ref[c, q], share), :]
            for h in range(halves):
                outs[q, pl.ds((c * halves + h) * share, share), :] = block[:, h * LANES : (h + 1) * LANES]
            rel = rel_ref[c, q]
            note = jnp.where(lane == 2 * c, rel >> 8, note)
            note = jnp.where(lane == 2 * c + 1, rel & 255, note)
        outs[q, pl.ds(cap * halves * share, 8), :] = note.astype(F32).astype(BF)
        if (q + 1) % lot == 0:
            i = q // lot
            at = pl.ds(i * lot, lot)
            copies += start_all([pltpu.make_async_copy(outs.at[at], out_ref.at[at], osem.at[i])])
    wait_all(copies)


def slot_weights(own, coef_refs, rel, blk, nblk, cs):
    groups = len(coef_refs)
    rows, width = coef_refs[0].shape
    chunks = rows // 16
    slots = rel.shape[1]
    parts = [jnp.zeros((16, slots), F32) for _ in coef_refs]
    for j in range(chunks):
        ids = lax.broadcasted_iota(jnp.int32, (width, slots), 0) + j * width
        hot = jnp.where(ids == rel, 1.0, 0.0).astype(BF)
        for r, ref in enumerate(coef_refs):
            parts[r] += jnp.dot(ref[pl.ds(j * 16, 16), :], hot, preferred_element_type=F32)
    for r in range(groups):
        cs[turn(lax.axis_index("basis"), -r, groups)] = parts[r][:own]
    coef = cs[...].reshape(groups * own, slots)
    return jnp.concatenate([jnp.where(blk == n, coef, 0.0) for n in range(nblk)], axis=0)


def weights_body(nblk, own, rel_ref, src_ref, c0, c1, c2, c3, out_ref, cs):
    out_ref[...] = slot_weights(own, (c0, c1, c2, c3), line(rel_ref), line(src_ref), nblk, cs).astype(BF)


def widen(x_ref, xf):
    step = 512

    def some(i, c):
        at = aligned(i, step)
        xf[at, :] = x_ref[at, :].astype(F32)
        return c

    lax.fori_loop(0, x_ref.shape[0] // step, some, 0)


def slot_rows(xf, peers, cap, halves, share, k):
    per = xf.shape[0] // peers
    return jnp.concatenate(
        [
            jnp.concatenate(
                [xf[pl.ds((c * halves + h) * share + k, peers, stride=per), :] for h in range(halves)], axis=1
            )
            for c in range(cap)
        ],
        axis=0,
    )


def rows_of(mf, base, nbase, nblk, share):
    return jnp.concatenate([get(mf, aligned(n * nbase + base, share)) for n in range(nblk)], axis=0)


def table_copies(table_ref, tab, sem):
    return [pltpu.make_async_copy(table_ref.at[g], tab.at[g], sem.at[g]) for g in range(tab.shape[0])]


def fwd_body(
    cap, nblk, own, dst_ref, count_ref, x_ref, dstv_ref, cnt_ref, c0, c1, c2, c3, sw_ref, table_ref, ent_ref,
    cot_ref, y0, y1, y2, y3, back_ref, xr_ref, pg_ref, rel_ref, act_ref,
    xf, mf, cs, at_ref, tab, ent, cot, ysc, back, xr, tsem, esem, csem, ysem, bsem, xsem,
):
    groups = tab.shape[0]
    nbase = groups * own
    width = tab.shape[2]
    halves = width // LANES
    share = BLK // groups
    peers = back.shape[0]
    per = xf.shape[0] // peers
    group0 = lax.axis_index("basis")
    first = group0 * share
    ecopies = start_all(own_row_copies(ent_ref, ent, esem, share))
    tcopies = start_all(table_copies(table_ref, tab, tsem))
    ccopies = start_all(own_row_copies(cot_ref, cot, csem, share))
    widen(x_ref, xf)
    notes = xf[pl.ds(cap * halves * share, peers, stride=per), :].astype(BF)
    lane = lax.broadcasted_iota(jnp.int32, (8, LANES), 1)
    row = lax.broadcasted_iota(jnp.int32, (8, LANES), 0)
    pick = jnp.where(lane == 2 * row, 256.0, jnp.where(lane == 2 * row + 1, 1.0, 0.0)).astype(BF)
    rels = lax.dot_general(pick, notes, NT, preferred_element_type=F32).astype(jnp.int32)
    rel = jnp.concatenate([rels[c : c + 1] for c in range(cap)], axis=1)
    rel_ref[...] = rel
    w = slot_weights(own, (c0, c1, c2, c3), rel, line(dstv_ref), nblk, cs)
    cnt = line(cnt_ref)

    def one(k, c):
        xk = slot_rows(xf, peers, cap, halves, share, k).astype(BF)
        xr[k] = xk
        wk = jnp.where(cnt > first + k, w, 0.0).astype(BF)
        put(mf, pl.ds(k, w.shape[0], stride=share), jnp.dot(wk, xk, preferred_element_type=F32))
        return c

    lax.fori_loop(0, share, one, 0, unroll=4)
    copies = start_all([pltpu.make_async_copy(xr, xr_ref, xsem)])
    wait_all(ecopies)
    acc = jnp.dot(ent[...], sw_ref[...], preferred_element_type=F32)
    rows = nblk * share
    wait_all(tcopies)
    for r in range(groups):
        group = turn(group0, r, groups)
        for b in range(own):
            mb = rows_of(mf, group * own + b, nbase, nblk, share).astype(BF)
            ysc[r, pl.ds(b * rows, rows), :] = mb
            acc += jnp.dot(mb, tab[group, pl.ds(b * width, width), :], preferred_element_type=F32)
    s = jax.nn.sigmoid(acc)
    at_ref[...] = (acc * s).T
    wait_all(ccopies)
    pg = (cot[...].astype(F32) * (s * (1.0 + acc * (1.0 - s)))).astype(BF)
    pg_ref[...] = pg
    k_of = lax.broadcasted_iota(jnp.int32, (share, width), 0) + first
    lots = bsem.shape[0]
    lot = peers // lots
    for q in range(peers):
        for c in range(cap):
            block = pg_ref[aligned(dst_ref[c, q], share), :]
            block = jnp.where(k_of < count_ref[c, q], block.astype(F32), 0.0).astype(BF)
            for h in range(halves):
                back[q, pl.ds((c * halves + h) * share, share), :] = block[:, h * LANES : (h + 1) * LANES]
        if (q + 1) % lot == 0:
            i = q // lot
            at = pl.ds(i * lot, lot)
            copies += start_all([pltpu.make_async_copy(back.at[at], back_ref.at[at], bsem.at[i])])
    cols = width // groups
    for r, y in enumerate((y0, y1, y2, y3)):
        ysc[r, pl.ds(own * rows, rows), :] = pg
        copies += start_all([pltpu.make_async_copy(ysc.at[r], y, ysem.at[r])])
        act_ref[r] = at_ref[aligned(turn(group0, r, groups), cols), :].astype(BF)
    wait_all(copies)


def score_body(nblk, own, pg_ref, dstv_ref, cnt_ref, xr_ref, table_ref, s0, s1, s2, s3, pf, ts, tab, xr, tsem, xsem):
    groups = tab.shape[0]
    nbase = groups * own
    width = tab.shape[2]
    share, slots = xr.shape[:2]
    group0 = lax.axis_index("basis")
    first = group0 * share
    tcopies = start_all(table_copies(table_ref, tab, tsem))
    xcopies = start_all([pltpu.make_async_copy(xr_ref, xr, xsem)])
    pg = pg_ref[...]
    for b in range(nbase):
        if b % own == 0:
            tcopies[b // own].wait()
        base = tab[b // own, pl.ds((b % own) * width, width), :]
        p = lax.dot_general(pg, base, NT, preferred_element_type=F32)
        for n in range(nblk):
            put(pf, pl.ds((n * nbase + b) * share, share), p[n * share : (n + 1) * share])
    cnt = line(cnt_ref)
    wait_all(xcopies)

    def one(k, acc):
        pk = get(pf, pl.ds(k, nblk * nbase, stride=share)).astype(BF)
        t = lax.dot_general(pk, xr[k], NT, preferred_element_type=F32)
        return acc + jnp.where(cnt > first + k, t, 0.0)

    acc = lax.fori_loop(0, share, one, jnp.zeros((nblk * nbase, slots), F32), unroll=4)
    blk = line(dstv_ref)
    total = jnp.zeros((nbase, slots), F32)
    for n in range(nblk):
        total += jnp.where(blk == n, acc[n * nbase : (n + 1) * nbase], 0.0)
    ts[...] = total
    for r, out in enumerate((s0, s1, s2, s3)):
        out[...] = ts[aligned(turn(group0, r, groups), own), :]


def coef_body(rel_ref, s0, s1, s2, s3, out_ref):
    own, slots = s0.shape
    width = out_ref.shape[1]
    chunks = out_ref.shape[0] // (2 * own)
    high, low = digits((s0[...] + s1[...]) + (s2[...] + s3[...]))
    both = jnp.concatenate([high.astype(F32), low.astype(F32)], axis=0).astype(BF)
    rel = rel_ref[...]
    parts = []
    for j in range(chunks):
        ids = lax.broadcasted_iota(jnp.int32, (width, slots), 0) + j * width
        hot = jnp.where(ids == rel, 1.0, 0.0).astype(BF)
        t = lax.dot_general(both, hot, NT, preferred_element_type=F32)
        parts.append(t[:own] + t[own:])
    pack(out_ref, 0, jnp.concatenate(parts, axis=0))


def pack(ref, at, value):
    high, low = digits(value)
    n = value.shape[0]
    ref[pl.ds(at, n), :] = high
    ref[pl.ds(at + n, n), :] = low


def unpack(value, at, n):
    return value[at : at + n].astype(F32) + value[at + n : at + 2 * n].astype(F32)


def basis_body(own, rows, peers, y0, y1, y2, y3, coef_ref, keep_ref, send_ref, tmp, outf):
    ys = (y0, y1, y2, y3)
    width = y0.shape[1]
    part = keep_ref.shape[0]
    each = part // NX
    deep = part * NC // (own * peers)
    nz = each // (own * deep)
    pg = jnp.concatenate([y[pl.ds(own * rows, rows), :] for y in ys], axis=0)
    for b in range(own):
        m = jnp.concatenate([y[pl.ds(b * rows, rows), :] for y in ys], axis=0)
        put(tmp, pl.ds(0, width), lax.dot_general(m, pg, TN, preferred_element_type=F32))
        for c in range(NC):
            for x in range(NX):
                for d in range(deep):
                    put(
                        outf,
                        pl.ds((c * NX + x) * each + b * deep + d, nz, stride=own * deep),
                        get(tmp, pl.ds((x * NC + c) * deep + d, nz, stride=NX * NC * deep)),
                    )
    core = lax.axis_index("c")
    keep_ref[...] = get(outf, aligned(core, part)).astype(BF)
    send_ref[pl.ds(0, part), :] = get(outf, aligned(1 - core, part)).astype(BF)
    send_ref[pl.ds(part, coef_ref.shape[0]), :] = coef_ref[...]


def core_body(keep_ref, got_ref, coef_ref, o0, o1, o2, o3, sums):
    part = keep_ref.shape[0]
    each = part // NX
    n = coef_ref.shape[0] // 2
    sums[...] = keep_ref[...].astype(F32) + got_ref[pl.ds(0, part), :].astype(F32)
    coef = unpack(coef_ref[...], 0, n) + unpack(got_ref[pl.ds(part, 2 * n), :], 0, n)
    for r, out in enumerate((o0, o1, o2, o3)):
        out[pl.ds(0, each), :] = sums[aligned(turn(lax.axis_index("x"), r, NX), each), :].astype(BF)
        pack(out, each, coef)


def x_body(i0, i1, i2, i3, out_ref, order):
    n = order.shape[1]
    each = i0.shape[0] - 2 * n
    nz = out_ref.shape[0]
    last = each // nz
    sums = sum(i[pl.ds(0, each), :].astype(F32) for i in (i0, i1, i2, i3))
    for r, i in enumerate((i0, i1, i2, i3)):
        order[turn(lax.axis_index("x"), -r, NX)] = unpack(i[pl.ds(each, 2 * n), :], 0, n)
    high, low = digits((order[0] + order[1]) + (order[2] + order[3]))
    for z in range(nz):
        out_ref[z, pl.ds(0, last), :] = sums[z * last : (z + 1) * last].astype(BF)
        out_ref[z, pl.ds(last, n), :] = high
        out_ref[z, pl.ds(last + n, n), :] = low


def z_body(own, in_ref, basis_ref, coef_ref):
    nz, rows, width = in_ref.shape
    last = basis_ref.shape[0]
    n = (rows - last) // 2
    basis = jnp.zeros((last, width), F32)
    coef = jnp.zeros((n, width), F32)
    for z in range(nz):
        basis += in_ref[z, pl.ds(0, last), :].astype(F32)
        coef += unpack(in_ref[z, pl.ds(last, 2 * n), :], 0, n)
    basis_ref[...] = basis
    relations = coef_ref.shape[1]
    for j in range(n // own):
        size = min(width, relations - j * width)
        coef_ref[:, pl.ds(j * width, size)] = coef[j * own : (j + 1) * own, :size]


def bwd_body(
    cap, own, x_ref, w_ref, act_ref, pg_ref, sw_ref, table_ref, o0, o1, o2, o3, xf, mf, at_ref, tab, tsem
):
    groups = tab.shape[0]
    nbase = groups * own
    width = tab.shape[2]
    halves = width // LANES
    share = BLK // groups
    slots = w_ref.shape[1]
    peers = slots // cap
    nblk = w_ref.shape[0] // nbase
    tcopies = start_all(table_copies(table_ref, tab, tsem))
    widen(x_ref, xf)
    w = w_ref[...]

    def one(k, c):
        xk = slot_rows(xf, peers, cap, halves, share, k).astype(BF)
        put(mf, pl.ds(k, w.shape[0], stride=share), jnp.dot(w, xk, preferred_element_type=F32))
        return c

    lax.fori_loop(0, share, one, 0, unroll=4)
    acc = lax.dot_general(pg_ref[...], sw_ref[...], NT, preferred_element_type=F32)
    wait_all(tcopies)
    for b in range(nbase):
        mb = rows_of(mf, b, nbase, nblk, share).astype(BF)
        base = tab[b // own, pl.ds((b % own) * width, width), :]
        acc += lax.dot_general(mb, base, NT, preferred_element_type=F32)
    at_ref[...] = acc.T
    cols = width // groups
    for r, out in enumerate((o0, o1, o2, o3)):
        out[0] = at_ref[aligned(turn(lax.axis_index("basis"), r, groups), cols), :].astype(BF)
        out[1] = act_ref[r]


def join_body(nblk, i0, i1, i2, i3, grad_ref, act_ref, order):
    groups = order.shape[0]
    share = BLK // groups
    for r, i in enumerate((i0, i1, i2, i3)):
        order[turn(lax.axis_index("basis"), -r, groups)] = i[...].astype(F32)
    for j, out in enumerate((grad_ref, act_ref)):
        for n in range(nblk):
            whole = jnp.concatenate([order[g, j, :, n * share : (n + 1) * share] for g in range(groups)], axis=1)
            out[:, n * BLK : (n + 1) * BLK] = whole.astype(BF)


def local(
    entity_rows,
    self_weight,
    bases,
    coefficients,
    send_block,
    edge_rel,
    edge_dst,
    edge_count,
    cotangent,
):
    peers = lax.axis_size(ENT)
    groups = lax.axis_size("basis")
    ent_dev, width = entity_rows.shape
    nblk = ent_dev // BLK
    own = bases.shape[0]
    nbase = own * groups
    relations = coefficients.shape[0]
    cap = send_block.shape[2]
    slots = peers * cap
    share = BLK // groups
    halves = width // LANES
    nz = lax.axis_size("z")
    rows = nblk * share
    dma = pltpu.SemaphoreType.DMA

    def over(axis, r, value):
        n = lax.axis_size(axis)
        return lax.ppermute(value, axis, [(i, (i + r) % n) for i in range(n)])

    src, rel_out = send_block[0].T, edge_rel[0].T
    dst, cnt = edge_dst[:, 0, :].T, edge_count[:, 0, :].T

    per = cap * halves * share
    outgoing = call(
        functools.partial(take_body, share),
        hbm(peers, per + 8, LANES),
        [SM, SM, HB],
        [
            pltpu.VMEM((rows, width), BF),
            pltpu.VMEM((peers, per + 8, LANES), BF),
            dma((nblk,)),
            dma((4,)),
        ],
        outs_in=HB,
    )(src, rel_out, far(entity_rows))
    incoming = lax.all_to_all(outgoing, ENT, split_axis=0, concat_axis=0, tiled=True)

    table = lax.all_gather(bases.reshape(own * width, width), "basis")
    chunks = -(-relations // width)
    coef = jnp.pad(coefficients.astype(BF).T, ((0, 16 - own), (0, chunks * width - relations)))
    coef = coef.reshape(16, chunks, width).transpose(1, 0, 2).reshape(chunks * 16, width)
    coefs = [coef] + [over("basis", r, coef) for r in range(1, groups)]
    w_out = call(
        functools.partial(weights_body, nblk, own),
        bf(nblk * nbase, slots),
        [VM] * 6,
        [pltpu.VMEM((groups, own, slots), F32)],
        limit=4,
    )(rel_out, src, *coefs)

    tables = pltpu.VMEM((groups, own * width, width), BF)
    *ys, back, xr, pg, rel_in, act = call(
        functools.partial(fwd_body, cap, nblk, own),
        (
            *[hbm((own + 1) * rows, width) for _ in range(groups)],
            hbm(peers, per, LANES),
            hbm(share, slots, width),
            bf(rows, width),
            jax.ShapeDtypeStruct((1, slots), jnp.int32),
            bf(groups, width // groups, rows),
        ),
        [SM] * 2 + [VM] * 8 + [HB] * 3,
        [
            pltpu.VMEM((peers * (per + 8), LANES), F32),
            rows_scratch(nbase * rows, width),
            pltpu.VMEM((groups, own, slots), F32),
            pltpu.VMEM((width, rows), F32),
            tables,
            pltpu.VMEM((rows, width), BF),
            pltpu.VMEM((rows, width), BF),
            pltpu.VMEM((groups, (own + 1) * rows, width), BF),
            pltpu.VMEM((peers, per, LANES), BF),
            pltpu.VMEM((share, slots, width), BF),
            dma((groups,)),
            dma((nblk,)),
            dma((nblk,)),
            dma((groups,)),
            dma((4,)),
            dma,
        ],
        limit=28,
        outs_in=(HB,) * (groups + 2) + (VM,) * 3,
    )(
        dst, cnt, incoming.reshape(peers * (per + 8), LANES), dst, cnt, *coefs, self_weight, far(table),
        far(entity_rows), far(cotangent),
    )

    returned = lax.all_to_all(back, ENT, split_axis=0, concat_axis=0, tiled=True)
    ys = [ys[0]] + [over("basis", r, ys[r]) for r in range(1, groups)]

    scores = call(
        functools.partial(score_body, nblk, own),
        tuple(jax.ShapeDtypeStruct((own, slots), F32) for _ in range(groups)),
        [VM] * 3 + [HB] * 2,
        [
            rows_scratch(nbase * rows, width),
            pltpu.VMEM((nbase, slots), F32),
            tables,
            pltpu.VMEM((share, slots, width), BF),
            dma((groups,)),
            dma,
        ],
    )(pg, dst, cnt, far(xr), far(table))
    scores = [scores[0]] + [over("basis", r, scores[r]) for r in range(1, groups)]
    lot = chunks * own
    coef_part = call(coef_body, bf(2 * lot, width), [VM] * 5, limit=4)(rel_in, *scores)

    part = own * width // NC
    keep, send = call(
        functools.partial(basis_body, own, rows, peers),
        (bf(part, width), bf(part + 2 * lot, width)),
        [VM] * 5,
        [rows_scratch(width, width), rows_scratch(NC * part, width)],
        limit=8,
    )(*ys, coef_part)
    got = over("c", 1, send)
    each = part // NX
    outs = call(
        core_body,
        tuple(bf(each + 2 * lot, width) for _ in range(NX)),
        [VM] * 3,
        [pltpu.VMEM((part, width), F32)],
        limit=8,
    )(keep, got, coef_part)
    ins = [outs[0]] + [over("x", r, outs[r]) for r in range(1, NX)]

    grads = call(
        functools.partial(bwd_body, cap, own),
        tuple(bf(2, width // groups, rows) for _ in range(groups)),
        [VM] * 5 + [HB],
        [
            pltpu.VMEM((peers * per, LANES), F32),
            rows_scratch(nbase * rows, width),
            pltpu.VMEM((width, rows), F32),
            tables,
            dma((groups,)),
        ],
        limit=18,
    )(returned.reshape(peers * per, LANES), w_out, act, pg, self_weight, far(table))

    ins = lax.optimization_barrier((*ins, grads[0]))[:NX]
    last = each // nz
    out = call(
        x_body,
        bf(nz, last + 2 * lot, width),
        [VM] * NX,
        [pltpu.VMEM((NX, lot, width), F32)],
        limit=4,
    )(*ins)
    out = lax.all_to_all(out, "z", split_axis=0, concat_axis=0, tiled=True)
    basis_grad, coef_grad = call(
        functools.partial(z_body, own),
        (jax.ShapeDtypeStruct((last, width), F32), jax.ShapeDtypeStruct((own, relations), F32)),
        [VM],
        limit=4,
    )(out)

    grads = [grads[0]] + [over("basis", r, grads[r]) for r in range(1, groups)]
    cols = width // groups
    entity_grad, activation = call(
        functools.partial(join_body, nblk),
        (bf(cols, ent_dev), bf(cols, ent_dev)),
        [VM] * groups,
        [pltpu.VMEM((groups, 2, cols, rows), F32)],
        limit=4,
    )(*grads)
    return (activation.T, basis_grad.reshape(own, width // peers, width), coef_grad.T, entity_grad.T)


def solution(mesh):
    nz = mesh.devices.shape[0] // (NX * NC)
    fine = Mesh(mesh.devices.reshape(nz, NX, NC, mesh.devices.shape[1]), (*ENT, "basis"))
    placed = (
        P(ENT, None),
        P(),
        P("basis", None, None),
        P(None, "basis"),
        P(ENT, None, None),
        P(ENT, None, None),
        P(None, ENT, None),
        P(None, ENT, None),
        P(ENT, None),
    )
    return jax.shard_map(
        local,
        mesh=fine,
        in_specs=placed,
        out_specs=(P(ENT, "basis"), P("basis", ENT, None), P(None, "basis"), P(ENT, "basis")),
        check_vma=False,
    )
```

```python
import functools

import jax
import jax.numpy as jnp
from jax import lax
from jax.experimental import pallas as pl
from jax.experimental.pallas import tpu as pltpu
from jax.sharding import Mesh
from jax.sharding import PartitionSpec as P

BLK = 128
LANES = 128
NX = 4
NC = 2
ENT = ("z", "x", "c")
BF = jnp.bfloat16
F32 = jnp.float32
NT = (((1,), (1,)), ((), ()))
TN = (((0,), (0,)), ((), ()))
MIB = 1024 * 1024
VM = pl.BlockSpec(memory_space=pltpu.VMEM)
SM = pl.BlockSpec(memory_space=pltpu.SMEM)
COST = pl.CostEstimate(flops=8 * 10**9, transcendentals=0, bytes_accessed=20 * 10**6)
HB = pl.BlockSpec(memory_space=pltpu.HBM)


def call(body, outs, ins, scratch=(), limit=16, outs_in=None, cost=None):
    return pl.pallas_call(
        body,
        out_shape=outs,
        in_specs=ins,
        out_specs=outs_in or jax.tree.map(lambda _: VM, outs),
        scratch_shapes=list(scratch),
        cost_estimate=cost,
        compiler_params=pltpu.CompilerParams(vmem_limit_bytes=limit * MIB),
    )


def bf(*shape):
    return jax.ShapeDtypeStruct(shape, BF)


def hbm(*shape):
    return pltpu.HBM(shape, BF)


def far(value):
    return pltpu.with_memory_space_constraint(value, pltpu.HBM)


def get(ref, at):
    return jnp.concatenate([ref[h, at, :] for h in range(ref.shape[0])], axis=1)


def put(ref, at, value):
    for h in range(ref.shape[0]):
        ref[h, at, :] = value[:, h * LANES : (h + 1) * LANES]


def rows_scratch(rows, width):
    return pltpu.VMEM((width // LANES, rows, LANES), F32)


def turn(i, r, n):
    return lax.rem(i + r + n, n)


def aligned(i, size):
    return pl.ds(pl.multiple_of(i * size, size), size)


def digits(value):
    high = value.astype(BF)
    return high, (value - high.astype(F32)).astype(BF)


def start_all(copies):
    for copy in copies:
        copy.start()
    return copies


def wait_all(copies):
    for copy in copies:
        copy.wait()


def own_row_copies(ref, scr, sem, share):
    first = lax.axis_index("basis") * share
    return [
        pltpu.make_async_copy(
            ref.at[pl.ds(pl.multiple_of(n * BLK + first, share), share), :],
            scr.at[pl.ds(n * share, share), :],
            sem.at[n],
        )
        for n in range(scr.shape[0] // share)
    ]


def line(ref):
    return jnp.concatenate([ref[c : c + 1, :] for c in range(ref.shape[0])], axis=1)


def take_body(share, src_ref, edge_ref, ent_ref, out_ref, idx_ref, rel_ref, own, outs, isem, sem, osem):
    copies = own_row_copies(ent_ref, own, sem, share)
    copies += [pltpu.make_async_copy(src_ref, idx_ref, isem.at[0]), pltpu.make_async_copy(edge_ref, rel_ref, isem.at[1])]
    wait_all(start_all(copies))
    cap, peers = idx_ref.shape
    halves = own.shape[1] // LANES
    lane = lax.broadcasted_iota(jnp.int32, (8, LANES), 1)
    lots = osem.shape[0]
    lot = peers // lots
    copies = []
    for q in range(peers):
        note = jnp.zeros((8, LANES), jnp.int32)
        for c in range(cap):
            block = own[aligned(idx_ref[c, q], share), :]
            for h in range(halves):
                outs[q, pl.ds((c * halves + h) * share, share), :] = block[:, h * LANES : (h + 1) * LANES]
            rel = rel_ref[c, q]
            note = jnp.where(lane == 2 * c, rel >> 8, note)
            note = jnp.where(lane == 2 * c + 1, rel & 255, note)
        outs[q, pl.ds(cap * halves * share, 8), :] = note.astype(F32).astype(BF)
        if (q + 1) % lot == 0:
            i = q // lot
            at = pl.ds(i * lot, lot)
            copies += start_all([pltpu.make_async_copy(outs.at[at], out_ref.at[at], osem.at[i])])
    wait_all(copies)


def slot_weights(own, coef_refs, rel, blk, nblk, cs):
    groups = len(coef_refs)
    rows, width = coef_refs[0].shape
    chunks = rows // 16
    slots = rel.shape[1]
    parts = [jnp.zeros((16, slots), F32) for _ in coef_refs]
    for j in range(chunks):
        ids = lax.broadcasted_iota(jnp.int32, (width, slots), 0) + j * width
        hot = jnp.where(ids == rel, 1.0, 0.0).astype(BF)
        for r, ref in enumerate(coef_refs):
            parts[r] += jnp.dot(ref[pl.ds(j * 16, 16), :], hot, preferred_element_type=F32)
    for r in range(groups):
        cs[turn(lax.axis_index("basis"), -r, groups)] = parts[r][:own]
    coef = cs[...].reshape(groups * own, slots)
    return jnp.concatenate([jnp.where(blk == n, coef, 0.0) for n in range(nblk)], axis=0)


def widen(x_ref, xf):
    step = 512

    def some(i, c):
        at = aligned(i, step)
        xf[at, :] = x_ref[at, :].astype(F32)
        return c

    lax.fori_loop(0, x_ref.shape[0] // step, some, 0)


def slot_rows(xf, peers, cap, halves, share, k):
    per = xf.shape[0] // peers
    return jnp.concatenate(
        [
            jnp.concatenate(
                [xf[pl.ds((c * halves + h) * share + k, peers, stride=per), :] for h in range(halves)], axis=1
            )
            for c in range(cap)
        ],
        axis=0,
    )


def rows_of(mf, base, nbase, nblk, share):
    return jnp.concatenate([get(mf, aligned(n * nbase + base, share)) for n in range(nblk)], axis=0)


def table_copies(table_ref, tab, sem):
    return [pltpu.make_async_copy(table_ref.at[g], tab.at[g], sem.at[g]) for g in range(tab.shape[0])]


def fwd_body(
    cap, nblk, own, dst_ref, count_ref, x_ref, dstv_ref, cnt_ref, c0, c1, c2, c3, sw_ref, table_ref, ent_ref,
    cot_ref, y0, y1, y2, y3, back_ref, pg_ref, rel_ref, act_ref,
    xf, mf, cs, at_ref, tab, ent, cot, ysc, back, tsem, esem, csem, ysem, psem, bsem,
):
    groups = tab.shape[0]
    nbase = groups * own
    width = tab.shape[2]
    halves = width // LANES
    share = BLK // groups
    peers = back.shape[0]
    per = xf.shape[0] // peers
    group0 = lax.axis_index("basis")
    first = group0 * share
    ecopies = start_all(own_row_copies(ent_ref, ent, esem, share))
    tcopies = start_all(table_copies(table_ref, tab, tsem))
    ccopies = start_all(own_row_copies(cot_ref, cot, csem, share))
    widen(x_ref, xf)
    notes = xf[pl.ds(cap * halves * share, peers, stride=per), :].astype(BF)
    lane = lax.broadcasted_iota(jnp.int32, (8, LANES), 1)
    row = lax.broadcasted_iota(jnp.int32, (8, LANES), 0)
    pick = jnp.where(lane == 2 * row, 256.0, jnp.where(lane == 2 * row + 1, 1.0, 0.0)).astype(BF)
    rels = lax.dot_general(pick, notes, NT, preferred_element_type=F32).astype(jnp.int32)
    rel = jnp.concatenate([rels[c : c + 1] for c in range(cap)], axis=1)
    rel_ref[...] = rel
    w = slot_weights(own, (c0, c1, c2, c3), rel, line(dstv_ref), nblk, cs)
    cnt = line(cnt_ref)

    def one(k, c):
        xk = slot_rows(xf, peers, cap, halves, share, k).astype(BF)
        wk = jnp.where(cnt > first + k, w, 0.0).astype(BF)
        put(mf, pl.ds(k, w.shape[0], stride=share), jnp.dot(wk, xk, preferred_element_type=F32))
        return c

    lax.fori_loop(0, share, one, 0, unroll=8)
    copies = []
    wait_all(ecopies)
    acc = jnp.dot(ent[...], sw_ref[...], preferred_element_type=F32)
    rows = nblk * share
    ys = (y0, y1, y2, y3)
    wait_all(tcopies)
    for r in range(groups):
        group = turn(group0, r, groups)
        for b in range(own):
            mb = rows_of(mf, group * own + b, nbase, nblk, share).astype(BF)
            ysc[r, pl.ds(b * rows, rows), :] = mb
            acc += jnp.dot(mb, tab[group, pl.ds(b * width, width), :], preferred_element_type=F32)
        if r:
            at = pl.ds(0, own * rows)
            copies += start_all([pltpu.make_async_copy(ysc.at[r, at], ys[r].at[at], ysem.at[r])])
    s = jax.nn.sigmoid(acc)
    at_ref[...] = (acc * s).T
    wait_all(ccopies)
    pg = (cot[...].astype(F32) * (s * (1.0 + acc * (1.0 - s)))).astype(BF)
    pg_ref[...] = pg
    k_of = lax.broadcasted_iota(jnp.int32, (share, width), 0) + first
    lots = bsem.shape[0]
    lot = peers // lots
    for q in range(peers):
        for c in range(cap):
            block = pg_ref[aligned(dst_ref[c, q], share), :]
            block = jnp.where(k_of < count_ref[c, q], block.astype(F32), 0.0).astype(BF)
            for h in range(halves):
                back[q, pl.ds((c * halves + h) * share, share), :] = block[:, h * LANES : (h + 1) * LANES]
        if (q + 1) % lot == 0:
            i = q // lot
            at = pl.ds(i * lot, lot)
            copies += start_all([pltpu.make_async_copy(back.at[at], back_ref.at[at], bsem.at[i])])
    cols = width // groups
    at = pl.ds(own * rows, rows)
    for r in range(groups):
        ysc[r, at, :] = pg
        copies += start_all([pltpu.make_async_copy(ysc.at[r, at] if r else ysc.at[r], ys[r].at[at] if r else ys[r], psem.at[r])])
        act_ref[r] = at_ref[aligned(turn(group0, r, groups), cols), :].astype(BF)
    wait_all(copies)


def score_body(
    cap, nblk, own, halves, pg_ref, dstv_ref, cnt_ref, x_ref, rel_ref, src_ref, c0, c1, c2, c3, table_ref,
    s0, s1, s2, s3, w_ref, xf, pf, ts, tab, cs, tsem,
):
    groups = tab.shape[0]
    nbase = groups * own
    width = tab.shape[2]
    peers = cnt_ref.shape[1]
    slots = cap * peers
    share = BLK // groups
    group0 = lax.axis_index("basis")
    first = group0 * share
    tcopies = start_all(table_copies(table_ref, tab, tsem))
    w_ref[...] = slot_weights(own, (c0, c1, c2, c3), line(rel_ref), line(src_ref), nblk, cs).astype(BF)
    widen(x_ref, xf)
    pg = pg_ref[...]
    for b in range(nbase):
        if b % own == 0:
            tcopies[b // own].wait()
        base = tab[b // own, pl.ds((b % own) * width, width), :]
        p = lax.dot_general(pg, base, NT, preferred_element_type=F32)
        for n in range(nblk):
            put(pf, pl.ds((n * nbase + b) * share, share), p[n * share : (n + 1) * share])
    cnt = line(cnt_ref)

    def one(k, acc):
        pk = get(pf, pl.ds(k, nblk * nbase, stride=share)).astype(BF)
        xk = slot_rows(xf, peers, cap, halves, share, k).astype(BF)
        t = lax.dot_general(pk, xk, NT, preferred_element_type=F32)
        return acc + jnp.where(cnt > first + k, t, 0.0)

    acc = lax.fori_loop(0, share, one, jnp.zeros((nblk * nbase, slots), F32), unroll=4)
    blk = line(dstv_ref)
    total = jnp.zeros((nbase, slots), F32)
    for n in range(nblk):
        total += jnp.where(blk == n, acc[n * nbase : (n + 1) * nbase], 0.0)
    ts[...] = total
    for r, out in enumerate((s0, s1, s2, s3)):
        out[...] = ts[aligned(turn(group0, r, groups), own), :]


def coef_body(rel_ref, s0, s1, s2, s3, out_ref):
    own, slots = s0.shape
    width = out_ref.shape[1]
    chunks = out_ref.shape[0] // (2 * own)
    high, low = digits((s0[...] + s1[...]) + (s2[...] + s3[...]))
    both = jnp.concatenate([high.astype(F32), low.astype(F32)], axis=0).astype(BF)
    rel = rel_ref[...]
    parts = []
    for j in range(chunks):
        ids = lax.broadcasted_iota(jnp.int32, (width, slots), 0) + j * width
        hot = jnp.where(ids == rel, 1.0, 0.0).astype(BF)
        t = lax.dot_general(both, hot, NT, preferred_element_type=F32)
        parts.append(t[:own] + t[own:])
    pack(out_ref, 0, jnp.concatenate(parts, axis=0))


def pack(ref, at, value):
    high, low = digits(value)
    n = value.shape[0]
    ref[pl.ds(at, n), :] = high
    ref[pl.ds(at + n, n), :] = low


def unpack(value, at, n):
    return value[at : at + n].astype(F32) + value[at + n : at + 2 * n].astype(F32)


def basis_body(own, rows, peers, y0, y1, y2, y3, keep_ref, send_ref, tmp, outf):
    ys = (y0, y1, y2, y3)
    width = y0.shape[1]
    part = keep_ref.shape[0]
    each = part // NX
    deep = part * NC // (own * peers)
    nz = each // (own * deep)
    pg = jnp.concatenate([y[pl.ds(own * rows, rows), :] for y in ys], axis=0)
    for b in range(own):
        m = jnp.concatenate([y[pl.ds(b * rows, rows), :] for y in ys], axis=0)
        put(tmp, pl.ds(0, width), lax.dot_general(m, pg, TN, preferred_element_type=F32))
        for c in range(NC):
            for x in range(NX):
                for d in range(deep):
                    put(
                        outf,
                        pl.ds((c * NX + x) * each + b * deep + d, nz, stride=own * deep),
                        get(tmp, pl.ds((x * NC + c) * deep + d, nz, stride=NX * NC * deep)),
                    )
    core = lax.axis_index("c")
    keep_ref[...] = get(outf, aligned(core, part)).astype(BF)
    send_ref[...] = get(outf, aligned(1 - core, part)).astype(BF)


def core_body(keep_ref, got_ref, coef_ref, other_ref, o0, o1, o2, o3, sums):
    part = keep_ref.shape[0]
    each = part // NX
    n = coef_ref.shape[0] // 2
    sums[...] = keep_ref[...].astype(F32) + got_ref[...].astype(F32)
    coef = unpack(coef_ref[...], 0, n) + unpack(other_ref[...], 0, n)
    for r, out in enumerate((o0, o1, o2, o3)):
        out[pl.ds(0, each), :] = sums[aligned(turn(lax.axis_index("x"), r, NX), each), :].astype(BF)
        pack(out, each, coef)


def x_body(i0, i1, i2, i3, out_ref, order):
    n = order.shape[1]
    each = i0.shape[0] - 2 * n
    nz = out_ref.shape[0]
    last = each // nz
    sums = sum(i[pl.ds(0, each), :].astype(F32) for i in (i0, i1, i2, i3))
    for r, i in enumerate((i0, i1, i2, i3)):
        order[turn(lax.axis_index("x"), -r, NX)] = unpack(i[pl.ds(each, 2 * n), :], 0, n)
    high, low = digits((order[0] + order[1]) + (order[2] + order[3]))
    for z in range(nz):
        out_ref[z, pl.ds(0, last), :] = sums[z * last : (z + 1) * last].astype(BF)
        out_ref[z, pl.ds(last, n), :] = high
        out_ref[z, pl.ds(last + n, n), :] = low


def z_body(own, in_ref, basis_ref, coef_ref):
    nz, rows, width = in_ref.shape
    last = basis_ref.shape[0]
    n = (rows - last) // 2
    basis = jnp.zeros((last, width), F32)
    coef = jnp.zeros((n, width), F32)
    for z in range(nz):
        basis += in_ref[z, pl.ds(0, last), :].astype(F32)
        coef += unpack(in_ref[z, pl.ds(last, 2 * n), :], 0, n)
    basis_ref[...] = basis
    relations = coef_ref.shape[1]
    for j in range(n // own):
        size = min(width, relations - j * width)
        coef_ref[:, pl.ds(j * width, size)] = coef[j * own : (j + 1) * own, :size]


def bwd_body(
    cap, own, x_ref, w_ref, act_ref, pg_ref, sw_ref, table_ref, o0, o1, o2, o3, xf, mf, at_ref, tab, tsem
):
    groups = tab.shape[0]
    nbase = groups * own
    width = tab.shape[2]
    halves = width // LANES
    share = BLK // groups
    slots = w_ref.shape[1]
    peers = slots // cap
    nblk = w_ref.shape[0] // nbase
    tcopies = start_all(table_copies(table_ref, tab, tsem))
    widen(x_ref, xf)
    w = w_ref[...]

    def one(k, c):
        xk = slot_rows(xf, peers, cap, halves, share, k).astype(BF)
        put(mf, pl.ds(k, w.shape[0], stride=share), jnp.dot(w, xk, preferred_element_type=F32))
        return c

    lax.fori_loop(0, share, one, 0, unroll=8)
    acc = lax.dot_general(pg_ref[...], sw_ref[...], NT, preferred_element_type=F32)
    wait_all(tcopies)
    for b in range(nbase):
        mb = rows_of(mf, b, nbase, nblk, share).astype(BF)
        base = tab[b // own, pl.ds((b % own) * width, width), :]
        acc += lax.dot_general(mb, base, NT, preferred_element_type=F32)
    at_ref[...] = acc.T
    cols = width // groups
    for r, out in enumerate((o0, o1, o2, o3)):
        out[0] = at_ref[aligned(turn(lax.axis_index("basis"), r, groups), cols), :].astype(BF)
        out[1] = act_ref[r]


def join_body(nblk, i0, i1, i2, i3, grad_ref, act_ref, order):
    groups = order.shape[0]
    share = BLK // groups
    for r, i in enumerate((i0, i1, i2, i3)):
        order[turn(lax.axis_index("basis"), -r, groups)] = i[...].astype(F32)
    for j, out in enumerate((grad_ref, act_ref)):
        for n in range(nblk):
            whole = jnp.concatenate([order[g, j, :, n * share : (n + 1) * share] for g in range(groups)], axis=1)
            out[:, n * BLK : (n + 1) * BLK] = whole.astype(BF)


def local(
    entity_rows,
    self_weight,
    bases,
    coefficients,
    send_block,
    edge_rel,
    edge_dst,
    edge_count,
    cotangent,
):
    peers = lax.axis_size(ENT)
    groups = lax.axis_size("basis")
    ent_dev, width = entity_rows.shape
    nblk = ent_dev // BLK
    own = bases.shape[0]
    nbase = own * groups
    relations = coefficients.shape[0]
    cap = send_block.shape[2]
    slots = peers * cap
    share = BLK // groups
    halves = width // LANES
    nz = lax.axis_size("z")
    rows = nblk * share
    dma = pltpu.SemaphoreType.DMA

    def over(axis, r, value):
        n = lax.axis_size(axis)
        return lax.ppermute(value, axis, [(i, (i + r) % n) for i in range(n)])

    src, rel_out = send_block[0].T, edge_rel[0].T
    dst, cnt = edge_dst[:, 0, :].T, edge_count[:, 0, :].T

    per = cap * halves * share
    outgoing = call(
        functools.partial(take_body, share),
        hbm(peers, per + 8, LANES),
        [HB] * 3,
        [
            pltpu.SMEM((cap, peers), jnp.int32),
            pltpu.SMEM((cap, peers), jnp.int32),
            pltpu.VMEM((rows, width), BF),
            pltpu.VMEM((peers, per + 8, LANES), BF),
            dma((2,)),
            dma((nblk,)),
            dma((4,)),
        ],
        outs_in=HB,
    )(far(src), far(rel_out), far(entity_rows))
    incoming = lax.all_to_all(outgoing, ENT, split_axis=0, concat_axis=0, tiled=True)

    bases, _ = lax.optimization_barrier((bases, outgoing))
    table = lax.all_gather(bases.reshape(own * width, width), "basis")
    chunks = -(-relations // width)
    coef = jnp.pad(coefficients.astype(BF).T, ((0, 16 - own), (0, chunks * width - relations)))
    coef = coef.reshape(16, chunks, width).transpose(1, 0, 2).reshape(chunks * 16, width)
    coefs = [coef] + [over("basis", r, coef) for r in range(1, groups)]
    tables = pltpu.VMEM((groups, own * width, width), BF)
    incoming = incoming.reshape(peers * (per + 8), LANES)
    *ys, back, pg, rel_in, act = call(
        functools.partial(fwd_body, cap, nblk, own),
        (
            *[hbm((own + 1) * rows, width) for _ in range(groups)],
            hbm(peers, per, LANES),
            bf(rows, width),
            jax.ShapeDtypeStruct((1, slots), jnp.int32),
            bf(groups, width // groups, rows),
        ),
        [SM] * 2 + [VM] * 8 + [HB] * 3,
        [
            pltpu.VMEM((peers * (per + 8), LANES), F32),
            rows_scratch(nbase * rows, width),
            pltpu.VMEM((groups, own, slots), F32),
            pltpu.VMEM((width, rows), F32),
            tables,
            pltpu.VMEM((rows, width), BF),
            pltpu.VMEM((rows, width), BF),
            pltpu.VMEM((groups, (own + 1) * rows, width), BF),
            pltpu.VMEM((peers, per, LANES), BF),
            dma((groups,)),
            dma((nblk,)),
            dma((nblk,)),
            dma((groups,)),
            dma((groups,)),
            dma((4,)),
        ],
        limit=28,
        outs_in=(HB,) * (groups + 1) + (VM,) * 3,
    )(
        dst, cnt, incoming, dst, cnt, *coefs, self_weight, far(table),
        far(entity_rows), far(cotangent),
    )

    returned = lax.all_to_all(back, ENT, split_axis=0, concat_axis=0, tiled=True)
    ys = [ys[0]] + [over("basis", r, ys[r]) for r in range(1, groups)]

    *scores, w_out = call(
        functools.partial(score_body, cap, nblk, own, halves),
        (*[jax.ShapeDtypeStruct((own, slots), F32) for _ in range(groups)], bf(nblk * nbase, slots)),
        [VM] * 10 + [HB],
        [
            pltpu.VMEM((peers * (per + 8), LANES), F32),
            rows_scratch(nbase * rows, width),
            pltpu.VMEM((nbase, slots), F32),
            tables,
            pltpu.VMEM((groups, own, slots), F32),
            dma((groups,)),
        ],
        limit=18,
        cost=COST,
    )(pg, dst, cnt, incoming, rel_out, src, *coefs, far(table))
    scores = [scores[0]] + [over("basis", r, scores[r]) for r in range(1, groups)]
    lot = chunks * own
    coef_part = call(coef_body, bf(2 * lot, width), [VM] * 5, limit=4)(rel_in, *scores)

    ys = lax.optimization_barrier((*ys, scores[1], scores[3]))[:groups]
    part = own * width // NC
    keep, send = call(
        functools.partial(basis_body, own, rows, peers),
        (bf(part, width), bf(part, width)),
        [VM] * 4,
        [rows_scratch(width, width), rows_scratch(NC * part, width)],
        limit=8,
    )(*ys)
    got = over("c", 1, send)
    each = part // NX
    outs = call(
        core_body,
        tuple(bf(each + 2 * lot, width) for _ in range(NX)),
        [VM] * 4,
        [pltpu.VMEM((part, width), F32)],
        limit=8,
    )(keep, got, coef_part, over("c", 1, coef_part))
    ins = [outs[0]] + [over("x", r, outs[r]) for r in range(1, NX)]

    grads = call(
        functools.partial(bwd_body, cap, own),
        tuple(bf(2, width // groups, rows) for _ in range(groups)),
        [VM] * 5 + [HB],
        [
            pltpu.VMEM((peers * per, LANES), F32),
            rows_scratch(nbase * rows, width),
            pltpu.VMEM((width, rows), F32),
            tables,
            dma((groups,)),
        ],
        limit=18,
    )(returned.reshape(peers * per, LANES), w_out, act, pg, self_weight, far(table))

    last = each // nz
    out = call(
        x_body,
        bf(nz, last + 2 * lot, width),
        [VM] * NX,
        [pltpu.VMEM((NX, lot, width), F32)],
        limit=4,
    )(*ins)
    out = lax.all_to_all(out, "z", split_axis=0, concat_axis=0, tiled=True)
    basis_grad, coef_grad = call(
        functools.partial(z_body, own),
        (jax.ShapeDtypeStruct((last, width), F32), jax.ShapeDtypeStruct((own, relations), F32)),
        [VM],
        limit=4,
    )(out)

    grads = [grads[0]] + [over("basis", r, grads[r]) for r in range(1, groups)]
    cols = width // groups
    entity_grad, activation = call(
        functools.partial(join_body, nblk),
        (bf(cols, ent_dev), bf(cols, ent_dev)),
        [VM] * groups,
        [pltpu.VMEM((groups, 2, cols, rows), F32)],
        limit=4,
    )(*grads)
    return (activation.T, basis_grad.reshape(own, width // peers, width), coef_grad.T, entity_grad.T)


def solution(mesh):
    nz = mesh.devices.shape[0] // (NX * NC)
    fine = Mesh(mesh.devices.reshape(nz, NX, NC, mesh.devices.shape[1]), (*ENT, "basis"))
    placed = (
        P(ENT, None),
        P(),
        P("basis", None, None),
        P(None, "basis"),
        P(ENT, None, None),
        P(ENT, None, None),
        P(None, ENT, None),
        P(None, ENT, None),
        P(ENT, None),
    )
    return jax.shard_map(
        local,
        mesh=fine,
        in_specs=placed,
        out_specs=(P(ENT, "basis"), P("basis", ENT, None), P(None, "basis"), P(ENT, "basis")),
        check_vma=False,
    )
```

```python
import functools

import jax
import jax.numpy as jnp
from jax import lax
from jax.experimental import pallas as pl
from jax.experimental.pallas import tpu as pltpu
from jax.sharding import Mesh
from jax.sharding import PartitionSpec as P

BLK = 128
LANES = 128
NX = 4
NC = 2
ENT = ("z", "x", "c")
BF = jnp.bfloat16
F32 = jnp.float32
NT = (((1,), (1,)), ((), ()))
TN = (((0,), (0,)), ((), ()))
MIB = 1024 * 1024
VM = pl.BlockSpec(memory_space=pltpu.VMEM)
SM = pl.BlockSpec(memory_space=pltpu.SMEM)
COST = pl.CostEstimate(flops=8 * 10**9, transcendentals=0, bytes_accessed=20 * 10**6)
HB = pl.BlockSpec(memory_space=pltpu.HBM)


def call(body, outs, ins, scratch=(), limit=16, outs_in=None, cost=None):
    return pl.pallas_call(
        body,
        out_shape=outs,
        in_specs=ins,
        out_specs=outs_in or jax.tree.map(lambda _: VM, outs),
        scratch_shapes=list(scratch),
        cost_estimate=cost,
        compiler_params=pltpu.CompilerParams(vmem_limit_bytes=limit * MIB),
    )


def bf(*shape):
    return jax.ShapeDtypeStruct(shape, BF)


def hbm(*shape):
    return pltpu.HBM(shape, BF)


def far(value):
    return pltpu.with_memory_space_constraint(value, pltpu.HBM)


def get(ref, at):
    return jnp.concatenate([ref[h, at, :] for h in range(ref.shape[0])], axis=1)


def put(ref, at, value):
    for h in range(ref.shape[0]):
        ref[h, at, :] = value[:, h * LANES : (h + 1) * LANES]


def rows_scratch(rows, width):
    return pltpu.VMEM((width // LANES, rows, LANES), F32)


def turn(i, r, n):
    return lax.rem(i + r + n, n)


def aligned(i, size):
    return pl.ds(pl.multiple_of(i * size, size), size)


def digits(value):
    high = value.astype(BF)
    return high, (value - high.astype(F32)).astype(BF)


def start_all(copies):
    for copy in copies:
        copy.start()
    return copies


def wait_all(copies):
    for copy in copies:
        copy.wait()


def own_row_copies(ref, scr, sem, share):
    first = lax.axis_index("basis") * share
    return [
        pltpu.make_async_copy(
            ref.at[pl.ds(pl.multiple_of(n * BLK + first, share), share), :],
            scr.at[pl.ds(n * share, share), :],
            sem.at[n],
        )
        for n in range(scr.shape[0] // share)
    ]


def line(ref):
    return jnp.concatenate([ref[c : c + 1, :] for c in range(ref.shape[0])], axis=1)


def take_body(share, src_ref, edge_ref, ent_ref, out_ref, idx_ref, rel_ref, own, outs, isem, sem, osem):
    copies = own_row_copies(ent_ref, own, sem, share)
    copies += [pltpu.make_async_copy(src_ref, idx_ref, isem.at[0]), pltpu.make_async_copy(edge_ref, rel_ref, isem.at[1])]
    wait_all(start_all(copies))
    cap, peers = idx_ref.shape
    halves = own.shape[1] // LANES
    lane = lax.broadcasted_iota(jnp.int32, (8, LANES), 1)
    lots = osem.shape[0]
    lot = peers // lots
    copies = []
    for q in range(peers):
        note = jnp.zeros((8, LANES), jnp.int32)
        for c in range(cap):
            block = own[aligned(idx_ref[c, q], share), :]
            for h in range(halves):
                outs[q, pl.ds((c * halves + h) * share, share), :] = block[:, h * LANES : (h + 1) * LANES]
            rel = rel_ref[c, q]
            note = jnp.where(lane == 2 * c, rel >> 8, note)
            note = jnp.where(lane == 2 * c + 1, rel & 255, note)
        outs[q, pl.ds(cap * halves * share, 8), :] = note.astype(F32).astype(BF)
        if (q + 1) % lot == 0:
            i = q // lot
            at = pl.ds(i * lot, lot)
            copies += start_all([pltpu.make_async_copy(outs.at[at], out_ref.at[at], osem.at[i])])
    wait_all(copies)


def slot_weights(own, coef_refs, rel, blk, nblk, cs):
    groups = len(coef_refs)
    rows, width = coef_refs[0].shape
    chunks = rows // 16
    slots = rel.shape[1]
    parts = [jnp.zeros((16, slots), F32) for _ in coef_refs]
    for j in range(chunks):
        ids = lax.broadcasted_iota(jnp.int32, (width, slots), 0) + j * width
        hot = jnp.where(ids == rel, 1.0, 0.0).astype(BF)
        for r, ref in enumerate(coef_refs):
            parts[r] += jnp.dot(ref[pl.ds(j * 16, 16), :], hot, preferred_element_type=F32)
    for r in range(groups):
        cs[turn(lax.axis_index("basis"), -r, groups)] = parts[r][:own]
    coef = cs[...].reshape(groups * own, slots)
    return jnp.concatenate([jnp.where(blk == n, coef, 0.0) for n in range(nblk)], axis=0)


def widen(x_ref, xf):
    step = 512

    def some(i, c):
        at = aligned(i, step)
        xf[at, :] = x_ref[at, :].astype(F32)
        return c

    lax.fori_loop(0, x_ref.shape[0] // step, some, 0)


def slot_rows(xf, peers, cap, halves, share, k):
    per = xf.shape[0] // peers
    return jnp.concatenate(
        [
            jnp.concatenate(
                [xf[pl.ds((c * halves + h) * share + k, peers, stride=per), :] for h in range(halves)], axis=1
            )
            for c in range(cap)
        ],
        axis=0,
    )


def rows_of(mf, base, nbase, nblk, share):
    return jnp.concatenate([get(mf, aligned(n * nbase + base, share)) for n in range(nblk)], axis=0)


def table_copies(table_ref, tab, sem):
    return [pltpu.make_async_copy(table_ref.at[g], tab.at[g], sem.at[g]) for g in range(tab.shape[0])]


def fwd_body(
    cap, nblk, own, dst_ref, count_ref, x_ref, dstv_ref, cnt_ref, c0, c1, c2, c3, sw_ref, table_ref, ent_ref,
    cot_ref, y0, y1, y2, y3, back_ref, pg_ref, rel_ref, act_ref,
    xf, mf, cs, at_ref, tab, ent, cot, ysc, back, tsem, esem, csem, ysem, psem, bsem,
):
    groups = tab.shape[0]
    nbase = groups * own
    width = tab.shape[2]
    halves = width // LANES
    share = BLK // groups
    peers = back.shape[0]
    per = xf.shape[0] // peers
    group0 = lax.axis_index("basis")
    first = group0 * share
    ecopies = start_all(own_row_copies(ent_ref, ent, esem, share))
    tcopies = start_all(table_copies(table_ref, tab, tsem))
    ccopies = start_all(own_row_copies(cot_ref, cot, csem, share))
    widen(x_ref, xf)
    notes = xf[pl.ds(cap * halves * share, peers, stride=per), :].astype(BF)
    lane = lax.broadcasted_iota(jnp.int32, (8, LANES), 1)
    row = lax.broadcasted_iota(jnp.int32, (8, LANES), 0)
    pick = jnp.where(lane == 2 * row, 256.0, jnp.where(lane == 2 * row + 1, 1.0, 0.0)).astype(BF)
    rels = lax.dot_general(pick, notes, NT, preferred_element_type=F32).astype(jnp.int32)
    rel = jnp.concatenate([rels[c : c + 1] for c in range(cap)], axis=1)
    rel_ref[...] = rel
    w = slot_weights(own, (c0, c1, c2, c3), rel, line(dstv_ref), nblk, cs)
    cnt = line(cnt_ref)

    def one(k, c):
        xk = slot_rows(xf, peers, cap, halves, share, k).astype(BF)
        wk = jnp.where(cnt > first + k, w, 0.0).astype(BF)
        put(mf, pl.ds(k, w.shape[0], stride=share), jnp.dot(wk, xk, preferred_element_type=F32))
        return c

    lax.fori_loop(0, share, one, 0, unroll=8)
    copies = []
    wait_all(ecopies)
    acc = jnp.dot(ent[...], sw_ref[...], preferred_element_type=F32)
    rows = nblk * share
    ys = (y0, y1, y2, y3)
    wait_all(tcopies)
    for r in range(groups):
        group = turn(group0, r, groups)
        for b in range(own):
            mb = rows_of(mf, group * own + b, nbase, nblk, share).astype(BF)
            ysc[r, pl.ds(b * rows, rows), :] = mb
            acc += jnp.dot(mb, tab[group, pl.ds(b * width, width), :], preferred_element_type=F32)
        if r:
            at = pl.ds(0, own * rows)
            copies += start_all([pltpu.make_async_copy(ysc.at[r, at], ys[r].at[at], ysem.at[r])])
    s = jax.nn.sigmoid(acc)
    at_ref[...] = (acc * s).T
    wait_all(ccopies)
    pg = (cot[...].astype(F32) * (s * (1.0 + acc * (1.0 - s)))).astype(BF)
    pg_ref[...] = pg
    k_of = lax.broadcasted_iota(jnp.int32, (share, width), 0) + first
    lots = bsem.shape[0]
    lot = peers // lots
    for q in range(peers):
        for c in range(cap):
            block = pg_ref[aligned(dst_ref[c, q], share), :]
            block = jnp.where(k_of < count_ref[c, q], block.astype(F32), 0.0).astype(BF)
            for h in range(halves):
                back[q, pl.ds((c * halves + h) * share, share), :] = block[:, h * LANES : (h + 1) * LANES]
        if (q + 1) % lot == 0:
            i = q // lot
            at = pl.ds(i * lot, lot)
            copies += start_all([pltpu.make_async_copy(back.at[at], back_ref.at[at], bsem.at[i])])
    cols = width // groups
    at = pl.ds(own * rows, rows)
    for r in range(groups):
        ysc[r, at, :] = pg
        copies += start_all([pltpu.make_async_copy(ysc.at[r, at] if r else ysc.at[r], ys[r].at[at] if r else ys[r], psem.at[r])])
        act_ref[r] = at_ref[aligned(turn(group0, r, groups), cols), :].astype(BF)
    wait_all(copies)


def score_body(
    cap, nblk, own, halves, pg_ref, dstv_ref, cnt_ref, x_ref, rel_ref, src_ref, c0, c1, c2, c3, table_ref,
    s0, s1, s2, s3, w_ref, xf, pf, ts, tab, cs, tsem,
):
    groups = tab.shape[0]
    nbase = groups * own
    width = tab.shape[2]
    peers = cnt_ref.shape[1]
    slots = cap * peers
    share = BLK // groups
    group0 = lax.axis_index("basis")
    first = group0 * share
    tcopies = start_all(table_copies(table_ref, tab, tsem))
    w_ref[...] = slot_weights(own, (c0, c1, c2, c3), line(rel_ref), line(src_ref), nblk, cs).astype(BF)
    widen(x_ref, xf)
    pg = pg_ref[...]
    for b in range(nbase):
        if b % own == 0:
            tcopies[b // own].wait()
        base = tab[b // own, pl.ds((b % own) * width, width), :]
        p = lax.dot_general(pg, base, NT, preferred_element_type=F32)
        for n in range(nblk):
            put(pf, pl.ds((n * nbase + b) * share, share), p[n * share : (n + 1) * share])
    cnt = line(cnt_ref)

    def one(k, acc):
        pk = get(pf, pl.ds(k, nblk * nbase, stride=share)).astype(BF)
        xk = slot_rows(xf, peers, cap, halves, share, k).astype(BF)
        t = lax.dot_general(pk, xk, NT, preferred_element_type=F32)
        return acc + jnp.where(cnt > first + k, t, 0.0)

    acc = lax.fori_loop(0, share, one, jnp.zeros((nblk * nbase, slots), F32), unroll=4)
    blk = line(dstv_ref)
    total = jnp.zeros((nbase, slots), F32)
    for n in range(nblk):
        total += jnp.where(blk == n, acc[n * nbase : (n + 1) * nbase], 0.0)
    ts[...] = total
    for r, out in enumerate((s0, s1, s2, s3)):
        out[...] = ts[aligned(turn(group0, r, groups), own), :]


def coef_body(rel_ref, s0, s1, s2, s3, out_ref):
    own, slots = s0.shape
    width = out_ref.shape[1]
    chunks = out_ref.shape[0] // own
    high, low = digits((s0[...] + s1[...]) + (s2[...] + s3[...]))
    both = jnp.concatenate([high.astype(F32), low.astype(F32)], axis=0).astype(BF)
    rel = rel_ref[...]
    parts = []
    for j in range(chunks):
        ids = lax.broadcasted_iota(jnp.int32, (width, slots), 0) + j * width
        hot = jnp.where(ids == rel, 1.0, 0.0).astype(BF)
        t = lax.dot_general(both, hot, NT, preferred_element_type=F32)
        parts.append(t[:own] + t[own:])
    out_ref[...] = jnp.concatenate(parts, axis=0).astype(BF)


def basis_body(own, rows, peers, y0, y1, y2, y3, keep_ref, send_ref, tmp, outf):
    ys = (y0, y1, y2, y3)
    width = y0.shape[1]
    part = keep_ref.shape[0]
    each = part // NX
    deep = part * NC // (own * peers)
    nz = each // (own * deep)
    pg = jnp.concatenate([y[pl.ds(own * rows, rows), :] for y in ys], axis=0)
    for b in range(own):
        m = jnp.concatenate([y[pl.ds(b * rows, rows), :] for y in ys], axis=0)
        put(tmp, pl.ds(0, width), lax.dot_general(m, pg, TN, preferred_element_type=F32))
        for c in range(NC):
            for x in range(NX):
                for d in range(deep):
                    put(
                        outf,
                        pl.ds((c * NX + x) * each + b * deep + d, nz, stride=own * deep),
                        get(tmp, pl.ds((x * NC + c) * deep + d, nz, stride=NX * NC * deep)),
                    )
    core = lax.axis_index("c")
    keep_ref[...] = get(outf, aligned(core, part)).astype(BF)
    send_ref[...] = get(outf, aligned(1 - core, part)).astype(BF)


def core_body(keep_ref, got_ref, coef_ref, other_ref, o0, o1, o2, o3, sums):
    part = keep_ref.shape[0]
    each = part // NX
    sums[...] = keep_ref[...].astype(F32) + got_ref[...].astype(F32)
    coef = (coef_ref[...].astype(F32) + other_ref[...].astype(F32)).astype(BF)
    for r, out in enumerate((o0, o1, o2, o3)):
        out[pl.ds(0, each), :] = sums[aligned(turn(lax.axis_index("x"), r, NX), each), :].astype(BF)
        out[pl.ds(each, coef.shape[0]), :] = coef


def x_body(i0, i1, i2, i3, out_ref, order):
    n = order.shape[1]
    each = i0.shape[0] - n
    nz = out_ref.shape[0]
    last = each // nz
    sums = sum(i[pl.ds(0, each), :].astype(F32) for i in (i0, i1, i2, i3))
    for r, i in enumerate((i0, i1, i2, i3)):
        order[turn(lax.axis_index("x"), -r, NX)] = i[pl.ds(each, n), :].astype(F32)
    coef = ((order[0] + order[1]) + (order[2] + order[3])).astype(BF)
    for z in range(nz):
        out_ref[z, pl.ds(0, last), :] = sums[z * last : (z + 1) * last].astype(BF)
        out_ref[z, pl.ds(last, n), :] = coef


def z_body(own, in_ref, basis_ref, coef_ref):
    nz, rows, width = in_ref.shape
    last = basis_ref.shape[0]
    n = rows - last
    basis = jnp.zeros((last, width), F32)
    coef = jnp.zeros((n, width), F32)
    for z in range(nz):
        basis += in_ref[z, pl.ds(0, last), :].astype(F32)
        coef += in_ref[z, pl.ds(last, n), :].astype(F32)
    basis_ref[...] = basis
    relations = coef_ref.shape[1]
    for j in range(n // own):
        size = min(width, relations - j * width)
        coef_ref[:, pl.ds(j * width, size)] = coef[j * own : (j + 1) * own, :size]


def bwd_body(
    cap, own, x_ref, w_ref, act_ref, pg_ref, sw_ref, table_ref, o0, o1, o2, o3, xf, mf, at_ref, tab, tsem
):
    groups = tab.shape[0]
    nbase = groups * own
    width = tab.shape[2]
    halves = width // LANES
    share = BLK // groups
    slots = w_ref.shape[1]
    peers = slots // cap
    nblk = w_ref.shape[0] // nbase
    tcopies = start_all(table_copies(table_ref, tab, tsem))
    widen(x_ref, xf)
    w = w_ref[...]

    def one(k, c):
        xk = slot_rows(xf, peers, cap, halves, share, k).astype(BF)
        put(mf, pl.ds(k, w.shape[0], stride=share), jnp.dot(w, xk, preferred_element_type=F32))
        return c

    lax.fori_loop(0, share, one, 0, unroll=8)
    acc = lax.dot_general(pg_ref[...], sw_ref[...], NT, preferred_element_type=F32)
    wait_all(tcopies)
    for b in range(nbase):
        mb = rows_of(mf, b, nbase, nblk, share).astype(BF)
        base = tab[b // own, pl.ds((b % own) * width, width), :]
        acc += lax.dot_general(mb, base, NT, preferred_element_type=F32)
    at_ref[...] = acc.T
    cols = width // groups
    for r, out in enumerate((o0, o1, o2, o3)):
        out[0] = at_ref[aligned(turn(lax.axis_index("basis"), r, groups), cols), :].astype(BF)
        out[1] = act_ref[r]


def join_body(nblk, i0, i1, i2, i3, grad_ref, act_ref, order):
    groups = order.shape[0]
    share = BLK // groups
    for r, i in enumerate((i0, i1, i2, i3)):
        order[turn(lax.axis_index("basis"), -r, groups)] = i[...].astype(F32)
    for j, out in enumerate((grad_ref, act_ref)):
        for n in range(nblk):
            whole = jnp.concatenate([order[g, j, :, n * share : (n + 1) * share] for g in range(groups)], axis=1)
            out[:, n * BLK : (n + 1) * BLK] = whole.astype(BF)


def local(
    entity_rows,
    self_weight,
    bases,
    coefficients,
    send_block,
    edge_rel,
    edge_dst,
    edge_count,
    cotangent,
):
    peers = lax.axis_size(ENT)
    groups = lax.axis_size("basis")
    ent_dev, width = entity_rows.shape
    nblk = ent_dev // BLK
    own = bases.shape[0]
    nbase = own * groups
    relations = coefficients.shape[0]
    cap = send_block.shape[2]
    slots = peers * cap
    share = BLK // groups
    halves = width // LANES
    nz = lax.axis_size("z")
    rows = nblk * share
    dma = pltpu.SemaphoreType.DMA

    def over(axis, r, value):
        n = lax.axis_size(axis)
        return lax.ppermute(value, axis, [(i, (i + r) % n) for i in range(n)])

    src, rel_out = send_block[0].T, edge_rel[0].T
    dst, cnt = edge_dst[:, 0, :].T, edge_count[:, 0, :].T

    per = cap * halves * share
    outgoing = call(
        functools.partial(take_body, share),
        hbm(peers, per + 8, LANES),
        [HB] * 3,
        [
            pltpu.SMEM((cap, peers), jnp.int32),
            pltpu.SMEM((cap, peers), jnp.int32),
            pltpu.VMEM((rows, width), BF),
            pltpu.VMEM((peers, per + 8, LANES), BF),
            dma((2,)),
            dma((nblk,)),
            dma((4,)),
        ],
        outs_in=HB,
    )(far(src), far(rel_out), far(entity_rows))
    incoming = lax.all_to_all(outgoing, ENT, split_axis=0, concat_axis=0, tiled=True)

    bases, _ = lax.optimization_barrier((bases, outgoing))
    table = lax.all_gather(bases.reshape(own * width, width), "basis")
    chunks = -(-relations // width)
    coef = jnp.pad(coefficients.astype(BF).T, ((0, 16 - own), (0, chunks * width - relations)))
    coef = coef.reshape(16, chunks, width).transpose(1, 0, 2).reshape(chunks * 16, width)
    coefs = [coef] + [over("basis", r, coef) for r in range(1, groups)]
    tables = pltpu.VMEM((groups, own * width, width), BF)
    incoming = incoming.reshape(peers * (per + 8), LANES)
    *ys, back, pg, rel_in, act = call(
        functools.partial(fwd_body, cap, nblk, own),
        (
            *[hbm((own + 1) * rows, width) for _ in range(groups)],
            hbm(peers, per, LANES),
            bf(rows, width),
            jax.ShapeDtypeStruct((1, slots), jnp.int32),
            bf(groups, width // groups, rows),
        ),
        [SM] * 2 + [VM] * 8 + [HB] * 3,
        [
            pltpu.VMEM((peers * (per + 8), LANES), F32),
            rows_scratch(nbase * rows, width),
            pltpu.VMEM((groups, own, slots), F32),
            pltpu.VMEM((width, rows), F32),
            tables,
            pltpu.VMEM((rows, width), BF),
            pltpu.VMEM((rows, width), BF),
            pltpu.VMEM((groups, (own + 1) * rows, width), BF),
            pltpu.VMEM((peers, per, LANES), BF),
            dma((groups,)),
            dma((nblk,)),
            dma((nblk,)),
            dma((groups,)),
            dma((groups,)),
            dma((4,)),
        ],
        limit=28,
        outs_in=(HB,) * (groups + 1) + (VM,) * 3,
    )(
        dst, cnt, incoming, dst, cnt, *coefs, self_weight, far(table),
        far(entity_rows), far(cotangent),
    )

    returned = lax.all_to_all(back, ENT, split_axis=0, concat_axis=0, tiled=True)
    ys = [ys[0]] + [over("basis", r, ys[r]) for r in range(1, groups)]

    *scores, w_out = call(
        functools.partial(score_body, cap, nblk, own, halves),
        (*[jax.ShapeDtypeStruct((own, slots), F32) for _ in range(groups)], bf(nblk * nbase, slots)),
        [VM] * 10 + [HB],
        [
            pltpu.VMEM((peers * (per + 8), LANES), F32),
            rows_scratch(nbase * rows, width),
            pltpu.VMEM((nbase, slots), F32),
            tables,
            pltpu.VMEM((groups, own, slots), F32),
            dma((groups,)),
        ],
        limit=18,
        cost=COST,
    )(pg, dst, cnt, incoming, rel_out, src, *coefs, far(table))
    scores = [scores[0]] + [over("basis", r, scores[r]) for r in range(1, groups)]
    lot = chunks * own
    coef_part = call(coef_body, bf(lot, width), [VM] * 5, limit=4)(rel_in, *scores)

    ys = lax.optimization_barrier((*ys, scores[1], scores[3]))[:groups]
    part = own * width // NC
    keep, send = call(
        functools.partial(basis_body, own, rows, peers),
        (bf(part, width), bf(part, width)),
        [VM] * 4,
        [rows_scratch(width, width), rows_scratch(NC * part, width)],
        limit=8,
    )(*ys)
    got = over("c", 1, send)
    each = part // NX
    outs = call(
        core_body,
        tuple(bf(each + lot, width) for _ in range(NX)),
        [VM] * 4,
        [pltpu.VMEM((part, width), F32)],
        limit=8,
    )(keep, got, coef_part, over("c", 1, coef_part))
    ins = [outs[0]] + [over("x", r, outs[r]) for r in range(1, NX)]

    grads = call(
        functools.partial(bwd_body, cap, own),
        tuple(bf(2, width // groups, rows) for _ in range(groups)),
        [VM] * 5 + [HB],
        [
            pltpu.VMEM((peers * per, LANES), F32),
            rows_scratch(nbase * rows, width),
            pltpu.VMEM((width, rows), F32),
            tables,
            dma((groups,)),
        ],
        limit=18,
    )(returned.reshape(peers * per, LANES), w_out, act, pg, self_weight, far(table))

    ins = lax.optimization_barrier((*ins, grads[0]))[:NX]
    last = each // nz
    out = call(
        x_body,
        bf(nz, last + lot, width),
        [VM] * NX,
        [pltpu.VMEM((NX, lot, width), F32)],
        limit=4,
    )(*ins)
    out = lax.all_to_all(out, "z", split_axis=0, concat_axis=0, tiled=True)
    basis_grad, coef_grad = call(
        functools.partial(z_body, own),
        (jax.ShapeDtypeStruct((last, width), F32), jax.ShapeDtypeStruct((own, relations), F32)),
        [VM],
        limit=4,
    )(out)

    grads = [grads[0]] + [over("basis", r, grads[r]) for r in range(1, groups)]
    cols = width // groups
    entity_grad, activation = call(
        functools.partial(join_body, nblk),
        (bf(cols, ent_dev), bf(cols, ent_dev)),
        [VM] * groups,
        [pltpu.VMEM((groups, 2, cols, rows), F32)],
        limit=4,
    )(*grads)
    return (activation.T, basis_grad.reshape(own, width // peers, width), coef_grad.T, entity_grad.T)


def solution(mesh):
    nz = mesh.devices.shape[0] // (NX * NC)
    fine = Mesh(mesh.devices.reshape(nz, NX, NC, mesh.devices.shape[1]), (*ENT, "basis"))
    placed = (
        P(ENT, None),
        P(),
        P("basis", None, None),
        P(None, "basis"),
        P(ENT, None, None),
        P(ENT, None, None),
        P(None, ENT, None),
        P(None, ENT, None),
        P(ENT, None),
    )
    return jax.shard_map(
        local,
        mesh=fine,
        in_specs=placed,
        out_specs=(P(ENT, "basis"), P("basis", ENT, None), P(None, "basis"), P(ENT, "basis")),
        check_vma=False,
    )
```

```python
import functools

import jax
import jax.numpy as jnp
from jax import lax
from jax.experimental import pallas as pl
from jax.experimental.pallas import tpu as pltpu
from jax.sharding import Mesh
from jax.sharding import PartitionSpec as P

BLK = 128
LANES = 128
NX = 4
NC = 2
ENT = ("z", "x", "c")
BF = jnp.bfloat16
F32 = jnp.float32
NT = (((1,), (1,)), ((), ()))
TN = (((0,), (0,)), ((), ()))
MIB = 1024 * 1024
VM = pl.BlockSpec(memory_space=pltpu.VMEM)
SM = pl.BlockSpec(memory_space=pltpu.SMEM)
COST = pl.CostEstimate(flops=8 * 10**9, transcendentals=0, bytes_accessed=20 * 10**6)
HB = pl.BlockSpec(memory_space=pltpu.HBM)


def call(body, outs, ins, scratch=(), limit=16, outs_in=None, cost=None):
    return pl.pallas_call(
        body,
        out_shape=outs,
        in_specs=ins,
        out_specs=outs_in or jax.tree.map(lambda _: VM, outs),
        scratch_shapes=list(scratch),
        cost_estimate=cost,
        compiler_params=pltpu.CompilerParams(vmem_limit_bytes=limit * MIB),
    )


def bf(*shape):
    return jax.ShapeDtypeStruct(shape, BF)


def hbm(*shape):
    return pltpu.HBM(shape, BF)


def far(value):
    return pltpu.with_memory_space_constraint(value, pltpu.HBM)


def get(ref, at):
    return jnp.concatenate([ref[h, at, :] for h in range(ref.shape[0])], axis=1)


def put(ref, at, value):
    for h in range(ref.shape[0]):
        ref[h, at, :] = value[:, h * LANES : (h + 1) * LANES]


def rows_scratch(rows, width):
    return pltpu.VMEM((width // LANES, rows, LANES), F32)


def turn(i, r, n):
    return lax.rem(i + r + n, n)


def aligned(i, size):
    return pl.ds(pl.multiple_of(i * size, size), size)


def digits(value):
    high = value.astype(BF)
    return high, (value - high.astype(F32)).astype(BF)


def start_all(copies):
    for copy in copies:
        copy.start()
    return copies


def wait_all(copies):
    for copy in copies:
        copy.wait()


def own_row_copies(ref, scr, sem, share):
    first = lax.axis_index("basis") * share
    return [
        pltpu.make_async_copy(
            ref.at[pl.ds(pl.multiple_of(n * BLK + first, share), share), :],
            scr.at[pl.ds(n * share, share), :],
            sem.at[n],
        )
        for n in range(scr.shape[0] // share)
    ]


def line(ref):
    return jnp.concatenate([ref[c : c + 1, :] for c in range(ref.shape[0])], axis=1)


def take_body(share, src_ref, edge_ref, ent_ref, out_ref, idx_ref, rel_ref, own, outs, isem, sem, osem):
    copies = own_row_copies(ent_ref, own, sem, share)
    copies += [pltpu.make_async_copy(src_ref, idx_ref, isem.at[0]), pltpu.make_async_copy(edge_ref, rel_ref, isem.at[1])]
    wait_all(start_all(copies))
    cap, peers = idx_ref.shape
    halves = own.shape[1] // LANES
    lane = lax.broadcasted_iota(jnp.int32, (8, LANES), 1)
    lots = osem.shape[0]
    lot = peers // lots
    copies = []
    for q in range(peers):
        note = jnp.zeros((8, LANES), jnp.int32)
        for c in range(cap):
            block = own[aligned(idx_ref[c, q], share), :]
            for h in range(halves):
                outs[q, pl.ds((c * halves + h) * share, share), :] = block[:, h * LANES : (h + 1) * LANES]
            rel = rel_ref[c, q]
            note = jnp.where(lane == 2 * c, rel >> 8, note)
            note = jnp.where(lane == 2 * c + 1, rel & 255, note)
        outs[q, pl.ds(cap * halves * share, 8), :] = note.astype(F32).astype(BF)
        if (q + 1) % lot == 0:
            i = q // lot
            at = pl.ds(i * lot, lot)
            copies += start_all([pltpu.make_async_copy(outs.at[at], out_ref.at[at], osem.at[i])])
    wait_all(copies)


def slot_weights(own, coef_refs, rel, blk, nblk, cs):
    groups = len(coef_refs)
    rows, width = coef_refs[0].shape
    chunks = rows // 16
    slots = rel.shape[1]
    parts = [jnp.zeros((16, slots), F32) for _ in coef_refs]
    for j in range(chunks):
        ids = lax.broadcasted_iota(jnp.int32, (width, slots), 0) + j * width
        hot = jnp.where(ids == rel, 1.0, 0.0).astype(BF)
        for r, ref in enumerate(coef_refs):
            parts[r] += jnp.dot(ref[pl.ds(j * 16, 16), :], hot, preferred_element_type=F32)
    for r in range(groups):
        cs[turn(lax.axis_index("basis"), -r, groups)] = parts[r][:own]
    coef = cs[...].reshape(groups * own, slots)
    return jnp.concatenate([jnp.where(blk == n, coef, 0.0) for n in range(nblk)], axis=0)


def widen(x_ref, xf):
    step = 512

    def some(i, c):
        at = aligned(i, step)
        xf[at, :] = x_ref[at, :].astype(F32)
        return c

    lax.fori_loop(0, x_ref.shape[0] // step, some, 0)


def slot_rows(xf, peers, cap, halves, share, k):
    per = xf.shape[0] // peers
    return jnp.concatenate(
        [
            jnp.concatenate(
                [xf[pl.ds((c * halves + h) * share + k, peers, stride=per), :] for h in range(halves)], axis=1
            )
            for c in range(cap)
        ],
        axis=0,
    )


def rows_of(mf, base, nbase, nblk, share):
    return jnp.concatenate([get(mf, aligned(n * nbase + base, share)) for n in range(nblk)], axis=0)


def table_copies(table_ref, tab, sem):
    return [pltpu.make_async_copy(table_ref.at[g], tab.at[g], sem.at[g]) for g in range(tab.shape[0])]


def fwd_body(
    cap, nblk, own, dst_ref, count_ref, x_ref, dstv_ref, cnt_ref, c0, c1, c2, c3, sw_ref, table_ref, ent_ref,
    cot_ref, y0, y1, y2, y3, back_ref, pg_ref, rel_ref, act_ref,
    xf, mf, cs, at_ref, tab, ent, cot, ysc, back, tsem, esem, csem, ysem, psem, bsem,
):
    groups = tab.shape[0]
    nbase = groups * own
    width = tab.shape[2]
    halves = width // LANES
    share = BLK // groups
    peers = back.shape[0]
    per = xf.shape[0] // peers
    group0 = lax.axis_index("basis")
    first = group0 * share
    ecopies = start_all(own_row_copies(ent_ref, ent, esem, share))
    tcopies = start_all(table_copies(table_ref, tab, tsem))
    ccopies = start_all(own_row_copies(cot_ref, cot, csem, share))
    widen(x_ref, xf)
    notes = xf[pl.ds(cap * halves * share, peers, stride=per), :].astype(BF)
    lane = lax.broadcasted_iota(jnp.int32, (8, LANES), 1)
    row = lax.broadcasted_iota(jnp.int32, (8, LANES), 0)
    pick = jnp.where(lane == 2 * row, 256.0, jnp.where(lane == 2 * row + 1, 1.0, 0.0)).astype(BF)
    rels = lax.dot_general(pick, notes, NT, preferred_element_type=F32).astype(jnp.int32)
    rel = jnp.concatenate([rels[c : c + 1] for c in range(cap)], axis=1)
    rel_ref[...] = rel
    w = slot_weights(own, (c0, c1, c2, c3), rel, line(dstv_ref), nblk, cs)
    cnt = line(cnt_ref)

    def one(k, c):
        xk = slot_rows(xf, peers, cap, halves, share, k).astype(BF)
        wk = jnp.where(cnt > first + k, w, 0.0).astype(BF)
        put(mf, pl.ds(k, w.shape[0], stride=share), jnp.dot(wk, xk, preferred_element_type=F32))
        return c

    lax.fori_loop(0, share, one, 0, unroll=8)
    copies = []
    wait_all(ecopies)
    acc = jnp.dot(ent[...], sw_ref[...], preferred_element_type=F32)
    rows = nblk * share
    ys = (y0, y1, y2, y3)
    wait_all(tcopies)
    for r in range(groups):
        group = turn(group0, r, groups)
        for b in range(own):
            mb = rows_of(mf, group * own + b, nbase, nblk, share).astype(BF)
            ysc[r, pl.ds(b * rows, rows), :] = mb
            acc += jnp.dot(mb, tab[group, pl.ds(b * width, width), :], preferred_element_type=F32)
        if r:
            at = pl.ds(0, own * rows)
            copies += start_all([pltpu.make_async_copy(ysc.at[r, at], ys[r].at[at], ysem.at[r])])
    s = jax.nn.sigmoid(acc)
    at_ref[...] = (acc * s).T
    wait_all(ccopies)
    pg = (cot[...].astype(F32) * (s * (1.0 + acc * (1.0 - s)))).astype(BF)
    pg_ref[...] = pg
    k_of = lax.broadcasted_iota(jnp.int32, (share, width), 0) + first
    lots = bsem.shape[0]
    lot = peers // lots
    for q in range(peers):
        for c in range(cap):
            block = pg_ref[aligned(dst_ref[c, q], share), :]
            block = jnp.where(k_of < count_ref[c, q], block.astype(F32), 0.0).astype(BF)
            for h in range(halves):
                back[q, pl.ds((c * halves + h) * share, share), :] = block[:, h * LANES : (h + 1) * LANES]
        if (q + 1) % lot == 0:
            i = q // lot
            at = pl.ds(i * lot, lot)
            copies += start_all([pltpu.make_async_copy(back.at[at], back_ref.at[at], bsem.at[i])])
    cols = width // groups
    at = pl.ds(own * rows, rows)
    for r in range(groups):
        ysc[r, at, :] = pg
        copies += start_all([pltpu.make_async_copy(ysc.at[r, at] if r else ysc.at[r], ys[r].at[at] if r else ys[r], psem.at[r])])
        act_ref[r] = at_ref[aligned(turn(group0, r, groups), cols), :].astype(BF)
    wait_all(copies)


def score_body(
    cap, nblk, own, halves, pg_ref, dstv_ref, cnt_ref, x_ref, rel_ref, src_ref, c0, c1, c2, c3, table_ref,
    s0, s1, s2, s3, w_ref, xf, pf, ts, tab, cs, tsem,
):
    groups = tab.shape[0]
    nbase = groups * own
    width = tab.shape[2]
    peers = cnt_ref.shape[1]
    slots = cap * peers
    share = BLK // groups
    group0 = lax.axis_index("basis")
    first = group0 * share
    tcopies = start_all(table_copies(table_ref, tab, tsem))
    w_ref[...] = slot_weights(own, (c0, c1, c2, c3), line(rel_ref), line(src_ref), nblk, cs).astype(BF)
    widen(x_ref, xf)
    pg = pg_ref[...]
    for b in range(nbase):
        if b % own == 0:
            tcopies[b // own].wait()
        base = tab[b // own, pl.ds((b % own) * width, width), :]
        p = lax.dot_general(pg, base, NT, preferred_element_type=F32)
        for n in range(nblk):
            put(pf, pl.ds((n * nbase + b) * share, share), p[n * share : (n + 1) * share])
    cnt = line(cnt_ref)

    def one(k, acc):
        pk = get(pf, pl.ds(k, nblk * nbase, stride=share)).astype(BF)
        xk = slot_rows(xf, peers, cap, halves, share, k).astype(BF)
        t = lax.dot_general(pk, xk, NT, preferred_element_type=F32)
        return acc + jnp.where(cnt > first + k, t, 0.0)

    acc = lax.fori_loop(0, share, one, jnp.zeros((nblk * nbase, slots), F32), unroll=4)
    blk = line(dstv_ref)
    total = jnp.zeros((nbase, slots), F32)
    for n in range(nblk):
        total += jnp.where(blk == n, acc[n * nbase : (n + 1) * nbase], 0.0)
    ts[...] = total
    for r, out in enumerate((s0, s1, s2, s3)):
        out[...] = ts[aligned(turn(group0, r, groups), own), :]


def coef_body(rel_ref, s0, s1, s2, s3, out_ref):
    own, slots = s0.shape
    width = out_ref.shape[1]
    chunks = out_ref.shape[0] // own
    high, low = digits((s0[...] + s1[...]) + (s2[...] + s3[...]))
    both = jnp.concatenate([high.astype(F32), low.astype(F32)], axis=0).astype(BF)
    rel = rel_ref[...]
    parts = []
    for j in range(chunks):
        ids = lax.broadcasted_iota(jnp.int32, (width, slots), 0) + j * width
        hot = jnp.where(ids == rel, 1.0, 0.0).astype(BF)
        t = lax.dot_general(both, hot, NT, preferred_element_type=F32)
        parts.append(t[:own] + t[own:])
    out_ref[...] = jnp.concatenate(parts, axis=0).astype(BF)


def basis_body(own, rows, peers, y0, y1, y2, y3, keep_ref, send_ref, tmp, outf):
    ys = (y0, y1, y2, y3)
    width = y0.shape[1]
    part = keep_ref.shape[0]
    each = part // NX
    deep = part * NC // (own * peers)
    nz = each // (own * deep)
    pg = jnp.concatenate([y[pl.ds(own * rows, rows), :] for y in ys], axis=0)
    for b in range(own):
        m = jnp.concatenate([y[pl.ds(b * rows, rows), :] for y in ys], axis=0)
        put(tmp, pl.ds(0, width), lax.dot_general(m, pg, TN, preferred_element_type=F32))
        for c in range(NC):
            for x in range(NX):
                for d in range(deep):
                    put(
                        outf,
                        pl.ds((c * NX + x) * each + b * deep + d, nz, stride=own * deep),
                        get(tmp, pl.ds((x * NC + c) * deep + d, nz, stride=NX * NC * deep)),
                    )
    core = lax.axis_index("c")
    keep_ref[...] = get(outf, aligned(core, part)).astype(BF)
    send_ref[...] = get(outf, aligned(1 - core, part)).astype(BF)


def core_body(keep_ref, got_ref, coef_ref, other_ref, o0, o1, o2, o3, sums):
    part = keep_ref.shape[0]
    each = part // NX
    sums[...] = keep_ref[...].astype(F32) + got_ref[...].astype(F32)
    coef = (coef_ref[...].astype(F32) + other_ref[...].astype(F32)).astype(BF)
    for r, out in enumerate((o0, o1, o2, o3)):
        out[pl.ds(0, each), :] = sums[aligned(turn(lax.axis_index("x"), r, NX), each), :].astype(BF)
        out[pl.ds(each, coef.shape[0]), :] = coef


def x_body(i0, i1, i2, i3, out_ref, order):
    n = order.shape[1]
    each = i0.shape[0] - n
    nz = out_ref.shape[0]
    last = each // nz
    sums = sum(i[pl.ds(0, each), :].astype(F32) for i in (i0, i1, i2, i3))
    for r, i in enumerate((i0, i1, i2, i3)):
        order[turn(lax.axis_index("x"), -r, NX)] = i[pl.ds(each, n), :].astype(F32)
    coef = ((order[0] + order[1]) + (order[2] + order[3])).astype(BF)
    for z in range(nz):
        out_ref[z, pl.ds(0, last), :] = sums[z * last : (z + 1) * last].astype(BF)
        out_ref[z, pl.ds(last, n), :] = coef


def z_body(own, in_ref, basis_ref, coef_ref):
    nz, rows, width = in_ref.shape
    deep = basis_ref.shape[1]
    last = own * deep
    n = rows - last
    basis = jnp.zeros((last, width), F32)
    coef = jnp.zeros((n, width), F32)
    for z in range(nz):
        basis += in_ref[z, pl.ds(0, last), :].astype(F32)
        coef += in_ref[z, pl.ds(last, n), :].astype(F32)
    for b in range(own):
        basis_ref[b] = basis[b * deep : (b + 1) * deep]
    relations = coef_ref.shape[1]
    for j in range(n // own):
        size = min(width, relations - j * width)
        coef_ref[:, pl.ds(j * width, size)] = coef[j * own : (j + 1) * own, :size]


def bwd_body(
    cap, own, w_ref, act_ref, pg_ref, sw_ref, x_ref, table_ref, o0, o1, o2, o3, xb, xf, mf, at_ref, tab, xsem, tsem
):
    groups = tab.shape[0]
    nbase = groups * own
    width = tab.shape[2]
    halves = width // LANES
    share = BLK // groups
    slots = w_ref.shape[1]
    peers = slots // cap
    nblk = w_ref.shape[0] // nbase
    lots = xsem.shape[0]
    lot = xb.shape[0] // lots
    lots_at = [pl.ds(i * lot, lot) for i in range(lots)]
    xcopies = start_all([pltpu.make_async_copy(x_ref.at[at], xb.at[at], xsem.at[i]) for i, at in enumerate(lots_at)])
    tcopies = start_all(table_copies(table_ref, tab, tsem))
    w = w_ref[...]
    for copy, at in zip(xcopies, lots_at):
        copy.wait()
        widen(xb.at[at], xf.at[at])

    def one(k, c):
        xk = slot_rows(xf, peers, cap, halves, share, k).astype(BF)
        put(mf, pl.ds(k, w.shape[0], stride=share), jnp.dot(w, xk, preferred_element_type=F32))
        return c

    lax.fori_loop(0, share, one, 0, unroll=8)
    acc = lax.dot_general(pg_ref[...], sw_ref[...], NT, preferred_element_type=F32)
    wait_all(tcopies)
    for b in range(nbase):
        mb = rows_of(mf, b, nbase, nblk, share).astype(BF)
        base = tab[b // own, pl.ds((b % own) * width, width), :]
        acc += lax.dot_general(mb, base, NT, preferred_element_type=F32)
    at_ref[...] = acc.T
    cols = width // groups
    for r, out in enumerate((o0, o1, o2, o3)):
        out[0] = at_ref[aligned(turn(lax.axis_index("basis"), r, groups), cols), :].astype(BF)
        out[1] = act_ref[r]


def join_body(nblk, i0, i1, i2, i3, grad_ref, act_ref, order):
    groups = order.shape[0]
    share = BLK // groups
    for r, i in enumerate((i0, i1, i2, i3)):
        order[turn(lax.axis_index("basis"), -r, groups)] = i[...].astype(F32)
    for j, out in enumerate((grad_ref, act_ref)):
        for n in range(nblk):
            whole = jnp.concatenate([order[g, j, :, n * share : (n + 1) * share] for g in range(groups)], axis=1)
            out[:, n * BLK : (n + 1) * BLK] = whole.astype(BF)


def local(
    entity_rows,
    self_weight,
    bases,
    coefficients,
    send_block,
    edge_rel,
    edge_dst,
    edge_count,
    cotangent,
):
    peers = lax.axis_size(ENT)
    groups = lax.axis_size("basis")
    ent_dev, width = entity_rows.shape
    nblk = ent_dev // BLK
    own = bases.shape[0]
    nbase = own * groups
    relations = coefficients.shape[0]
    cap = send_block.shape[2]
    slots = peers * cap
    share = BLK // groups
    halves = width // LANES
    nz = lax.axis_size("z")
    rows = nblk * share
    dma = pltpu.SemaphoreType.DMA

    def over(axis, r, value):
        n = lax.axis_size(axis)
        return lax.ppermute(value, axis, [(i, (i + r) % n) for i in range(n)])

    src, rel_out = send_block[0].T, edge_rel[0].T
    dst, cnt = edge_dst[:, 0, :].T, edge_count[:, 0, :].T

    per = cap * halves * share
    outgoing = call(
        functools.partial(take_body, share),
        hbm(peers, per + 8, LANES),
        [HB] * 3,
        [
            pltpu.SMEM((cap, peers), jnp.int32),
            pltpu.SMEM((cap, peers), jnp.int32),
            pltpu.VMEM((rows, width), BF),
            pltpu.VMEM((peers, per + 8, LANES), BF),
            dma((2,)),
            dma((nblk,)),
            dma((4,)),
        ],
        outs_in=HB,
    )(far(src), far(rel_out), far(entity_rows))
    incoming = lax.all_to_all(outgoing, ENT, split_axis=0, concat_axis=0, tiled=True)

    bases, _ = lax.optimization_barrier((bases, outgoing))
    table = lax.all_gather(bases.reshape(own * width, width), "basis")
    chunks = -(-relations // width)
    coef = jnp.pad(coefficients.astype(BF).T, ((0, 16 - own), (0, chunks * width - relations)))
    coef = coef.reshape(16, chunks, width).transpose(1, 0, 2).reshape(chunks * 16, width)
    coefs = [coef] + [over("basis", r, coef) for r in range(1, groups)]
    tables = pltpu.VMEM((groups, own * width, width), BF)
    incoming = incoming.reshape(peers * (per + 8), LANES)
    *ys, back, pg, rel_in, act = call(
        functools.partial(fwd_body, cap, nblk, own),
        (
            *[hbm((own + 1) * rows, width) for _ in range(groups)],
            hbm(peers, per, LANES),
            bf(rows, width),
            jax.ShapeDtypeStruct((1, slots), jnp.int32),
            bf(groups, width // groups, rows),
        ),
        [SM] * 2 + [VM] * 8 + [HB] * 3,
        [
            pltpu.VMEM((peers * (per + 8), LANES), F32),
            rows_scratch(nbase * rows, width),
            pltpu.VMEM((groups, own, slots), F32),
            pltpu.VMEM((width, rows), F32),
            tables,
            pltpu.VMEM((rows, width), BF),
            pltpu.VMEM((rows, width), BF),
            pltpu.VMEM((groups, (own + 1) * rows, width), BF),
            pltpu.VMEM((peers, per, LANES), BF),
            dma((groups,)),
            dma((nblk,)),
            dma((nblk,)),
            dma((groups,)),
            dma((groups,)),
            dma((4,)),
        ],
        limit=28,
        outs_in=(HB,) * (groups + 1) + (VM,) * 3,
    )(
        dst, cnt, incoming, dst, cnt, *coefs, self_weight, far(table),
        far(entity_rows), far(cotangent),
    )

    returned = lax.all_to_all(back, ENT, split_axis=0, concat_axis=0, tiled=True)
    ys = [ys[0]] + [over("basis", r, ys[r]) for r in range(1, groups)]

    *scores, w_out = call(
        functools.partial(score_body, cap, nblk, own, halves),
        (*[jax.ShapeDtypeStruct((own, slots), F32) for _ in range(groups)], bf(nblk * nbase, slots)),
        [VM] * 10 + [HB],
        [
            pltpu.VMEM((peers * (per + 8), LANES), F32),
            rows_scratch(nbase * rows, width),
            pltpu.VMEM((nbase, slots), F32),
            tables,
            pltpu.VMEM((groups, own, slots), F32),
            dma((groups,)),
        ],
        limit=18,
        cost=COST,
    )(pg, dst, cnt, incoming, rel_out, src, *coefs, far(table))
    scores = [scores[0]] + [over("basis", r, scores[r]) for r in range(1, groups)]
    lot = chunks * own
    coef_part = call(coef_body, bf(lot, width), [VM] * 5, limit=4)(rel_in, *scores)

    ys = lax.optimization_barrier((*ys, scores[1], scores[3]))[:groups]
    part = own * width // NC
    keep, send = call(
        functools.partial(basis_body, own, rows, peers),
        (bf(part, width), bf(part, width)),
        [VM] * 4,
        [rows_scratch(width, width), rows_scratch(NC * part, width)],
        limit=8,
    )(*ys)
    got = over("c", 1, send)
    each = part // NX
    outs = call(
        core_body,
        tuple(bf(each + lot, width) for _ in range(NX)),
        [VM] * 4,
        [pltpu.VMEM((part, width), F32)],
        limit=8,
    )(keep, got, coef_part, over("c", 1, coef_part))
    ins = [outs[0]] + [over("x", r, outs[r]) for r in range(1, NX)]

    grads = call(
        functools.partial(bwd_body, cap, own),
        tuple(bf(2, width // groups, rows) for _ in range(groups)),
        [VM] * 4 + [HB] * 2,
        [
            pltpu.VMEM((peers * per, LANES), BF),
            pltpu.VMEM((peers * per, LANES), F32),
            rows_scratch(nbase * rows, width),
            pltpu.VMEM((width, rows), F32),
            tables,
            dma((8,)),
            dma((groups,)),
        ],
        limit=18,
    )(w_out, act, pg, self_weight, far(returned.reshape(peers * per, LANES)), far(table))

    ins = lax.optimization_barrier((*ins, grads[0]))[:NX]
    last = each // nz
    out = call(
        x_body,
        bf(nz, last + lot, width),
        [VM] * NX,
        [pltpu.VMEM((NX, lot, width), F32)],
        limit=4,
    )(*ins)
    out = lax.all_to_all(out, "z", split_axis=0, concat_axis=0, tiled=True)
    basis_grad, coef_grad = call(
        functools.partial(z_body, own),
        (jax.ShapeDtypeStruct((own, width // peers, width), F32), jax.ShapeDtypeStruct((own, relations), F32)),
        [VM],
        limit=4,
    )(out)

    grads = [grads[0]] + [over("basis", r, grads[r]) for r in range(1, groups)]
    cols = width // groups
    entity_grad, activation = call(
        functools.partial(join_body, nblk),
        (bf(cols, ent_dev), bf(cols, ent_dev)),
        [VM] * groups,
        [pltpu.VMEM((groups, 2, cols, rows), F32)],
        limit=4,
    )(*grads)
    return (activation.T, basis_grad, coef_grad.T, entity_grad.T)


def solution(mesh):
    nz = mesh.devices.shape[0] // (NX * NC)
    fine = Mesh(mesh.devices.reshape(nz, NX, NC, mesh.devices.shape[1]), (*ENT, "basis"))
    placed = (
        P(ENT, None),
        P(),
        P("basis", None, None),
        P(None, "basis"),
        P(ENT, None, None),
        P(ENT, None, None),
        P(None, ENT, None),
        P(None, ENT, None),
        P(ENT, None),
    )
    return jax.shard_map(
        local,
        mesh=fine,
        in_specs=placed,
        out_specs=(P(ENT, "basis"), P("basis", ENT, None), P(None, "basis"), P(ENT, "basis")),
        check_vma=False,
    )
```

```python
import functools

import jax
import jax.numpy as jnp
from jax import lax
from jax.experimental import pallas as pl
from jax.experimental.pallas import tpu as pltpu
from jax.sharding import Mesh
from jax.sharding import PartitionSpec as P

BLK = 128
LANES = 128
GAP = 8
NX = 4
NC = 2
ENT = ("z", "x", "c")
BF = jnp.bfloat16
F32 = jnp.float32
NT = (((1,), (1,)), ((), ()))
TN = (((0,), (0,)), ((), ()))
MIB = 1024 * 1024
VM = pl.BlockSpec(memory_space=pltpu.VMEM)
SM = pl.BlockSpec(memory_space=pltpu.SMEM)
COST = pl.CostEstimate(flops=8 * 10**9, transcendentals=0, bytes_accessed=20 * 10**6)
HB = pl.BlockSpec(memory_space=pltpu.HBM)


def call(body, outs, ins, scratch=(), limit=16, outs_in=None, cost=None):
    return pl.pallas_call(
        body,
        out_shape=outs,
        in_specs=ins,
        out_specs=outs_in or jax.tree.map(lambda _: VM, outs),
        scratch_shapes=list(scratch),
        cost_estimate=cost,
        compiler_params=pltpu.CompilerParams(vmem_limit_bytes=limit * MIB),
    )


def bf(*shape):
    return jax.ShapeDtypeStruct(shape, BF)


def hbm(*shape):
    return pltpu.HBM(shape, BF)


def far(value):
    return pltpu.with_memory_space_constraint(value, pltpu.HBM)


def get(ref, at):
    return jnp.concatenate([ref[h, at, :] for h in range(ref.shape[0])], axis=1)


def put(ref, at, value):
    for h in range(ref.shape[0]):
        ref[h, at, :] = value[:, h * LANES : (h + 1) * LANES]


def rows_scratch(rows, width):
    return pltpu.VMEM((width // LANES, rows, LANES), F32)


def turn(i, r, n):
    return lax.rem(i + r + n, n)


def spaced(i, size):
    return pl.ds(pl.multiple_of(i * (size + GAP), 8), size)


def aligned(i, size):
    return pl.ds(pl.multiple_of(i * size, size), size)


def digits(value):
    high = value.astype(BF)
    return high, (value - high.astype(F32)).astype(BF)


def start_all(copies):
    for copy in copies:
        copy.start()
    return copies


def wait_all(copies):
    for copy in copies:
        copy.wait()


def own_row_copies(ref, scr, sem, share):
    first = lax.axis_index("basis") * share
    return [
        pltpu.make_async_copy(
            ref.at[pl.ds(pl.multiple_of(n * BLK + first, share), share), :],
            scr.at[pl.ds(n * share, share), :],
            sem.at[n],
        )
        for n in range(scr.shape[0] // share)
    ]


def line(ref):
    return jnp.concatenate([ref[c : c + 1, :] for c in range(ref.shape[0])], axis=1)


def take_body(share, src_ref, edge_ref, ent_ref, out_ref, idx_ref, rel_ref, own, outs, isem, sem, osem):
    copies = own_row_copies(ent_ref, own, sem, share)
    copies += [pltpu.make_async_copy(src_ref, idx_ref, isem.at[0]), pltpu.make_async_copy(edge_ref, rel_ref, isem.at[1])]
    wait_all(start_all(copies))
    cap, peers = idx_ref.shape
    halves = own.shape[1] // LANES
    lane = lax.broadcasted_iota(jnp.int32, (8, LANES), 1)
    lots = osem.shape[0]
    lot = peers // lots
    copies = []
    for q in range(peers):
        note = jnp.zeros((8, LANES), jnp.int32)
        for c in range(cap):
            block = own[aligned(idx_ref[c, q], share), :]
            for h in range(halves):
                outs[q, pl.ds((c * halves + h) * share, share), :] = block[:, h * LANES : (h + 1) * LANES]
            rel = rel_ref[c, q]
            note = jnp.where(lane == 2 * c, rel >> 8, note)
            note = jnp.where(lane == 2 * c + 1, rel & 255, note)
        outs[q, pl.ds(cap * halves * share, 8), :] = note.astype(F32).astype(BF)
        if (q + 1) % lot == 0:
            i = q // lot
            at = pl.ds(i * lot, lot)
            copies += start_all([pltpu.make_async_copy(outs.at[at], out_ref.at[at], osem.at[i])])
    wait_all(copies)


def slot_weights(own, coef_refs, rel, blk, nblk, cs):
    groups = len(coef_refs)
    rows, width = coef_refs[0].shape
    chunks = rows // 16
    slots = rel.shape[1]
    parts = [jnp.zeros((16, slots), F32) for _ in coef_refs]
    for j in range(chunks):
        ids = lax.broadcasted_iota(jnp.int32, (width, slots), 0) + j * width
        hot = jnp.where(ids == rel, 1.0, 0.0).astype(BF)
        for r, ref in enumerate(coef_refs):
            parts[r] += jnp.dot(ref[pl.ds(j * 16, 16), :], hot, preferred_element_type=F32)
    for r in range(groups):
        cs[turn(lax.axis_index("basis"), -r, groups)] = parts[r][:own]
    coef = cs[...].reshape(groups * own, slots)
    return jnp.concatenate([jnp.where(blk == n, coef, 0.0) for n in range(nblk)], axis=0)


def widen(x_ref, xf, peers):
    per = x_ref.shape[0] // peers
    space = xf.shape[0] // peers

    def some(p, c):
        xf[pl.ds(pl.multiple_of(p * space, 8), per), :] = x_ref[aligned(p, per), :].astype(F32)
        return c

    def straight(i, c):
        at = aligned(i, 4 * LANES)
        xf[at, :] = x_ref[at, :].astype(F32)
        return c

    if space == per:
        lax.fori_loop(0, x_ref.shape[0] // (4 * LANES), straight, 0)
    else:
        lax.fori_loop(0, peers, some, 0, unroll=4)


def slot_rows(xf, peers, cap, halves, share, k):
    per = xf.shape[0] // peers
    return jnp.concatenate(
        [
            jnp.concatenate(
                [xf[pl.ds((c * halves + h) * share + k, peers, stride=per), :] for h in range(halves)], axis=1
            )
            for c in range(cap)
        ],
        axis=0,
    )


def rows_of(mf, base, nbase, nblk, share):
    return jnp.concatenate([get(mf, spaced(n * nbase + base, share)) for n in range(nblk)], axis=0)


def table_copies(table_ref, tab, sem):
    return [pltpu.make_async_copy(table_ref.at[g], tab.at[g], sem.at[g]) for g in range(tab.shape[0])]


def fwd_body(
    cap, nblk, own, dst_ref, count_ref, x_ref, dstv_ref, cnt_ref, c0, c1, c2, c3, sw_ref, table_ref, ent_ref,
    cot_ref, y0, y1, y2, y3, back_ref, pg_ref, rel_ref, act_ref,
    xf, mf, cs, at_ref, tab, ent, cot, ysc, back, tsem, esem, csem, ysem, psem, bsem,
):
    groups = tab.shape[0]
    nbase = groups * own
    width = tab.shape[2]
    halves = width // LANES
    share = BLK // groups
    peers = back.shape[0]
    per = xf.shape[0] // peers
    group0 = lax.axis_index("basis")
    first = group0 * share
    ecopies = start_all(own_row_copies(ent_ref, ent, esem, share))
    tcopies = start_all(table_copies(table_ref, tab, tsem))
    ccopies = start_all(own_row_copies(cot_ref, cot, csem, share))
    widen(x_ref, xf, peers)
    notes = xf[pl.ds(cap * halves * share, peers, stride=per), :].astype(BF)
    lane = lax.broadcasted_iota(jnp.int32, (8, LANES), 1)
    row = lax.broadcasted_iota(jnp.int32, (8, LANES), 0)
    pick = jnp.where(lane == 2 * row, 256.0, jnp.where(lane == 2 * row + 1, 1.0, 0.0)).astype(BF)
    rels = lax.dot_general(pick, notes, NT, preferred_element_type=F32).astype(jnp.int32)
    rel = jnp.concatenate([rels[c : c + 1] for c in range(cap)], axis=1)
    rel_ref[...] = rel
    w = slot_weights(own, (c0, c1, c2, c3), rel, line(dstv_ref), nblk, cs)
    cnt = line(cnt_ref)

    def one(k, c):
        xk = slot_rows(xf, peers, cap, halves, share, k).astype(BF)
        wk = jnp.where(cnt > first + k, w, 0.0).astype(BF)
        put(mf, pl.ds(k, w.shape[0], stride=share + GAP), jnp.dot(wk, xk, preferred_element_type=F32))
        return c

    lax.fori_loop(0, share, one, 0, unroll=8)
    copies = []
    wait_all(ecopies)
    acc = jnp.dot(ent[...], sw_ref[...], preferred_element_type=F32)
    rows = nblk * share
    ys = (y0, y1, y2, y3)
    wait_all(tcopies)
    for r in range(groups):
        group = turn(group0, r, groups)
        for b in range(own):
            mb = rows_of(mf, group * own + b, nbase, nblk, share).astype(BF)
            ysc[r, pl.ds(b * rows, rows), :] = mb
            acc += jnp.dot(mb, tab[group, pl.ds(b * width, width), :], preferred_element_type=F32)
        if r:
            at = pl.ds(0, own * rows)
            copies += start_all([pltpu.make_async_copy(ysc.at[r, at], ys[r].at[at], ysem.at[r])])
    s = jax.nn.sigmoid(acc)
    at_ref[...] = (acc * s).T
    wait_all(ccopies)
    pg = (cot[...].astype(F32) * (s * (1.0 + acc * (1.0 - s)))).astype(BF)
    pg_ref[...] = pg
    k_of = lax.broadcasted_iota(jnp.int32, (share, width), 0) + first
    lots = bsem.shape[0]
    lot = peers // lots
    for q in range(peers):
        for c in range(cap):
            block = pg_ref[aligned(dst_ref[c, q], share), :]
            block = jnp.where(k_of < count_ref[c, q], block.astype(F32), 0.0).astype(BF)
            for h in range(halves):
                back[q, pl.ds((c * halves + h) * share, share), :] = block[:, h * LANES : (h + 1) * LANES]
        if (q + 1) % lot == 0:
            i = q // lot
            at = pl.ds(i * lot, lot)
            copies += start_all([pltpu.make_async_copy(back.at[at], back_ref.at[at], bsem.at[i])])
    cols = width // groups
    at = pl.ds(own * rows, rows)
    for r in range(groups):
        ysc[r, at, :] = pg
        copies += start_all([pltpu.make_async_copy(ysc.at[r, at] if r else ysc.at[r], ys[r].at[at] if r else ys[r], psem.at[r])])
        act_ref[r] = at_ref[aligned(turn(group0, r, groups), cols), :].astype(BF)
    wait_all(copies)


def score_body(
    cap, nblk, own, halves, pg_ref, dstv_ref, cnt_ref, x_ref, rel_ref, src_ref, c0, c1, c2, c3, table_ref,
    s0, s1, s2, s3, w_ref, xf, pf, ts, tab, cs, tsem,
):
    groups = tab.shape[0]
    nbase = groups * own
    width = tab.shape[2]
    peers = cnt_ref.shape[1]
    slots = cap * peers
    share = BLK // groups
    group0 = lax.axis_index("basis")
    first = group0 * share
    tcopies = start_all(table_copies(table_ref, tab, tsem))
    w_ref[...] = slot_weights(own, (c0, c1, c2, c3), line(rel_ref), line(src_ref), nblk, cs).astype(BF)
    widen(x_ref, xf, peers)
    pg = pg_ref[...]
    for b in range(nbase):
        if b % own == 0:
            tcopies[b // own].wait()
        base = tab[b // own, pl.ds((b % own) * width, width), :]
        p = lax.dot_general(pg, base, NT, preferred_element_type=F32)
        for n in range(nblk):
            put(pf, spaced(n * nbase + b, share), p[n * share : (n + 1) * share])
    cnt = line(cnt_ref)

    def one(k, acc):
        pk = get(pf, pl.ds(k, nblk * nbase, stride=share + GAP)).astype(BF)
        xk = slot_rows(xf, peers, cap, halves, share, k).astype(BF)
        t = lax.dot_general(pk, xk, NT, preferred_element_type=F32)
        return acc + jnp.where(cnt > first + k, t, 0.0)

    acc = lax.fori_loop(0, share, one, jnp.zeros((nblk * nbase, slots), F32), unroll=4)
    blk = line(dstv_ref)
    total = jnp.zeros((nbase, slots), F32)
    for n in range(nblk):
        total += jnp.where(blk == n, acc[n * nbase : (n + 1) * nbase], 0.0)
    ts[...] = total
    for r, out in enumerate((s0, s1, s2, s3)):
        out[...] = ts[aligned(turn(group0, r, groups), own), :]


def coef_body(rel_ref, s0, s1, s2, s3, out_ref):
    own, slots = s0.shape
    width = out_ref.shape[1]
    chunks = out_ref.shape[0] // own
    high, low = digits((s0[...] + s1[...]) + (s2[...] + s3[...]))
    both = jnp.concatenate([high.astype(F32), low.astype(F32)], axis=0).astype(BF)
    rel = rel_ref[...]
    parts = []
    for j in range(chunks):
        ids = lax.broadcasted_iota(jnp.int32, (width, slots), 0) + j * width
        hot = jnp.where(ids == rel, 1.0, 0.0).astype(BF)
        t = lax.dot_general(both, hot, NT, preferred_element_type=F32)
        parts.append(t[:own] + t[own:])
    out_ref[...] = jnp.concatenate(parts, axis=0).astype(BF)


def basis_body(own, rows, peers, y0, y1, y2, y3, keep_ref, send_ref, tmp, outf):
    ys = (y0, y1, y2, y3)
    width = y0.shape[1]
    part = keep_ref.shape[0]
    each = part // NX
    deep = part * NC // (own * peers)
    lines = own * deep
    nz = each // lines
    plane = NX * NC * deep
    pg = jnp.concatenate([y[pl.ds(own * rows, rows), :] for y in ys], axis=0)
    for b in range(own):
        m = jnp.concatenate([y[pl.ds(b * rows, rows), :] for y in ys], axis=0)
        t = lax.dot_general(m, pg, TN, preferred_element_type=F32)
        for z in range(nz):
            put(tmp, spaced(z, plane), t[z * plane : (z + 1) * plane])
        for c in range(NC):
            for x in range(NX):
                for d in range(deep):
                    put(
                        outf,
                        pl.ds((c * NX + x) * nz * (lines + GAP) + b * deep + d, nz, stride=lines + GAP),
                        get(tmp, pl.ds((x * NC + c) * deep + d, nz, stride=plane + GAP)),
                    )
    core = lax.axis_index("c")
    for i in range(NX * nz):
        keep_ref[pl.ds(i * lines, lines), :] = get(outf, spaced(core * (NX * nz) + i, lines)).astype(BF)
        send_ref[pl.ds(i * lines, lines), :] = get(outf, spaced((1 - core) * (NX * nz) + i, lines)).astype(BF)


def core_body(keep_ref, got_ref, coef_ref, other_ref, o0, o1, o2, o3, sums):
    part = keep_ref.shape[0]
    each = part // NX
    sums[...] = keep_ref[...].astype(F32) + got_ref[...].astype(F32)
    coef = (coef_ref[...].astype(F32) + other_ref[...].astype(F32)).astype(BF)
    for r, out in enumerate((o0, o1, o2, o3)):
        out[pl.ds(0, each), :] = sums[aligned(turn(lax.axis_index("x"), r, NX), each), :].astype(BF)
        out[pl.ds(each, coef.shape[0]), :] = coef


def x_body(i0, i1, i2, i3, out_ref, order):
    n = order.shape[1]
    each = i0.shape[0] - n
    nz = out_ref.shape[0]
    last = each // nz
    sums = sum(i[pl.ds(0, each), :].astype(F32) for i in (i0, i1, i2, i3))
    for r, i in enumerate((i0, i1, i2, i3)):
        order[turn(lax.axis_index("x"), -r, NX)] = i[pl.ds(each, n), :].astype(F32)
    coef = ((order[0] + order[1]) + (order[2] + order[3])).astype(BF)
    for z in range(nz):
        out_ref[z, pl.ds(0, last), :] = sums[z * last : (z + 1) * last].astype(BF)
        out_ref[z, pl.ds(last, n), :] = coef


def z_body(own, in_ref, basis_ref, coef_ref):
    nz, rows, width = in_ref.shape
    deep = basis_ref.shape[1]
    last = own * deep
    n = rows - last
    basis = jnp.zeros((last, width), F32)
    coef = jnp.zeros((n, width), F32)
    for z in range(nz):
        basis += in_ref[z, pl.ds(0, last), :].astype(F32)
        coef += in_ref[z, pl.ds(last, n), :].astype(F32)
    for b in range(own):
        basis_ref[b] = basis[b * deep : (b + 1) * deep]
    relations = coef_ref.shape[1]
    for j in range(n // own):
        size = min(width, relations - j * width)
        coef_ref[:, pl.ds(j * width, size)] = coef[j * own : (j + 1) * own, :size]


def bwd_body(
    cap, own, x_ref, w_ref, act_ref, pg_ref, sw_ref, table_ref, o0, o1, o2, o3, xf, mf, at_ref, tab, tsem
):
    groups = tab.shape[0]
    nbase = groups * own
    width = tab.shape[2]
    halves = width // LANES
    share = BLK // groups
    slots = w_ref.shape[1]
    peers = slots // cap
    nblk = w_ref.shape[0] // nbase
    tcopies = start_all(table_copies(table_ref, tab, tsem))
    widen(x_ref, xf, peers)
    w = w_ref[...]

    def one(k, c):
        xk = slot_rows(xf, peers, cap, halves, share, k).astype(BF)
        put(mf, pl.ds(k, w.shape[0], stride=share + GAP), jnp.dot(w, xk, preferred_element_type=F32))
        return c

    lax.fori_loop(0, share, one, 0, unroll=8)
    acc = lax.dot_general(sw_ref[...], pg_ref[...], NT, preferred_element_type=F32)
    wait_all(tcopies)
    for b in range(nbase):
        mb = rows_of(mf, b, nbase, nblk, share).astype(BF)
        base = tab[b // own, pl.ds((b % own) * width, width), :]
        acc += lax.dot_general(base, mb, NT, preferred_element_type=F32)
    at_ref[...] = acc
    cols = width // groups
    for r, out in enumerate((o0, o1, o2, o3)):
        out[0] = at_ref[aligned(turn(lax.axis_index("basis"), r, groups), cols), :].astype(BF)
        out[1] = act_ref[r]


def join_body(nblk, i0, i1, i2, i3, grad_ref, act_ref, order):
    groups = order.shape[0]
    share = BLK // groups
    for r, i in enumerate((i0, i1, i2, i3)):
        order[turn(lax.axis_index("basis"), -r, groups)] = i[...].astype(F32)
    for j, out in enumerate((grad_ref, act_ref)):
        for n in range(nblk):
            whole = jnp.concatenate([order[g, j, :, n * share : (n + 1) * share] for g in range(groups)], axis=1)
            out[:, n * BLK : (n + 1) * BLK] = whole.astype(BF)


def local(
    entity_rows,
    self_weight,
    bases,
    coefficients,
    send_block,
    edge_rel,
    edge_dst,
    edge_count,
    cotangent,
):
    peers = lax.axis_size(ENT)
    groups = lax.axis_size("basis")
    ent_dev, width = entity_rows.shape
    nblk = ent_dev // BLK
    own = bases.shape[0]
    nbase = own * groups
    relations = coefficients.shape[0]
    cap = send_block.shape[2]
    slots = peers * cap
    share = BLK // groups
    halves = width // LANES
    nz = lax.axis_size("z")
    rows = nblk * share
    dma = pltpu.SemaphoreType.DMA

    def over(axis, r, value):
        n = lax.axis_size(axis)
        return lax.ppermute(value, axis, [(i, (i + r) % n) for i in range(n)])

    src, rel_out = send_block[0].T, edge_rel[0].T
    dst, cnt = edge_dst[:, 0, :].T, edge_count[:, 0, :].T

    per = cap * halves * share
    outgoing = call(
        functools.partial(take_body, share),
        hbm(peers, per + 8, LANES),
        [HB] * 3,
        [
            pltpu.SMEM((cap, peers), jnp.int32),
            pltpu.SMEM((cap, peers), jnp.int32),
            pltpu.VMEM((rows, width), BF),
            pltpu.VMEM((peers, per + 8, LANES), BF),
            dma((2,)),
            dma((nblk,)),
            dma((4,)),
        ],
        outs_in=HB,
    )(far(src), far(rel_out), far(entity_rows))
    incoming = lax.all_to_all(outgoing, ENT, split_axis=0, concat_axis=0, tiled=True)

    bases, _ = lax.optimization_barrier((bases, outgoing))
    table = lax.all_gather(bases.reshape(own * width, width), "basis")
    chunks = -(-relations // width)
    coef = jnp.pad(coefficients.astype(BF).T, ((0, 16 - own), (0, chunks * width - relations)))
    coef = coef.reshape(16, chunks, width).transpose(1, 0, 2).reshape(chunks * 16, width)
    coefs = [coef] + [over("basis", r, coef) for r in range(1, groups)]
    tables = pltpu.VMEM((groups, own * width, width), BF)
    incoming = incoming.reshape(peers * (per + 8), LANES)
    *ys, back, pg, rel_in, act = call(
        functools.partial(fwd_body, cap, nblk, own),
        (
            *[hbm((own + 1) * rows, width) for _ in range(groups)],
            hbm(peers, per, LANES),
            bf(rows, width),
            jax.ShapeDtypeStruct((1, slots), jnp.int32),
            bf(groups, width // groups, rows),
        ),
        [SM] * 2 + [VM] * 8 + [HB] * 3,
        [
            pltpu.VMEM((peers * (per + 8), LANES), F32),
            rows_scratch(nbase * nblk * (share + GAP), width),
            pltpu.VMEM((groups, own, slots), F32),
            pltpu.VMEM((width, rows), F32),
            tables,
            pltpu.VMEM((rows, width), BF),
            pltpu.VMEM((rows, width), BF),
            pltpu.VMEM((groups, (own + 1) * rows, width), BF),
            pltpu.VMEM((peers, per, LANES), BF),
            dma((groups,)),
            dma((nblk,)),
            dma((nblk,)),
            dma((groups,)),
            dma((groups,)),
            dma((4,)),
        ],
        limit=30,
        outs_in=(HB,) * (groups + 1) + (VM,) * 3,
    )(
        dst, cnt, incoming, dst, cnt, *coefs, self_weight, far(table),
        far(entity_rows), far(cotangent),
    )

    returned = lax.all_to_all(back, ENT, split_axis=0, concat_axis=0, tiled=True)
    ys = [ys[0]] + [over("basis", r, ys[r]) for r in range(1, groups)]

    *scores, w_out = call(
        functools.partial(score_body, cap, nblk, own, halves),
        (*[jax.ShapeDtypeStruct((own, slots), F32) for _ in range(groups)], bf(nblk * nbase, slots)),
        [VM] * 10 + [HB],
        [
            pltpu.VMEM((peers * (per + 8), LANES), F32),
            rows_scratch(nbase * nblk * (share + GAP), width),
            pltpu.VMEM((nbase, slots), F32),
            tables,
            pltpu.VMEM((groups, own, slots), F32),
            dma((groups,)),
        ],
        limit=20,
        cost=COST,
    )(pg, dst, cnt, incoming, rel_out, src, *coefs, far(table))
    scores = [scores[0]] + [over("basis", r, scores[r]) for r in range(1, groups)]
    lot = chunks * own
    coef_part = call(coef_body, bf(lot, width), [VM] * 5, limit=4)(rel_in, *scores)

    ys = lax.optimization_barrier((*ys, scores[1], scores[3]))[:groups]
    part = own * width // NC
    keep, send = call(
        functools.partial(basis_body, own, rows, peers),
        (bf(part, width), bf(part, width)),
        [VM] * 4,
        [rows_scratch(2 * width, width), rows_scratch(2 * NC * part, width)],
        limit=12,
    )(*ys)
    got = over("c", 1, send)
    each = part // NX
    outs = call(
        core_body,
        tuple(bf(each + lot, width) for _ in range(NX)),
        [VM] * 4,
        [pltpu.VMEM((part, width), F32)],
        limit=8,
    )(keep, got, coef_part, over("c", 1, coef_part))
    ins = [outs[0]] + [over("x", r, outs[r]) for r in range(1, NX)]

    grads = call(
        functools.partial(bwd_body, cap, own),
        tuple(bf(2, width // groups, rows) for _ in range(groups)),
        [VM] * 5 + [HB],
        [
            pltpu.VMEM((peers * (per + GAP), LANES), F32),
            rows_scratch(nbase * nblk * (share + GAP), width),
            pltpu.VMEM((width, rows), F32),
            tables,
            dma((groups,)),
        ],
        limit=20,
    )(returned.reshape(peers * per, LANES), w_out, act, pg, self_weight, far(table))

    ins = lax.optimization_barrier((*ins, grads[0]))[:NX]
    last = each // nz
    out = call(
        x_body,
        bf(nz, last + lot, width),
        [VM] * NX,
        [pltpu.VMEM((NX, lot, width), F32)],
        limit=4,
    )(*ins)
    out = lax.all_to_all(out, "z", split_axis=0, concat_axis=0, tiled=True)
    basis_grad, coef_grad = call(
        functools.partial(z_body, own),
        (jax.ShapeDtypeStruct((own, width // peers, width), F32), jax.ShapeDtypeStruct((own, relations), F32)),
        [VM],
        limit=4,
    )(out)

    grads = [grads[0]] + [over("basis", r, grads[r]) for r in range(1, groups)]
    cols = width // groups
    entity_grad, activation = call(
        functools.partial(join_body, nblk),
        (bf(cols, ent_dev), bf(cols, ent_dev)),
        [VM] * groups,
        [pltpu.VMEM((groups, 2, cols, rows), F32)],
        limit=4,
    )(*grads)
    return (activation.T, basis_grad, coef_grad.T, entity_grad.T)


def solution(mesh):
    nz = mesh.devices.shape[0] // (NX * NC)
    fine = Mesh(mesh.devices.reshape(nz, NX, NC, mesh.devices.shape[1]), (*ENT, "basis"))
    placed = (
        P(ENT, None),
        P(),
        P("basis", None, None),
        P(None, "basis"),
        P(ENT, None, None),
        P(ENT, None, None),
        P(None, ENT, None),
        P(None, ENT, None),
        P(ENT, None),
    )
    return jax.shard_map(
        local,
        mesh=fine,
        in_specs=placed,
        out_specs=(P(ENT, "basis"), P("basis", ENT, None), P(None, "basis"), P(ENT, "basis")),
        check_vma=False,
    )
```

```python
import functools

import jax
import jax.numpy as jnp
from jax import lax
from jax.experimental import pallas as pl
from jax.experimental.pallas import tpu as pltpu
from jax.sharding import Mesh
from jax.sharding import PartitionSpec as P

BLK = 128
LANES = 128
GAP = 8
NX = 4
NC = 2
ENT = ("z", "x", "c")
BF = jnp.bfloat16
F32 = jnp.float32
NT = (((1,), (1,)), ((), ()))
TN = (((0,), (0,)), ((), ()))
MIB = 1024 * 1024
VM = pl.BlockSpec(memory_space=pltpu.VMEM)
SM = pl.BlockSpec(memory_space=pltpu.SMEM)
COST = pl.CostEstimate(flops=8 * 10**9, transcendentals=0, bytes_accessed=20 * 10**6)
HB = pl.BlockSpec(memory_space=pltpu.HBM)


def call(body, outs, ins, scratch=(), limit=16, outs_in=None, cost=None):
    return pl.pallas_call(
        body,
        out_shape=outs,
        in_specs=ins,
        out_specs=outs_in or jax.tree.map(lambda _: VM, outs),
        scratch_shapes=list(scratch),
        cost_estimate=cost,
        compiler_params=pltpu.CompilerParams(vmem_limit_bytes=limit * MIB),
    )


def bf(*shape):
    return jax.ShapeDtypeStruct(shape, BF)


def hbm(*shape):
    return pltpu.HBM(shape, BF)


def far(value):
    return pltpu.with_memory_space_constraint(value, pltpu.HBM)


def get(ref, at):
    return jnp.concatenate([ref[h, at, :] for h in range(ref.shape[0])], axis=1)


def put(ref, at, value):
    for h in range(ref.shape[0]):
        ref[h, at, :] = value[:, h * LANES : (h + 1) * LANES]


def rows_scratch(rows, width):
    return pltpu.VMEM((width // LANES, rows, LANES), F32)


def turn(i, r, n):
    return lax.rem(i + r + n, n)


def spaced(i, size):
    return pl.ds(pl.multiple_of(i * (size + GAP), 8), size)


def aligned(i, size):
    return pl.ds(pl.multiple_of(i * size, size), size)


def digits(value):
    high = value.astype(BF)
    return high, (value - high.astype(F32)).astype(BF)


def start_all(copies):
    for copy in copies:
        copy.start()
    return copies


def wait_all(copies):
    for copy in copies:
        copy.wait()


def own_row_copies(ref, scr, sem, share):
    first = lax.axis_index("basis") * share
    return [
        pltpu.make_async_copy(
            ref.at[pl.ds(pl.multiple_of(n * BLK + first, share), share), :],
            scr.at[pl.ds(n * share, share), :],
            sem.at[n],
        )
        for n in range(scr.shape[0] // share)
    ]


def line(ref):
    return jnp.concatenate([ref[c : c + 1, :] for c in range(ref.shape[0])], axis=1)


def take_body(share, src_ref, edge_ref, ent_ref, out_ref, idx_ref, rel_ref, own, outs, isem, sem, osem):
    copies = own_row_copies(ent_ref, own, sem, share)
    copies += [pltpu.make_async_copy(src_ref, idx_ref, isem.at[0]), pltpu.make_async_copy(edge_ref, rel_ref, isem.at[1])]
    wait_all(start_all(copies))
    cap, peers = idx_ref.shape
    halves = own.shape[1] // LANES
    lane = lax.broadcasted_iota(jnp.int32, (8, LANES), 1)
    lots = osem.shape[0]
    lot = peers // lots
    copies = []
    for q in range(peers):
        note = jnp.zeros((8, LANES), jnp.int32)
        for c in range(cap):
            block = own[aligned(idx_ref[c, q], share), :]
            for h in range(halves):
                outs[q, pl.ds((c * halves + h) * share, share), :] = block[:, h * LANES : (h + 1) * LANES]
            rel = rel_ref[c, q]
            note = jnp.where(lane == 2 * c, rel >> 8, note)
            note = jnp.where(lane == 2 * c + 1, rel & 255, note)
        outs[q, pl.ds(cap * halves * share, 8), :] = note.astype(F32).astype(BF)
        if (q + 1) % lot == 0:
            i = q // lot
            at = pl.ds(i * lot, lot)
            copies += start_all([pltpu.make_async_copy(outs.at[at], out_ref.at[at], osem.at[i])])
    wait_all(copies)


def slot_weights(own, coef_refs, rel, blk, nblk, cs):
    groups = len(coef_refs)
    rows, width = coef_refs[0].shape
    chunks = rows // 16
    slots = rel.shape[1]
    parts = [jnp.zeros((16, slots), F32) for _ in coef_refs]
    for j in range(chunks):
        ids = lax.broadcasted_iota(jnp.int32, (width, slots), 0) + j * width
        hot = jnp.where(ids == rel, 1.0, 0.0).astype(BF)
        for r, ref in enumerate(coef_refs):
            parts[r] += jnp.dot(ref[pl.ds(j * 16, 16), :], hot, preferred_element_type=F32)
    for r in range(groups):
        cs[turn(lax.axis_index("basis"), -r, groups)] = parts[r][:own]
    coef = cs[...].reshape(groups * own, slots)
    return jnp.concatenate([jnp.where(blk == n, coef, 0.0) for n in range(nblk)], axis=0)


def widen(x_ref, xf, peers):
    per = x_ref.shape[0] // peers
    space = xf.shape[0] // peers

    def some(p, c):
        xf[pl.ds(pl.multiple_of(p * space, 8), per), :] = x_ref[aligned(p, per), :].astype(F32)
        return c

    def straight(i, c):
        at = aligned(i, 4 * LANES)
        xf[at, :] = x_ref[at, :].astype(F32)
        return c

    if space == per:
        lax.fori_loop(0, x_ref.shape[0] // (4 * LANES), straight, 0)
    else:
        lax.fori_loop(0, peers, some, 0, unroll=4)


def slot_rows(xf, peers, cap, halves, share, k):
    per = xf.shape[0] // peers
    return jnp.concatenate(
        [
            jnp.concatenate(
                [xf[pl.ds((c * halves + h) * share + k, peers, stride=per), :] for h in range(halves)], axis=1
            )
            for c in range(cap)
        ],
        axis=0,
    )


def rows_of(mf, base, nbase, nblk, share):
    return jnp.concatenate([get(mf, spaced(n * nbase + base, share)) for n in range(nblk)], axis=0)


def table_copies(table_ref, tab, sem):
    return [pltpu.make_async_copy(table_ref.at[g], tab.at[g], sem.at[g]) for g in range(tab.shape[0])]


def fwd_body(
    cap, nblk, own, dst_ref, count_ref, x_ref, dstv_ref, cnt_ref, c0, c1, c2, c3, sw_ref, table_ref, ent_ref,
    cot_ref, y0, y1, y2, y3, back_ref, pg_ref, rel_ref, act_ref,
    xf, mf, cs, at_ref, tab, ent, cot, ysc, back, tsem, esem, csem, ysem, psem, bsem,
):
    groups = tab.shape[0]
    nbase = groups * own
    width = tab.shape[2]
    halves = width // LANES
    share = BLK // groups
    peers = back.shape[0]
    per = xf.shape[0] // peers
    group0 = lax.axis_index("basis")
    first = group0 * share
    ecopies = start_all(own_row_copies(ent_ref, ent, esem, share))
    tcopies = start_all(table_copies(table_ref, tab, tsem))
    ccopies = start_all(own_row_copies(cot_ref, cot, csem, share))
    widen(x_ref, xf, peers)
    notes = xf[pl.ds(cap * halves * share, peers, stride=per), :].astype(BF)
    lane = lax.broadcasted_iota(jnp.int32, (8, LANES), 1)
    row = lax.broadcasted_iota(jnp.int32, (8, LANES), 0)
    pick = jnp.where(lane == 2 * row, 256.0, jnp.where(lane == 2 * row + 1, 1.0, 0.0)).astype(BF)
    rels = lax.dot_general(pick, notes, NT, preferred_element_type=F32).astype(jnp.int32)
    rel = jnp.concatenate([rels[c : c + 1] for c in range(cap)], axis=1)
    rel_ref[...] = rel
    w = slot_weights(own, (c0, c1, c2, c3), rel, line(dstv_ref), nblk, cs)
    cnt = line(cnt_ref)

    def one(k, c):
        xk = slot_rows(xf, peers, cap, halves, share, k).astype(BF)
        wk = jnp.where(cnt > first + k, w, 0.0).astype(BF)
        put(mf, pl.ds(k, w.shape[0], stride=share + GAP), jnp.dot(wk, xk, preferred_element_type=F32))
        return c

    lax.fori_loop(0, share, one, 0, unroll=8)
    copies = []
    wait_all(ecopies)
    acc = jnp.dot(ent[...], sw_ref[...], preferred_element_type=F32)
    rows = nblk * share
    ys = (y0, y1, y2, y3)
    wait_all(tcopies)
    for r in range(groups):
        group = turn(group0, r, groups)
        for b in range(own):
            mb = rows_of(mf, group * own + b, nbase, nblk, share).astype(BF)
            ysc[r, pl.ds(b * rows, rows), :] = mb
            acc += jnp.dot(mb, tab[group, pl.ds(b * width, width), :], preferred_element_type=F32)
        if r:
            at = pl.ds(0, own * rows)
            copies += start_all([pltpu.make_async_copy(ysc.at[r, at], ys[r].at[at], ysem.at[r])])
    s = jax.nn.sigmoid(acc)
    at_ref[...] = (acc * s).T
    wait_all(ccopies)
    pg = (cot[...].astype(F32) * (s * (1.0 + acc * (1.0 - s)))).astype(BF)
    pg_ref[...] = pg
    k_of = lax.broadcasted_iota(jnp.int32, (share, width), 0) + first
    lots = bsem.shape[0]
    lot = peers // lots
    for q in range(peers):
        for c in range(cap):
            block = pg_ref[aligned(dst_ref[c, q], share), :]
            block = jnp.where(k_of < count_ref[c, q], block.astype(F32), 0.0).astype(BF)
            for h in range(halves):
                back[q, pl.ds((c * halves + h) * share, share), :] = block[:, h * LANES : (h + 1) * LANES]
        if (q + 1) % lot == 0:
            i = q // lot
            at = pl.ds(i * lot, lot)
            copies += start_all([pltpu.make_async_copy(back.at[at], back_ref.at[at], bsem.at[i])])
    cols = width // groups
    at = pl.ds(own * rows, rows)
    for r in range(groups):
        ysc[r, at, :] = pg
        copies += start_all([pltpu.make_async_copy(ysc.at[r, at] if r else ysc.at[r], ys[r].at[at] if r else ys[r], psem.at[r])])
        act_ref[r] = at_ref[aligned(turn(group0, r, groups), cols), :].astype(BF)
    wait_all(copies)


def score_body(
    cap, nblk, own, halves, pg_ref, dstv_ref, cnt_ref, x_ref, rel_ref, src_ref, c0, c1, c2, c3, table_ref,
    s0, s1, s2, s3, w_ref, xf, pf, ts, tab, cs, tsem,
):
    groups = tab.shape[0]
    nbase = groups * own
    width = tab.shape[2]
    peers = cnt_ref.shape[1]
    slots = cap * peers
    share = BLK // groups
    group0 = lax.axis_index("basis")
    first = group0 * share
    tcopies = start_all(table_copies(table_ref, tab, tsem))
    w_ref[...] = slot_weights(own, (c0, c1, c2, c3), line(rel_ref), line(src_ref), nblk, cs).astype(BF)
    widen(x_ref, xf, peers)
    pg = pg_ref[...]
    for b in range(nbase):
        if b % own == 0:
            tcopies[b // own].wait()
        base = tab[b // own, pl.ds((b % own) * width, width), :]
        p = lax.dot_general(pg, base, NT, preferred_element_type=F32)
        for n in range(nblk):
            put(pf, spaced(n * nbase + b, share), p[n * share : (n + 1) * share])
    cnt = line(cnt_ref)

    def one(k, acc):
        pk = get(pf, pl.ds(k, nblk * nbase, stride=share + GAP)).astype(BF)
        xk = slot_rows(xf, peers, cap, halves, share, k).astype(BF)
        t = lax.dot_general(pk, xk, NT, preferred_element_type=F32)
        return acc + jnp.where(cnt > first + k, t, 0.0)

    acc = lax.fori_loop(0, share, one, jnp.zeros((nblk * nbase, slots), F32), unroll=4)
    blk = line(dstv_ref)
    total = jnp.zeros((nbase, slots), F32)
    for n in range(nblk):
        total += jnp.where(blk == n, acc[n * nbase : (n + 1) * nbase], 0.0)
    ts[...] = total
    for r, out in enumerate((s0, s1, s2, s3)):
        out[...] = ts[aligned(turn(group0, r, groups), own), :]


def coef_body(rel_ref, s0, s1, s2, s3, out_ref):
    own, slots = s0.shape
    width = out_ref.shape[1]
    chunks = out_ref.shape[0] // own
    high, low = digits((s0[...] + s1[...]) + (s2[...] + s3[...]))
    both = jnp.concatenate([high.astype(F32), low.astype(F32)], axis=0).astype(BF)
    rel = rel_ref[...]
    parts = []
    for j in range(chunks):
        ids = lax.broadcasted_iota(jnp.int32, (width, slots), 0) + j * width
        hot = jnp.where(ids == rel, 1.0, 0.0).astype(BF)
        t = lax.dot_general(both, hot, NT, preferred_element_type=F32)
        parts.append(t[:own] + t[own:])
    out_ref[...] = jnp.concatenate(parts, axis=0).astype(BF)


def basis_body(own, rows, peers, y0, y1, y2, y3, keep_ref, send_ref, tmp, outf):
    ys = (y0, y1, y2, y3)
    width = y0.shape[1]
    part = keep_ref.shape[0]
    each = part // NX
    deep = part * NC // (own * peers)
    lines = own * deep
    nz = each // lines
    plane = NX * NC * deep
    pg = jnp.concatenate([y[pl.ds(own * rows, rows), :] for y in ys], axis=0)
    for b in range(own):
        m = jnp.concatenate([y[pl.ds(b * rows, rows), :] for y in ys], axis=0)
        t = lax.dot_general(m, pg, TN, preferred_element_type=F32)
        for z in range(nz):
            put(tmp, spaced(z, plane), t[z * plane : (z + 1) * plane])
        for c in range(NC):
            for x in range(NX):
                for d in range(deep):
                    put(
                        outf,
                        pl.ds((c * NX + x) * nz * (lines + GAP) + b * deep + d, nz, stride=lines + GAP),
                        get(tmp, pl.ds((x * NC + c) * deep + d, nz, stride=plane + GAP)),
                    )
    core = lax.axis_index("c")
    for i in range(NX * nz):
        keep_ref[pl.ds(i * lines, lines), :] = get(outf, spaced(core * (NX * nz) + i, lines)).astype(BF)
        send_ref[pl.ds(i * lines, lines), :] = get(outf, spaced((1 - core) * (NX * nz) + i, lines)).astype(BF)


def core_body(keep_ref, got_ref, coef_ref, other_ref, o0, o1, o2, o3, sums):
    part = keep_ref.shape[0]
    each = part // NX
    sums[...] = keep_ref[...].astype(F32) + got_ref[...].astype(F32)
    coef = (coef_ref[...].astype(F32) + other_ref[...].astype(F32)).astype(BF)
    for r, out in enumerate((o0, o1, o2, o3)):
        out[pl.ds(0, each), :] = sums[aligned(turn(lax.axis_index("x"), r, NX), each), :].astype(BF)
        out[pl.ds(each, coef.shape[0]), :] = coef


def x_body(i0, i1, i2, i3, out_ref, order):
    n = order.shape[1]
    each = i0.shape[0] - n
    nz = out_ref.shape[0]
    last = each // nz
    sums = sum(i[pl.ds(0, each), :].astype(F32) for i in (i0, i1, i2, i3))
    for r, i in enumerate((i0, i1, i2, i3)):
        order[turn(lax.axis_index("x"), -r, NX)] = i[pl.ds(each, n), :].astype(F32)
    coef = ((order[0] + order[1]) + (order[2] + order[3])).astype(BF)
    for z in range(nz):
        out_ref[z, pl.ds(0, last), :] = sums[z * last : (z + 1) * last].astype(BF)
        out_ref[z, pl.ds(last, n), :] = coef


def z_body(own, in_ref, basis_ref, coef_ref):
    nz, rows, width = in_ref.shape
    deep = basis_ref.shape[1]
    last = own * deep
    n = rows - last
    basis = jnp.zeros((last, width), F32)
    coef = jnp.zeros((n, width), F32)
    for z in range(nz):
        basis += in_ref[z, pl.ds(0, last), :].astype(F32)
        coef += in_ref[z, pl.ds(last, n), :].astype(F32)
    for b in range(own):
        basis_ref[b] = basis[b * deep : (b + 1) * deep]
    relations = coef_ref.shape[1]
    for j in range(n // own):
        size = min(width, relations - j * width)
        coef_ref[:, pl.ds(j * width, size)] = coef[j * own : (j + 1) * own, :size]


def bwd_body(
    cap, own, x_ref, w_ref, act_ref, pg_ref, sw_ref, table_ref, o0, o1, o2, o3, xf, mf, at_ref, tab, tsem
):
    groups = tab.shape[0]
    nbase = groups * own
    width = tab.shape[2]
    halves = width // LANES
    share = BLK // groups
    slots = w_ref.shape[1]
    peers = slots // cap
    nblk = w_ref.shape[0] // nbase
    tcopies = start_all(table_copies(table_ref, tab, tsem))
    widen(x_ref, xf, peers)
    w = w_ref[...]

    def one(k, c):
        xk = slot_rows(xf, peers, cap, halves, share, k).astype(BF)
        put(mf, pl.ds(k, w.shape[0], stride=share + GAP), jnp.dot(w, xk, preferred_element_type=F32))
        return c

    lax.fori_loop(0, share, one, 0, unroll=8)
    acc = lax.dot_general(sw_ref[...], pg_ref[...], NT, preferred_element_type=F32)
    wait_all(tcopies)
    for b in range(nbase):
        mb = rows_of(mf, b, nbase, nblk, share).astype(BF)
        base = tab[b // own, pl.ds((b % own) * width, width), :]
        acc += lax.dot_general(base, mb, NT, preferred_element_type=F32)
    at_ref[...] = acc
    cols = width // groups
    for r, out in enumerate((o0, o1, o2, o3)):
        out[0] = at_ref[aligned(turn(lax.axis_index("basis"), r, groups), cols), :].astype(BF)
        out[1] = act_ref[r]


def join_body(nblk, i0, i1, i2, i3, grad_ref, act_ref, order):
    groups = order.shape[0]
    share = BLK // groups
    for r, i in enumerate((i0, i1, i2, i3)):
        order[turn(lax.axis_index("basis"), -r, groups)] = i[...].astype(F32)
    for j, out in enumerate((grad_ref, act_ref)):
        for n in range(nblk):
            whole = jnp.concatenate([order[g, j, :, n * share : (n + 1) * share] for g in range(groups)], axis=1)
            out[:, n * BLK : (n + 1) * BLK] = whole.astype(BF)


def local(
    entity_rows,
    self_weight,
    bases,
    coefficients,
    send_block,
    edge_rel,
    edge_dst,
    edge_count,
    cotangent,
):
    peers = lax.axis_size(ENT)
    groups = lax.axis_size("basis")
    ent_dev, width = entity_rows.shape
    nblk = ent_dev // BLK
    own = bases.shape[0]
    nbase = own * groups
    relations = coefficients.shape[0]
    cap = send_block.shape[2]
    slots = peers * cap
    share = BLK // groups
    halves = width // LANES
    nz = lax.axis_size("z")
    rows = nblk * share
    dma = pltpu.SemaphoreType.DMA

    def over(axis, r, value):
        n = lax.axis_size(axis)
        return lax.ppermute(value, axis, [(i, (i + r) % n) for i in range(n)])

    src, rel_out = send_block[0].T, edge_rel[0].T
    dst, cnt = edge_dst[:, 0, :].T, edge_count[:, 0, :].T

    per = cap * halves * share
    outgoing = call(
        functools.partial(take_body, share),
        hbm(peers, per + 8, LANES),
        [HB] * 3,
        [
            pltpu.SMEM((cap, peers), jnp.int32),
            pltpu.SMEM((cap, peers), jnp.int32),
            pltpu.VMEM((rows, width), BF),
            pltpu.VMEM((peers, per + 8, LANES), BF),
            dma((2,)),
            dma((nblk,)),
            dma((4,)),
        ],
        outs_in=HB,
    )(far(src), far(rel_out), far(entity_rows))
    incoming = lax.all_to_all(outgoing, ENT, split_axis=0, concat_axis=0, tiled=True)

    bases, _ = lax.optimization_barrier((bases, outgoing))
    table = lax.all_gather(bases.reshape(own * width, width), "basis")
    chunks = -(-relations // width)
    coef = jnp.pad(coefficients.astype(BF).T, ((0, 16 - own), (0, chunks * width - relations)))
    coef = coef.reshape(16, chunks, width).transpose(1, 0, 2).reshape(chunks * 16, width)
    coefs = [coef] + [over("basis", r, coef) for r in range(1, groups)]
    tables = pltpu.VMEM((groups, own * width, width), BF)
    incoming = incoming.reshape(peers * (per + 8), LANES)
    *ys, back, pg, rel_in, act = call(
        functools.partial(fwd_body, cap, nblk, own),
        (
            *[hbm((own + 1) * rows, width) for _ in range(groups)],
            hbm(peers, per, LANES),
            bf(rows, width),
            jax.ShapeDtypeStruct((1, slots), jnp.int32),
            bf(groups, width // groups, rows),
        ),
        [SM] * 2 + [VM] * 8 + [HB] * 3,
        [
            pltpu.VMEM((peers * (per + 8), LANES), F32),
            rows_scratch(nbase * nblk * (share + GAP), width),
            pltpu.VMEM((groups, own, slots), F32),
            pltpu.VMEM((width, rows), F32),
            tables,
            pltpu.VMEM((rows, width), BF),
            pltpu.VMEM((rows, width), BF),
            pltpu.VMEM((groups, (own + 1) * rows, width), BF),
            pltpu.VMEM((peers, per, LANES), BF),
            dma((groups,)),
            dma((nblk,)),
            dma((nblk,)),
            dma((groups,)),
            dma((groups,)),
            dma((4,)),
        ],
        limit=30,
        outs_in=(HB,) * (groups + 1) + (VM,) * 3,
    )(
        dst, cnt, incoming, dst, cnt, *coefs, self_weight, far(table),
        far(entity_rows), far(cotangent),
    )

    returned = lax.all_to_all(back, ENT, split_axis=0, concat_axis=0, tiled=True)
    ys = [ys[0]] + [over("basis", r, ys[r]) for r in range(1, groups)]

    *scores, w_out = call(
        functools.partial(score_body, cap, nblk, own, halves),
        (*[jax.ShapeDtypeStruct((own, slots), F32) for _ in range(groups)], bf(nblk * nbase, slots)),
        [VM] * 10 + [HB],
        [
            pltpu.VMEM((peers * (per + 8), LANES), F32),
            rows_scratch(nbase * nblk * (share + GAP), width),
            pltpu.VMEM((nbase, slots), F32),
            tables,
            pltpu.VMEM((groups, own, slots), F32),
            dma((groups,)),
        ],
        limit=20,
        cost=COST,
    )(pg, dst, cnt, incoming, rel_out, src, *coefs, far(table))
    scores = [scores[0]] + [over("basis", r, scores[r]) for r in range(1, groups)]
    lot = chunks * own
    coef_part = call(coef_body, bf(lot, width), [VM] * 5, limit=4)(rel_in, *scores)

    ys = lax.optimization_barrier((*ys, scores[2], scores[3]))[:groups]
    part = own * width // NC
    keep, send = call(
        functools.partial(basis_body, own, rows, peers),
        (bf(part, width), bf(part, width)),
        [VM] * 4,
        [rows_scratch(2 * width, width), rows_scratch(2 * NC * part, width)],
        limit=12,
    )(*ys)
    got = over("c", 1, send)
    each = part // NX
    outs = call(
        core_body,
        tuple(bf(each + lot, width) for _ in range(NX)),
        [VM] * 4,
        [pltpu.VMEM((part, width), F32)],
        limit=8,
    )(keep, got, coef_part, over("c", 1, coef_part))
    ins = [outs[0]] + [over("x", r, outs[r]) for r in range(1, NX)]

    grads = call(
        functools.partial(bwd_body, cap, own),
        tuple(bf(2, width // groups, rows) for _ in range(groups)),
        [VM] * 5 + [HB],
        [
            pltpu.VMEM((peers * (per + GAP), LANES), F32),
            rows_scratch(nbase * nblk * (share + GAP), width),
            pltpu.VMEM((width, rows), F32),
            tables,
            dma((groups,)),
        ],
        limit=20,
    )(returned.reshape(peers * per, LANES), w_out, act, pg, self_weight, far(table))

    last = each // nz
    out = call(
        x_body,
        bf(nz, last + lot, width),
        [VM] * NX,
        [pltpu.VMEM((NX, lot, width), F32)],
        limit=4,
    )(*ins)
    out = lax.all_to_all(out, "z", split_axis=0, concat_axis=0, tiled=True)
    basis_grad, coef_grad = call(
        functools.partial(z_body, own),
        (jax.ShapeDtypeStruct((own, width // peers, width), F32), jax.ShapeDtypeStruct((own, relations), F32)),
        [VM],
        limit=4,
    )(out)

    grads = [grads[0]] + [over("basis", r, grads[r]) for r in range(1, groups)]
    cols = width // groups
    entity_grad, activation = call(
        functools.partial(join_body, nblk),
        (bf(cols, ent_dev), bf(cols, ent_dev)),
        [VM] * groups,
        [pltpu.VMEM((groups, 2, cols, rows), F32)],
        limit=4,
    )(*grads)
    return (activation.T, basis_grad, coef_grad.T, entity_grad.T)


def solution(mesh):
    nz = mesh.devices.shape[0] // (NX * NC)
    fine = Mesh(mesh.devices.reshape(nz, NX, NC, mesh.devices.shape[1]), (*ENT, "basis"))
    placed = (
        P(ENT, None),
        P(),
        P("basis", None, None),
        P(None, "basis"),
        P(ENT, None, None),
        P(ENT, None, None),
        P(None, ENT, None),
        P(None, ENT, None),
        P(ENT, None),
    )
    return jax.shard_map(
        local,
        mesh=fine,
        in_specs=placed,
        out_specs=(P(ENT, "basis"), P("basis", ENT, None), P(None, "basis"), P(ENT, "basis")),
        check_vma=False,
    )
```

```python
import functools

import jax
import jax.numpy as jnp
from jax import lax
from jax.experimental import pallas as pl
from jax.experimental.pallas import tpu as pltpu
from jax.sharding import Mesh
from jax.sharding import PartitionSpec as P

BLK = 128
LANES = 128
GAP = 8
ORDER = (0, 2, 1, 3)
NX = 4
NC = 2
ENT = ("z", "x", "c")
BF = jnp.bfloat16
F32 = jnp.float32
NT = (((1,), (1,)), ((), ()))
TN = (((0,), (0,)), ((), ()))
MIB = 1024 * 1024
VM = pl.BlockSpec(memory_space=pltpu.VMEM)
SM = pl.BlockSpec(memory_space=pltpu.SMEM)
COST = pl.CostEstimate(flops=8 * 10**9, transcendentals=0, bytes_accessed=20 * 10**6)
HB = pl.BlockSpec(memory_space=pltpu.HBM)


def call(body, outs, ins, scratch=(), limit=16, outs_in=None, cost=None):
    return pl.pallas_call(
        body,
        out_shape=outs,
        in_specs=ins,
        out_specs=outs_in or jax.tree.map(lambda _: VM, outs),
        scratch_shapes=list(scratch),
        cost_estimate=cost,
        compiler_params=pltpu.CompilerParams(vmem_limit_bytes=limit * MIB),
    )


def bf(*shape):
    return jax.ShapeDtypeStruct(shape, BF)


def hbm(*shape):
    return pltpu.HBM(shape, BF)


def far(value):
    return pltpu.with_memory_space_constraint(value, pltpu.HBM)


def get(ref, at):
    return jnp.concatenate([ref[h, at, :] for h in range(ref.shape[0])], axis=1)


def put(ref, at, value):
    for h in range(ref.shape[0]):
        ref[h, at, :] = value[:, h * LANES : (h + 1) * LANES]


def rows_scratch(rows, width):
    return pltpu.VMEM((width // LANES, rows, LANES), F32)


def turn(i, r, n):
    return lax.rem(i + r + n, n)


def spaced(i, size):
    return pl.ds(pl.multiple_of(i * (size + GAP), 8), size)


def aligned(i, size):
    return pl.ds(pl.multiple_of(i * size, size), size)


def digits(value):
    high = value.astype(BF)
    return high, (value - high.astype(F32)).astype(BF)


def start_all(copies):
    for copy in copies:
        copy.start()
    return copies


def wait_all(copies):
    for copy in copies:
        copy.wait()


def own_row_copies(ref, scr, sem, share):
    first = lax.axis_index("basis") * share
    return [
        pltpu.make_async_copy(
            ref.at[pl.ds(pl.multiple_of(n * BLK + first, share), share), :],
            scr.at[pl.ds(n * share, share), :],
            sem.at[n],
        )
        for n in range(scr.shape[0] // share)
    ]


def line(ref):
    return jnp.concatenate([ref[c : c + 1, :] for c in range(ref.shape[0])], axis=1)


def take_body(share, src_ref, edge_ref, ent_ref, out_ref, idx_ref, rel_ref, own, outs, isem, sem, osem):
    copies = own_row_copies(ent_ref, own, sem, share)
    copies += [pltpu.make_async_copy(src_ref, idx_ref, isem.at[0]), pltpu.make_async_copy(edge_ref, rel_ref, isem.at[1])]
    wait_all(start_all(copies))
    cap, peers = idx_ref.shape
    halves = own.shape[1] // LANES
    lane = lax.broadcasted_iota(jnp.int32, (8, LANES), 1)
    lots = osem.shape[0]
    lot = peers // lots
    copies = []
    for q in range(peers):
        note = jnp.zeros((8, LANES), jnp.int32)
        for c in range(cap):
            block = own[aligned(idx_ref[c, q], share), :]
            for h in range(halves):
                outs[q, pl.ds((c * halves + h) * share, share), :] = block[:, h * LANES : (h + 1) * LANES]
            rel = rel_ref[c, q]
            note = jnp.where(lane == 2 * c, rel >> 8, note)
            note = jnp.where(lane == 2 * c + 1, rel & 255, note)
        outs[q, pl.ds(cap * halves * share, 8), :] = note.astype(F32).astype(BF)
        if (q + 1) % lot == 0:
            i = q // lot
            at = pl.ds(i * lot, lot)
            copies += start_all([pltpu.make_async_copy(outs.at[at], out_ref.at[at], osem.at[i])])
    wait_all(copies)


def slot_weights(own, coef_refs, rel, blk, nblk, cs):
    groups = len(coef_refs)
    rows, width = coef_refs[0].shape
    chunks = rows // 16
    slots = rel.shape[1]
    parts = [jnp.zeros((16, slots), F32) for _ in coef_refs]
    for j in range(chunks):
        ids = lax.broadcasted_iota(jnp.int32, (width, slots), 0) + j * width
        hot = jnp.where(ids == rel, 1.0, 0.0).astype(BF)
        for r, ref in enumerate(coef_refs):
            parts[r] += jnp.dot(ref[pl.ds(j * 16, 16), :], hot, preferred_element_type=F32)
    for r in range(groups):
        cs[turn(lax.axis_index("basis"), -r, groups)] = parts[r][:own]
    coef = cs[...].reshape(groups * own, slots)
    return jnp.concatenate([jnp.where(blk == n, coef, 0.0) for n in range(nblk)], axis=0)


def widen(x_ref, xf, peers):
    per = x_ref.shape[0] // peers
    space = xf.shape[0] // peers

    def some(p, c):
        xf[pl.ds(pl.multiple_of(p * space, 8), per), :] = x_ref[aligned(p, per), :].astype(F32)
        return c

    def straight(i, c):
        at = aligned(i, 4 * LANES)
        xf[at, :] = x_ref[at, :].astype(F32)
        return c

    if space == per:
        lax.fori_loop(0, x_ref.shape[0] // (4 * LANES), straight, 0)
    else:
        lax.fori_loop(0, peers, some, 0, unroll=4)


def slot_rows(xf, peers, cap, halves, share, k):
    per = xf.shape[0] // peers
    return jnp.concatenate(
        [
            jnp.concatenate(
                [xf[pl.ds((c * halves + h) * share + k, peers, stride=per), :] for h in range(halves)], axis=1
            )
            for c in range(cap)
        ],
        axis=0,
    )


def rows_of(mf, base, nbase, nblk, share):
    return jnp.concatenate([get(mf, spaced(n * nbase + base, share)) for n in range(nblk)], axis=0)


def table_copies(table_ref, tab, sem):
    return [pltpu.make_async_copy(table_ref.at[g], tab.at[g], sem.at[g]) for g in range(tab.shape[0])]


def fwd_body(
    cap, nblk, own, dst_ref, count_ref, x_ref, dstv_ref, cnt_ref, c0, c1, c2, c3, sw_ref, table_ref, ent_ref,
    cot_ref, y0, y1, y2, y3, back_ref, pg_ref, rel_ref, act_ref,
    xf, mf, cs, at_ref, tab, ent, cot, ysc, back, tsem, esem, csem, ysem, psem, bsem,
):
    groups = tab.shape[0]
    nbase = groups * own
    width = tab.shape[2]
    halves = width // LANES
    share = BLK // groups
    peers = back.shape[0]
    per = xf.shape[0] // peers
    group0 = lax.axis_index("basis")
    first = group0 * share
    ecopies = start_all(own_row_copies(ent_ref, ent, esem, share))
    tcopies = start_all(table_copies(table_ref, tab, tsem))
    ccopies = start_all(own_row_copies(cot_ref, cot, csem, share))
    widen(x_ref, xf, peers)
    notes = xf[pl.ds(cap * halves * share, peers, stride=per), :].astype(BF)
    lane = lax.broadcasted_iota(jnp.int32, (8, LANES), 1)
    row = lax.broadcasted_iota(jnp.int32, (8, LANES), 0)
    pick = jnp.where(lane == 2 * row, 256.0, jnp.where(lane == 2 * row + 1, 1.0, 0.0)).astype(BF)
    rels = lax.dot_general(pick, notes, NT, preferred_element_type=F32).astype(jnp.int32)
    rel = jnp.concatenate([rels[c : c + 1] for c in range(cap)], axis=1)
    rel_ref[...] = rel
    w = slot_weights(own, (c0, c1, c2, c3), rel, line(dstv_ref), nblk, cs)
    cnt = line(cnt_ref)

    def one(k, c):
        xk = slot_rows(xf, peers, cap, halves, share, k).astype(BF)
        wk = jnp.where(cnt > first + k, w, 0.0).astype(BF)
        put(mf, pl.ds(k, w.shape[0], stride=share + GAP), jnp.dot(wk, xk, preferred_element_type=F32))
        return c

    lax.fori_loop(0, share, one, 0, unroll=8)
    copies = []
    wait_all(ecopies)
    acc = jnp.dot(ent[...], sw_ref[...], preferred_element_type=F32)
    rows = nblk * share
    ys = (y0, y1, y2, y3)
    wait_all(tcopies)
    for r in range(groups):
        group = turn(group0, r, groups)
        for b in range(own):
            mb = rows_of(mf, group * own + b, nbase, nblk, share).astype(BF)
            ysc[r, pl.ds(b * rows, rows), :] = mb
            acc += jnp.dot(mb, tab[group, pl.ds(b * width, width), :], preferred_element_type=F32)
        if r:
            at = pl.ds(0, own * rows)
            copies += start_all([pltpu.make_async_copy(ysc.at[r, at], ys[r].at[at], ysem.at[r])])
    s = jax.nn.sigmoid(acc)
    at_ref[...] = (acc * s).T
    wait_all(ccopies)
    pg = (cot[...].astype(F32) * (s * (1.0 + acc * (1.0 - s)))).astype(BF)
    pg_ref[...] = pg
    k_of = lax.broadcasted_iota(jnp.int32, (share, width), 0) + first
    lots = bsem.shape[0]
    lot = peers // lots
    for q in range(peers):
        for c in range(cap):
            block = pg_ref[aligned(dst_ref[c, q], share), :]
            block = jnp.where(k_of < count_ref[c, q], block.astype(F32), 0.0).astype(BF)
            for h in range(halves):
                back[q, pl.ds((c * halves + h) * share, share), :] = block[:, h * LANES : (h + 1) * LANES]
        if (q + 1) % lot == 0:
            i = q // lot
            at = pl.ds(i * lot, lot)
            copies += start_all([pltpu.make_async_copy(back.at[at], back_ref.at[at], bsem.at[i])])
    cols = width // groups
    at = pl.ds(own * rows, rows)
    for r in range(groups):
        ysc[r, at, :] = pg
        copies += start_all([pltpu.make_async_copy(ysc.at[r, at] if r else ysc.at[r], ys[r].at[at] if r else ys[r], psem.at[r])])
        act_ref[r] = at_ref[aligned(turn(group0, r, groups), cols), :].astype(BF)
    wait_all(copies)


def score_body(
    cap, nblk, own, halves, pg_ref, dstv_ref, cnt_ref, x_ref, rel_ref, src_ref, c0, c1, c2, c3, table_ref,
    s0, s1, s2, s3, w_ref, xf, pf, ts, tab, cs, tsem,
):
    groups = tab.shape[0]
    nbase = groups * own
    width = tab.shape[2]
    peers = cnt_ref.shape[1]
    slots = cap * peers
    share = BLK // groups
    group0 = lax.axis_index("basis")
    first = group0 * share
    tcopies = start_all(table_copies(table_ref, tab, tsem))
    w_ref[...] = slot_weights(own, (c0, c1, c2, c3), line(rel_ref), line(src_ref), nblk, cs).astype(BF)
    widen(x_ref, xf, peers)
    pg = pg_ref[...]
    for b in range(nbase):
        if b % own == 0:
            tcopies[b // own].wait()
        base = tab[b // own, pl.ds((b % own) * width, width), :]
        p = lax.dot_general(pg, base, NT, preferred_element_type=F32)
        for n in range(nblk):
            put(pf, spaced(n * nbase + b, share), p[n * share : (n + 1) * share])
    cnt = line(cnt_ref)

    def one(k, acc):
        pk = get(pf, pl.ds(k, nblk * nbase, stride=share + GAP)).astype(BF)
        xk = slot_rows(xf, peers, cap, halves, share, k).astype(BF)
        t = lax.dot_general(pk, xk, NT, preferred_element_type=F32)
        return acc + jnp.where(cnt > first + k, t, 0.0)

    acc = lax.fori_loop(0, share, one, jnp.zeros((nblk * nbase, slots), F32), unroll=4)
    blk = line(dstv_ref)
    total = jnp.zeros((nbase, slots), F32)
    for n in range(nblk):
        total += jnp.where(blk == n, acc[n * nbase : (n + 1) * nbase], 0.0)
    ts[...] = total
    for r, out in enumerate((s0, s1, s2, s3)):
        out[...] = ts[aligned(turn(group0, r, groups), own), :]


def coef_body(rel_ref, s0, s1, s2, s3, out_ref):
    own, slots = s0.shape
    width = out_ref.shape[1]
    chunks = out_ref.shape[0] // own
    high, low = digits((s0[...] + s1[...]) + (s2[...] + s3[...]))
    both = jnp.concatenate([high.astype(F32), low.astype(F32)], axis=0).astype(BF)
    rel = rel_ref[...]
    parts = []
    for j in range(chunks):
        ids = lax.broadcasted_iota(jnp.int32, (width, slots), 0) + j * width
        hot = jnp.where(ids == rel, 1.0, 0.0).astype(BF)
        t = lax.dot_general(both, hot, NT, preferred_element_type=F32)
        parts.append(t[:own] + t[own:])
    out_ref[...] = jnp.concatenate(parts, axis=0).astype(BF)


def basis_body(own, rows, peers, y0, y1, y2, y3, keep_ref, send_ref, tmp, outf):
    ys = (y0, y1, y2, y3)
    width = y0.shape[1]
    part = keep_ref.shape[0]
    each = part // NX
    deep = part * NC // (own * peers)
    lines = own * deep
    nz = each // lines
    plane = NX * NC * deep
    pg = jnp.concatenate([y[pl.ds(own * rows, rows), :] for y in ys], axis=0)
    for b in range(own):
        m = jnp.concatenate([y[pl.ds(b * rows, rows), :] for y in ys], axis=0)
        t = lax.dot_general(m, pg, TN, preferred_element_type=F32)
        for z in range(nz):
            put(tmp, spaced(z, plane), t[z * plane : (z + 1) * plane])
        for c in range(NC):
            for x in range(NX):
                for d in range(deep):
                    put(
                        outf,
                        pl.ds((c * NX + x) * nz * (lines + GAP) + b * deep + d, nz, stride=lines + GAP),
                        get(tmp, pl.ds((x * NC + c) * deep + d, nz, stride=plane + GAP)),
                    )
    core = lax.axis_index("c")
    for i in range(NX * nz):
        keep_ref[pl.ds(i * lines, lines), :] = get(outf, spaced(core * (NX * nz) + i, lines)).astype(BF)
        send_ref[pl.ds(i * lines, lines), :] = get(outf, spaced((1 - core) * (NX * nz) + i, lines)).astype(BF)


def core_body(keep_ref, got_ref, coef_ref, other_ref, o0, o1, o2, o3, sums):
    part = keep_ref.shape[0]
    each = part // NX
    sums[...] = keep_ref[...].astype(F32) + got_ref[...].astype(F32)
    coef = (coef_ref[...].astype(F32) + other_ref[...].astype(F32)).astype(BF)
    for r, out in enumerate((o0, o1, o2, o3)):
        out[pl.ds(0, each), :] = sums[aligned(turn(lax.axis_index("x"), r, NX), each), :].astype(BF)
        out[pl.ds(each, coef.shape[0]), :] = coef


def x_body(i0, i1, i2, i3, out_ref, order):
    n = order.shape[1]
    each = i0.shape[0] - n
    nz = out_ref.shape[0]
    last = each // nz
    sums = sum(i[pl.ds(0, each), :].astype(F32) for i in (i0, i1, i2, i3))
    for r, i in zip(ORDER, (i0, i1, i2, i3)):
        order[turn(lax.axis_index("x"), -r, NX)] = i[pl.ds(each, n), :].astype(F32)
    coef = ((order[0] + order[1]) + (order[2] + order[3])).astype(BF)
    for z in range(nz):
        out_ref[z, pl.ds(0, last), :] = sums[z * last : (z + 1) * last].astype(BF)
        out_ref[z, pl.ds(last, n), :] = coef


def z_body(own, in_ref, basis_ref, coef_ref):
    nz, rows, width = in_ref.shape
    deep = basis_ref.shape[1]
    last = own * deep
    n = rows - last
    basis = jnp.zeros((last, width), F32)
    coef = jnp.zeros((n, width), F32)
    for z in range(nz):
        basis += in_ref[z, pl.ds(0, last), :].astype(F32)
        coef += in_ref[z, pl.ds(last, n), :].astype(F32)
    for b in range(own):
        basis_ref[b] = basis[b * deep : (b + 1) * deep]
    relations = coef_ref.shape[1]
    for j in range(n // own):
        size = min(width, relations - j * width)
        coef_ref[:, pl.ds(j * width, size)] = coef[j * own : (j + 1) * own, :size]


def bwd_body(
    cap, own, x_ref, w_ref, act_ref, pg_ref, sw_ref, table_ref, o0, o1, o2, o3, xf, mf, at_ref, tab, tsem
):
    groups = tab.shape[0]
    nbase = groups * own
    width = tab.shape[2]
    halves = width // LANES
    share = BLK // groups
    slots = w_ref.shape[1]
    peers = slots // cap
    nblk = w_ref.shape[0] // nbase
    tcopies = start_all(table_copies(table_ref, tab, tsem))
    widen(x_ref, xf, peers)
    w = w_ref[...]

    def one(k, c):
        xk = slot_rows(xf, peers, cap, halves, share, k).astype(BF)
        put(mf, pl.ds(k, w.shape[0], stride=share + GAP), jnp.dot(w, xk, preferred_element_type=F32))
        return c

    lax.fori_loop(0, share, one, 0, unroll=8)
    acc = lax.dot_general(sw_ref[...], pg_ref[...], NT, preferred_element_type=F32)
    wait_all(tcopies)
    for b in range(nbase):
        mb = rows_of(mf, b, nbase, nblk, share).astype(BF)
        base = tab[b // own, pl.ds((b % own) * width, width), :]
        acc += lax.dot_general(base, mb, NT, preferred_element_type=F32)
    at_ref[...] = acc
    cols = width // groups
    for r, out in enumerate((o0, o1, o2, o3)):
        out[0] = at_ref[aligned(turn(lax.axis_index("basis"), r, groups), cols), :].astype(BF)
        out[1] = act_ref[r]


def join_body(nblk, i0, i1, i2, i3, grad_ref, act_ref, order):
    groups = order.shape[0]
    share = BLK // groups
    for r, i in zip(ORDER, (i0, i1, i2, i3)):
        order[turn(lax.axis_index("basis"), -r, groups)] = i[...].astype(F32)
    for j, out in enumerate((grad_ref, act_ref)):
        for n in range(nblk):
            whole = jnp.concatenate([order[g, j, :, n * share : (n + 1) * share] for g in range(groups)], axis=1)
            out[:, n * BLK : (n + 1) * BLK] = whole.astype(BF)


def local(
    entity_rows,
    self_weight,
    bases,
    coefficients,
    send_block,
    edge_rel,
    edge_dst,
    edge_count,
    cotangent,
):
    peers = lax.axis_size(ENT)
    groups = lax.axis_size("basis")
    ent_dev, width = entity_rows.shape
    nblk = ent_dev // BLK
    own = bases.shape[0]
    nbase = own * groups
    relations = coefficients.shape[0]
    cap = send_block.shape[2]
    slots = peers * cap
    share = BLK // groups
    halves = width // LANES
    nz = lax.axis_size("z")
    rows = nblk * share
    dma = pltpu.SemaphoreType.DMA

    def over(axis, r, value):
        n = lax.axis_size(axis)
        return lax.ppermute(value, axis, [(i, (i + r) % n) for i in range(n)])

    def exchange(axis, values):
        return [over(axis, r, values[r]) if r else values[0] for r in ORDER]

    src, rel_out = send_block[0].T, edge_rel[0].T
    dst, cnt = edge_dst[:, 0, :].T, edge_count[:, 0, :].T

    per = cap * halves * share
    outgoing = call(
        functools.partial(take_body, share),
        hbm(peers, per + 8, LANES),
        [HB] * 3,
        [
            pltpu.SMEM((cap, peers), jnp.int32),
            pltpu.SMEM((cap, peers), jnp.int32),
            pltpu.VMEM((rows, width), BF),
            pltpu.VMEM((peers, per + 8, LANES), BF),
            dma((2,)),
            dma((nblk,)),
            dma((4,)),
        ],
        outs_in=HB,
    )(far(src), far(rel_out), far(entity_rows))
    incoming = lax.all_to_all(outgoing, ENT, split_axis=0, concat_axis=0, tiled=True)

    bases, _ = lax.optimization_barrier((bases, outgoing))
    table = lax.all_gather(bases.reshape(own * width, width), "basis")
    chunks = -(-relations // width)
    coef = jnp.pad(coefficients.astype(BF).T, ((0, 16 - own), (0, chunks * width - relations)))
    coef = coef.reshape(16, chunks, width).transpose(1, 0, 2).reshape(chunks * 16, width)
    coefs = [coef] + [over("basis", r, coef) for r in range(1, groups)]
    tables = pltpu.VMEM((groups, own * width, width), BF)
    incoming = incoming.reshape(peers * (per + 8), LANES)
    *ys, back, pg, rel_in, act = call(
        functools.partial(fwd_body, cap, nblk, own),
        (
            *[hbm((own + 1) * rows, width) for _ in range(groups)],
            hbm(peers, per, LANES),
            bf(rows, width),
            jax.ShapeDtypeStruct((1, slots), jnp.int32),
            bf(groups, width // groups, rows),
        ),
        [SM] * 2 + [VM] * 8 + [HB] * 3,
        [
            pltpu.VMEM((peers * (per + 8), LANES), F32),
            rows_scratch(nbase * nblk * (share + GAP), width),
            pltpu.VMEM((groups, own, slots), F32),
            pltpu.VMEM((width, rows), F32),
            tables,
            pltpu.VMEM((rows, width), BF),
            pltpu.VMEM((rows, width), BF),
            pltpu.VMEM((groups, (own + 1) * rows, width), BF),
            pltpu.VMEM((peers, per, LANES), BF),
            dma((groups,)),
            dma((nblk,)),
            dma((nblk,)),
            dma((groups,)),
            dma((groups,)),
            dma((4,)),
        ],
        limit=30,
        outs_in=(HB,) * (groups + 1) + (VM,) * 3,
    )(
        dst, cnt, incoming, dst, cnt, *coefs, self_weight, far(table),
        far(entity_rows), far(cotangent),
    )

    returned = lax.all_to_all(back, ENT, split_axis=0, concat_axis=0, tiled=True)
    ys = exchange("basis", ys)

    *scores, w_out = call(
        functools.partial(score_body, cap, nblk, own, halves),
        (*[jax.ShapeDtypeStruct((own, slots), F32) for _ in range(groups)], bf(nblk * nbase, slots)),
        [VM] * 10 + [HB],
        [
            pltpu.VMEM((peers * (per + 8), LANES), F32),
            rows_scratch(nbase * nblk * (share + GAP), width),
            pltpu.VMEM((nbase, slots), F32),
            tables,
            pltpu.VMEM((groups, own, slots), F32),
            dma((groups,)),
        ],
        limit=20,
        cost=COST,
    )(pg, dst, cnt, incoming, rel_out, src, *coefs, far(table))
    scores = [scores[0]] + [over("basis", r, scores[r]) for r in range(1, groups)]
    lot = chunks * own
    coef_part = call(coef_body, bf(lot, width), [VM] * 5, limit=4)(rel_in, *scores)

    ys = lax.optimization_barrier((*ys, scores[2], scores[3]))[:groups]
    part = own * width // NC
    keep, send = call(
        functools.partial(basis_body, own, rows, peers),
        (bf(part, width), bf(part, width)),
        [VM] * 4,
        [rows_scratch(2 * width, width), rows_scratch(2 * NC * part, width)],
        limit=12,
    )(*ys)
    got = over("c", 1, send)
    each = part // NX
    outs = call(
        core_body,
        tuple(bf(each + lot, width) for _ in range(NX)),
        [VM] * 4,
        [pltpu.VMEM((part, width), F32)],
        limit=8,
    )(keep, got, coef_part, over("c", 1, coef_part))
    ins = exchange("x", outs)

    grads = call(
        functools.partial(bwd_body, cap, own),
        tuple(bf(2, width // groups, rows) for _ in range(groups)),
        [VM] * 5 + [HB],
        [
            pltpu.VMEM((peers * (per + GAP), LANES), F32),
            rows_scratch(nbase * nblk * (share + GAP), width),
            pltpu.VMEM((width, rows), F32),
            tables,
            dma((groups,)),
        ],
        limit=20,
    )(returned.reshape(peers * per, LANES), w_out, act, pg, self_weight, far(table))

    last = each // nz
    out = call(
        x_body,
        bf(nz, last + lot, width),
        [VM] * NX,
        [pltpu.VMEM((NX, lot, width), F32)],
        limit=4,
    )(*ins)
    out = lax.all_to_all(out, "z", split_axis=0, concat_axis=0, tiled=True)
    basis_grad, coef_grad = call(
        functools.partial(z_body, own),
        (jax.ShapeDtypeStruct((own, width // peers, width), F32), jax.ShapeDtypeStruct((own, relations), F32)),
        [VM],
        limit=4,
    )(out)

    grads = exchange("basis", grads)
    cols = width // groups
    entity_grad, activation = call(
        functools.partial(join_body, nblk),
        (bf(cols, ent_dev), bf(cols, ent_dev)),
        [VM] * groups,
        [pltpu.VMEM((groups, 2, cols, rows), F32)],
        limit=4,
    )(*grads)
    return (activation.T, basis_grad, coef_grad.T, entity_grad.T)


def solution(mesh):
    nz = mesh.devices.shape[0] // (NX * NC)
    fine = Mesh(mesh.devices.reshape(nz, NX, NC, mesh.devices.shape[1]), (*ENT, "basis"))
    placed = (
        P(ENT, None),
        P(),
        P("basis", None, None),
        P(None, "basis"),
        P(ENT, None, None),
        P(ENT, None, None),
        P(None, ENT, None),
        P(None, ENT, None),
        P(ENT, None),
    )
    return jax.shard_map(
        local,
        mesh=fine,
        in_specs=placed,
        out_specs=(P(ENT, "basis"), P("basis", ENT, None), P(None, "basis"), P(ENT, "basis")),
        check_vma=False,
    )
```

```python
import functools

import jax
import jax.numpy as jnp
from jax import lax
from jax.experimental import pallas as pl
from jax.experimental.pallas import tpu as pltpu
from jax.sharding import Mesh
from jax.sharding import PartitionSpec as P

BLK = 128
LANES = 128
GAP = 8
ORDER = (0, 2, 1, 3)
NX = 4
NC = 2
ENT = ("z", "x", "c")
BF = jnp.bfloat16
F32 = jnp.float32
NT = (((1,), (1,)), ((), ()))
TN = (((0,), (0,)), ((), ()))
MIB = 1024 * 1024
VM = pl.BlockSpec(memory_space=pltpu.VMEM)
SM = pl.BlockSpec(memory_space=pltpu.SMEM)
COST = pl.CostEstimate(flops=8 * 10**9, transcendentals=0, bytes_accessed=20 * 10**6)
HB = pl.BlockSpec(memory_space=pltpu.HBM)


def call(body, outs, ins, scratch=(), limit=16, outs_in=None, cost=None):
    return pl.pallas_call(
        body,
        out_shape=outs,
        in_specs=ins,
        out_specs=outs_in or jax.tree.map(lambda _: VM, outs),
        scratch_shapes=list(scratch),
        cost_estimate=cost,
        compiler_params=pltpu.CompilerParams(vmem_limit_bytes=limit * MIB),
    )


def bf(*shape):
    return jax.ShapeDtypeStruct(shape, BF)


def hbm(*shape):
    return pltpu.HBM(shape, BF)


def far(value):
    return pltpu.with_memory_space_constraint(value, pltpu.HBM)


def get(ref, at):
    return jnp.concatenate([ref[h, at, :] for h in range(ref.shape[0])], axis=1)


def put(ref, at, value):
    for h in range(ref.shape[0]):
        ref[h, at, :] = value[:, h * LANES : (h + 1) * LANES]


def rows_scratch(rows, width):
    return pltpu.VMEM((width // LANES, rows, LANES), F32)


def turn(i, r, n):
    return lax.rem(i + r + n, n)


def spaced(i, size):
    return pl.ds(pl.multiple_of(i * (size + GAP), 8), size)


def aligned(i, size):
    return pl.ds(pl.multiple_of(i * size, size), size)


def digits(value):
    high = value.astype(BF)
    return high, (value - high.astype(F32)).astype(BF)


def start_all(copies):
    for copy in copies:
        copy.start()
    return copies


def wait_all(copies):
    for copy in copies:
        copy.wait()


def own_row_copies(ref, scr, sem, share):
    first = lax.axis_index("basis") * share
    return [
        pltpu.make_async_copy(
            ref.at[pl.ds(pl.multiple_of(n * BLK + first, share), share), :],
            scr.at[pl.ds(n * share, share), :],
            sem.at[n],
        )
        for n in range(scr.shape[0] // share)
    ]


def line(ref):
    return jnp.concatenate([ref[c : c + 1, :] for c in range(ref.shape[0])], axis=1)


def take_body(share, src_ref, edge_ref, ent_ref, out_ref, idx_ref, rel_ref, own, outs, isem, sem, osem):
    copies = own_row_copies(ent_ref, own, sem, share)
    copies += [pltpu.make_async_copy(src_ref, idx_ref, isem.at[0]), pltpu.make_async_copy(edge_ref, rel_ref, isem.at[1])]
    wait_all(start_all(copies))
    cap, peers = idx_ref.shape
    halves = own.shape[1] // LANES
    lane = lax.broadcasted_iota(jnp.int32, (8, LANES), 1)
    lots = osem.shape[0]
    lot = peers // lots
    copies = []
    for q in range(peers):
        note = jnp.zeros((8, LANES), jnp.int32)
        for c in range(cap):
            block = own[aligned(idx_ref[c, q], share), :]
            for h in range(halves):
                outs[q, pl.ds((c * halves + h) * share, share), :] = block[:, h * LANES : (h + 1) * LANES]
            rel = rel_ref[c, q]
            note = jnp.where(lane == 2 * c, rel >> 8, note)
            note = jnp.where(lane == 2 * c + 1, rel & 255, note)
        outs[q, pl.ds(cap * halves * share, 8), :] = note.astype(F32).astype(BF)
        if (q + 1) % lot == 0:
            i = q // lot
            at = pl.ds(i * lot, lot)
            copies += start_all([pltpu.make_async_copy(outs.at[at], out_ref.at[at], osem.at[i])])
    wait_all(copies)


def slot_weights(own, coef_refs, rel, blk, nblk, cs):
    groups = len(coef_refs)
    rows, width = coef_refs[0].shape
    chunks = rows // 16
    slots = rel.shape[1]
    parts = [jnp.zeros((16, slots), F32) for _ in coef_refs]
    for j in range(chunks):
        ids = lax.broadcasted_iota(jnp.int32, (width, slots), 0) + j * width
        hot = jnp.where(ids == rel, 1.0, 0.0).astype(BF)
        for r, ref in enumerate(coef_refs):
            parts[r] += jnp.dot(ref[pl.ds(j * 16, 16), :], hot, preferred_element_type=F32)
    for r in range(groups):
        cs[turn(lax.axis_index("basis"), -r, groups)] = parts[r][:own]
    coef = cs[...].reshape(groups * own, slots)
    return jnp.concatenate([jnp.where(blk == n, coef, 0.0) for n in range(nblk)], axis=0)


def widen(x_ref, xf, peers):
    per = x_ref.shape[0] // peers
    space = xf.shape[0] // peers

    def some(p, c):
        xf[pl.ds(pl.multiple_of(p * space, 8), per), :] = x_ref[aligned(p, per), :].astype(F32)
        return c

    def straight(i, c):
        at = aligned(i, 4 * LANES)
        xf[at, :] = x_ref[at, :].astype(F32)
        return c

    if space == per:
        lax.fori_loop(0, x_ref.shape[0] // (4 * LANES), straight, 0)
    else:
        lax.fori_loop(0, peers, some, 0, unroll=4)


def slot_rows(xf, peers, cap, halves, share, k):
    per = xf.shape[0] // peers
    return jnp.concatenate(
        [
            jnp.concatenate(
                [xf[pl.ds((c * halves + h) * share + k, peers, stride=per), :] for h in range(halves)], axis=1
            )
            for c in range(cap)
        ],
        axis=0,
    )


def rows_of(mf, base, nbase, nblk, share):
    return jnp.concatenate([get(mf, spaced(n * nbase + base, share)) for n in range(nblk)], axis=0)


def table_copies(table_ref, tab, sem):
    return [pltpu.make_async_copy(table_ref.at[g], tab.at[g], sem.at[g]) for g in range(tab.shape[0])]


def fwd_body(
    cap, nblk, own, dst_ref, count_ref, x_ref, dstv_ref, cnt_ref, c0, c1, c2, c3, sw_ref, table_ref, ent_ref,
    cot_ref, y0, y1, y2, y3, back_ref, pg_ref, rel_ref, act_ref,
    xf, mf, cs, at_ref, tab, ent, cot, ysc, back, tsem, esem, csem, ysem, psem, bsem,
):
    groups = tab.shape[0]
    nbase = groups * own
    width = tab.shape[2]
    halves = width // LANES
    share = BLK // groups
    peers = back.shape[0]
    per = xf.shape[0] // peers
    group0 = lax.axis_index("basis")
    first = group0 * share
    ecopies = start_all(own_row_copies(ent_ref, ent, esem, share))
    tcopies = start_all(table_copies(table_ref, tab, tsem))
    ccopies = start_all(own_row_copies(cot_ref, cot, csem, share))
    widen(x_ref, xf, peers)
    notes = xf[pl.ds(cap * halves * share, peers, stride=per), :].astype(BF)
    lane = lax.broadcasted_iota(jnp.int32, (8, LANES), 1)
    row = lax.broadcasted_iota(jnp.int32, (8, LANES), 0)
    pick = jnp.where(lane == 2 * row, 256.0, jnp.where(lane == 2 * row + 1, 1.0, 0.0)).astype(BF)
    rels = lax.dot_general(pick, notes, NT, preferred_element_type=F32).astype(jnp.int32)
    rel = jnp.concatenate([rels[c : c + 1] for c in range(cap)], axis=1)
    rel_ref[...] = rel
    w = slot_weights(own, (c0, c1, c2, c3), rel, line(dstv_ref), nblk, cs)
    cnt = line(cnt_ref)

    def one(k, c):
        xk = slot_rows(xf, peers, cap, halves, share, k).astype(BF)
        wk = jnp.where(cnt > first + k, w, 0.0).astype(BF)
        put(mf, pl.ds(k, w.shape[0], stride=share + GAP), jnp.dot(wk, xk, preferred_element_type=F32))
        return c

    lax.fori_loop(0, share, one, 0, unroll=8)
    copies = []
    wait_all(ecopies)
    acc = jnp.dot(ent[...], sw_ref[...], preferred_element_type=F32)
    rows = nblk * share
    ys = (y0, y1, y2, y3)
    wait_all(tcopies)
    for r in range(groups):
        group = turn(group0, r, groups)
        for b in range(own):
            mb = rows_of(mf, group * own + b, nbase, nblk, share).astype(BF)
            ysc[r, pl.ds(b * rows, rows), :] = mb
            acc += jnp.dot(mb, tab[group, pl.ds(b * width, width), :], preferred_element_type=F32)
        if r:
            at = pl.ds(0, own * rows)
            copies += start_all([pltpu.make_async_copy(ysc.at[r, at], ys[r].at[at], ysem.at[r])])
    s = jax.nn.sigmoid(acc)
    at_ref[...] = (acc * s).T
    wait_all(ccopies)
    pg = (cot[...].astype(F32) * (s * (1.0 + acc * (1.0 - s)))).astype(BF)
    pg_ref[...] = pg
    k_of = lax.broadcasted_iota(jnp.int32, (share, width), 0) + first
    lots = bsem.shape[0]
    lot = peers // lots
    for q in range(peers):
        for c in range(cap):
            block = pg_ref[aligned(dst_ref[c, q], share), :]
            block = jnp.where(k_of < count_ref[c, q], block.astype(F32), 0.0).astype(BF)
            for h in range(halves):
                back[q, pl.ds((c * halves + h) * share, share), :] = block[:, h * LANES : (h + 1) * LANES]
        if (q + 1) % lot == 0:
            i = q // lot
            at = pl.ds(i * lot, lot)
            copies += start_all([pltpu.make_async_copy(back.at[at], back_ref.at[at], bsem.at[i])])
    cols = width // groups
    at = pl.ds(own * rows, rows)
    for r in range(groups):
        ysc[r, at, :] = pg
        copies += start_all([pltpu.make_async_copy(ysc.at[r, at] if r else ysc.at[r], ys[r].at[at] if r else ys[r], psem.at[r])])
        act_ref[r] = at_ref[aligned(turn(group0, r, groups), cols), :].astype(BF)
    wait_all(copies)


def score_body(
    cap, nblk, own, halves, pg_ref, dstv_ref, cnt_ref, x_ref, rel_ref, src_ref, c0, c1, c2, c3, table_ref,
    s0, s1, s2, s3, w_ref, xf, pf, ts, tab, cs, tsem,
):
    groups = tab.shape[0]
    nbase = groups * own
    width = tab.shape[2]
    peers = cnt_ref.shape[1]
    slots = cap * peers
    share = BLK // groups
    group0 = lax.axis_index("basis")
    first = group0 * share
    tcopies = start_all(table_copies(table_ref, tab, tsem))
    w_ref[...] = slot_weights(own, (c0, c1, c2, c3), line(rel_ref), line(src_ref), nblk, cs).astype(BF)
    widen(x_ref, xf, peers)
    pg = pg_ref[...]
    for b in range(nbase):
        if b % own == 0:
            tcopies[b // own].wait()
        base = tab[b // own, pl.ds((b % own) * width, width), :]
        p = lax.dot_general(pg, base, NT, preferred_element_type=F32)
        for n in range(nblk):
            put(pf, spaced(n * nbase + b, share), p[n * share : (n + 1) * share])
    cnt = line(cnt_ref)

    def one(k, acc):
        pk = get(pf, pl.ds(k, nblk * nbase, stride=share + GAP)).astype(BF)
        xk = slot_rows(xf, peers, cap, halves, share, k).astype(BF)
        t = lax.dot_general(pk, xk, NT, preferred_element_type=F32)
        return acc + jnp.where(cnt > first + k, t, 0.0)

    acc = lax.fori_loop(0, share, one, jnp.zeros((nblk * nbase, slots), F32), unroll=4)
    blk = line(dstv_ref)
    total = jnp.zeros((nbase, slots), F32)
    for n in range(nblk):
        total += jnp.where(blk == n, acc[n * nbase : (n + 1) * nbase], 0.0)
    ts[...] = total
    for r, out in enumerate((s0, s1, s2, s3)):
        out[...] = ts[aligned(turn(group0, r, groups), own), :]


def coef_body(rel_ref, s0, s1, s2, s3, out_ref):
    own, slots = s0.shape
    width = out_ref.shape[1]
    chunks = out_ref.shape[0] // own
    high, low = digits((s0[...] + s1[...]) + (s2[...] + s3[...]))
    both = jnp.concatenate([high.astype(F32), low.astype(F32)], axis=0).astype(BF)
    rel = rel_ref[...]
    parts = []
    for j in range(chunks):
        ids = lax.broadcasted_iota(jnp.int32, (width, slots), 0) + j * width
        hot = jnp.where(ids == rel, 1.0, 0.0).astype(BF)
        t = lax.dot_general(both, hot, NT, preferred_element_type=F32)
        parts.append(t[:own] + t[own:])
    out_ref[...] = jnp.concatenate(parts, axis=0).astype(BF)


def basis_body(own, rows, peers, y0, y1, y2, y3, keep_ref, send_ref, tmp, outf):
    ys = (y0, y1, y2, y3)
    width = y0.shape[1]
    part = keep_ref.shape[0]
    each = part // NX
    deep = part * NC // (own * peers)
    lines = own * deep
    nz = each // lines
    plane = NX * NC * deep
    pg = jnp.concatenate([y[pl.ds(own * rows, rows), :] for y in ys], axis=0)
    for b in range(own):
        m = jnp.concatenate([y[pl.ds(b * rows, rows), :] for y in ys], axis=0)
        t = lax.dot_general(m, pg, TN, preferred_element_type=F32)
        for z in range(nz):
            put(tmp, spaced(z, plane), t[z * plane : (z + 1) * plane])
        for c in range(NC):
            for x in range(NX):
                for d in range(deep):
                    put(
                        outf,
                        pl.ds((c * NX + x) * nz * (lines + GAP) + b * deep + d, nz, stride=lines + GAP),
                        get(tmp, pl.ds((x * NC + c) * deep + d, nz, stride=plane + GAP)),
                    )
    core = lax.axis_index("c")
    for i in range(NX * nz):
        keep_ref[pl.ds(i * lines, lines), :] = get(outf, spaced(core * (NX * nz) + i, lines)).astype(BF)
        send_ref[pl.ds(i * lines, lines), :] = get(outf, spaced((1 - core) * (NX * nz) + i, lines)).astype(BF)


def core_body(keep_ref, got_ref, coef_ref, other_ref, o0, o1, o2, o3, sums):
    part = keep_ref.shape[0]
    each = part // NX
    sums[...] = keep_ref[...].astype(F32) + got_ref[...].astype(F32)
    coef = (coef_ref[...].astype(F32) + other_ref[...].astype(F32)).astype(BF)
    for r, out in enumerate((o0, o1, o2, o3)):
        out[pl.ds(0, each), :] = sums[aligned(turn(lax.axis_index("x"), r, NX), each), :].astype(BF)
        out[pl.ds(each, coef.shape[0]), :] = coef


def x_body(i0, i1, i2, i3, out_ref, order):
    n = order.shape[1]
    each = i0.shape[0] - n
    nz = out_ref.shape[0]
    last = each // nz
    sums = sum(i[pl.ds(0, each), :].astype(F32) for i in (i0, i1, i2, i3))
    for r, i in zip(ORDER, (i0, i1, i2, i3)):
        order[turn(lax.axis_index("x"), -r, NX)] = i[pl.ds(each, n), :].astype(F32)
    coef = ((order[0] + order[1]) + (order[2] + order[3])).astype(BF)
    for z in range(nz):
        out_ref[z, pl.ds(0, last), :] = sums[z * last : (z + 1) * last].astype(BF)
        out_ref[z, pl.ds(last, n), :] = coef


def z_body(own, in_ref, basis_ref, coef_ref):
    nz, rows, width = in_ref.shape
    deep = basis_ref.shape[1]
    last = own * deep
    n = rows - last
    basis = jnp.zeros((last, width), F32)
    coef = jnp.zeros((n, width), F32)
    for z in range(nz):
        basis += in_ref[z, pl.ds(0, last), :].astype(F32)
        coef += in_ref[z, pl.ds(last, n), :].astype(F32)
    for b in range(own):
        basis_ref[b] = basis[b * deep : (b + 1) * deep]
    relations = coef_ref.shape[1]
    for j in range(n // own):
        size = min(width, relations - j * width)
        coef_ref[:, pl.ds(j * width, size)] = coef[j * own : (j + 1) * own, :size]


def bwd_body(
    cap, own, x_ref, w_ref, act_ref, pg_ref, sw_ref, table_ref, o0, o1, o2, o3, xf, mf, at_ref, tab, tsem
):
    groups = tab.shape[0]
    nbase = groups * own
    width = tab.shape[2]
    halves = width // LANES
    share = BLK // groups
    slots = w_ref.shape[1]
    peers = slots // cap
    nblk = w_ref.shape[0] // nbase
    tcopies = start_all(table_copies(table_ref, tab, tsem))
    widen(x_ref, xf, peers)
    w = w_ref[...]

    def one(k, c):
        xk = slot_rows(xf, peers, cap, halves, share, k).astype(BF)
        put(mf, pl.ds(k, w.shape[0], stride=share + GAP), jnp.dot(w, xk, preferred_element_type=F32))
        return c

    lax.fori_loop(0, share, one, 0, unroll=8)
    acc = lax.dot_general(sw_ref[...], pg_ref[...], NT, preferred_element_type=F32)
    wait_all(tcopies)
    for b in range(nbase):
        mb = rows_of(mf, b, nbase, nblk, share).astype(BF)
        base = tab[b // own, pl.ds((b % own) * width, width), :]
        acc += lax.dot_general(base, mb, NT, preferred_element_type=F32)
    at_ref[...] = acc
    cols = width // groups
    for r, out in enumerate((o0, o1, o2, o3)):
        out[0] = at_ref[aligned(turn(lax.axis_index("basis"), r, groups), cols), :].astype(BF)
        out[1] = act_ref[r]


def join_body(nblk, i0, i1, i2, i3, grad_ref, act_ref, order):
    groups = order.shape[0]
    share = BLK // groups
    for r, i in zip(ORDER, (i0, i1, i2, i3)):
        order[turn(lax.axis_index("basis"), -r, groups)] = i[...].astype(F32)
    for j, out in enumerate((grad_ref, act_ref)):
        for n in range(nblk):
            whole = jnp.concatenate([order[g, j, :, n * share : (n + 1) * share] for g in range(groups)], axis=1)
            out[:, n * BLK : (n + 1) * BLK] = whole.astype(BF)


def local(
    entity_rows,
    self_weight,
    bases,
    coefficients,
    send_block,
    edge_rel,
    edge_dst,
    edge_count,
    cotangent,
):
    peers = lax.axis_size(ENT)
    groups = lax.axis_size("basis")
    ent_dev, width = entity_rows.shape
    nblk = ent_dev // BLK
    own = bases.shape[0]
    nbase = own * groups
    relations = coefficients.shape[0]
    cap = send_block.shape[2]
    slots = peers * cap
    share = BLK // groups
    halves = width // LANES
    nz = lax.axis_size("z")
    rows = nblk * share
    dma = pltpu.SemaphoreType.DMA

    def over(axis, r, value):
        n = lax.axis_size(axis)
        return lax.ppermute(value, axis, [(i, (i + r) % n) for i in range(n)])

    def exchange(axis, values):
        return [over(axis, r, values[r]) if r else values[0] for r in ORDER]

    src, rel_out = send_block[0].T, edge_rel[0].T
    dst, cnt = edge_dst[:, 0, :].T, edge_count[:, 0, :].T

    per = cap * halves * share
    outgoing = call(
        functools.partial(take_body, share),
        hbm(peers, per + 8, LANES),
        [HB] * 3,
        [
            pltpu.SMEM((cap, peers), jnp.int32),
            pltpu.SMEM((cap, peers), jnp.int32),
            pltpu.VMEM((rows, width), BF),
            pltpu.VMEM((peers, per + 8, LANES), BF),
            dma((2,)),
            dma((nblk,)),
            dma((4,)),
        ],
        outs_in=HB,
    )(far(src), far(rel_out), far(entity_rows))
    incoming = lax.all_to_all(outgoing, ENT, split_axis=0, concat_axis=0, tiled=True)

    bases, _ = lax.optimization_barrier((bases, outgoing))
    table = lax.all_gather(bases.reshape(own * width, width), "basis")
    chunks = -(-relations // width)
    coef = jnp.pad(coefficients.astype(BF).T, ((0, 16 - own), (0, chunks * width - relations)))
    coef = coef.reshape(16, chunks, width).transpose(1, 0, 2).reshape(chunks * 16, width)
    coefs = [coef] + [over("basis", r, coef) for r in range(1, groups)]
    tables = pltpu.VMEM((groups, own * width, width), BF)
    incoming = incoming.reshape(peers * (per + 8), LANES)
    *ys, back, pg, rel_in, act = call(
        functools.partial(fwd_body, cap, nblk, own),
        (
            *[hbm((own + 1) * rows, width) for _ in range(groups)],
            hbm(peers, per, LANES),
            bf(rows, width),
            jax.ShapeDtypeStruct((1, slots), jnp.int32),
            bf(groups, width // groups, rows),
        ),
        [SM] * 2 + [VM] * 8 + [HB] * 3,
        [
            pltpu.VMEM((peers * (per + 8), LANES), F32),
            rows_scratch(nbase * nblk * (share + GAP), width),
            pltpu.VMEM((groups, own, slots), F32),
            pltpu.VMEM((width, rows), F32),
            tables,
            pltpu.VMEM((rows, width), BF),
            pltpu.VMEM((rows, width), BF),
            pltpu.VMEM((groups, (own + 1) * rows, width), BF),
            pltpu.VMEM((peers, per, LANES), BF),
            dma((groups,)),
            dma((nblk,)),
            dma((nblk,)),
            dma((groups,)),
            dma((groups,)),
            dma((4,)),
        ],
        limit=30,
        outs_in=(HB,) * (groups + 1) + (VM,) * 3,
    )(
        dst, cnt, incoming, dst, cnt, *coefs, self_weight, far(table),
        far(entity_rows), far(cotangent),
    )

    returned = lax.all_to_all(back, ENT, split_axis=0, concat_axis=0, tiled=True)
    ys = exchange("basis", ys)

    *scores, w_out = call(
        functools.partial(score_body, cap, nblk, own, halves),
        (*[jax.ShapeDtypeStruct((own, slots), F32) for _ in range(groups)], bf(nblk * nbase, slots)),
        [VM] * 10 + [HB],
        [
            pltpu.VMEM((peers * (per + 8), LANES), F32),
            rows_scratch(nbase * nblk * (share + GAP), width),
            pltpu.VMEM((nbase, slots), F32),
            tables,
            pltpu.VMEM((groups, own, slots), F32),
            dma((groups,)),
        ],
        limit=20,
        cost=COST,
    )(pg, dst, cnt, incoming, rel_out, src, *coefs, far(table))
    scores = [scores[0]] + [over("basis", r, scores[r]) for r in range(1, groups)]
    lot = chunks * own
    coef_part = call(coef_body, bf(lot, width), [VM] * 5, limit=4)(rel_in, *scores)

    ys = lax.optimization_barrier((*ys, scores[2], scores[3]))[:groups]
    part = own * width // NC
    keep, send = call(
        functools.partial(basis_body, own, rows, peers),
        (bf(part, width), bf(part, width)),
        [VM] * 4,
        [rows_scratch(2 * width, width), rows_scratch(2 * NC * part, width)],
        limit=12,
    )(*ys)
    got = over("c", 1, send)
    each = part // NX
    outs = call(
        core_body,
        tuple(bf(each + lot, width) for _ in range(NX)),
        [VM] * 4,
        [pltpu.VMEM((part, width), F32)],
        limit=8,
    )(keep, got, coef_part, over("c", 1, coef_part))
    ins = exchange("x", outs)

    grads = call(
        functools.partial(bwd_body, cap, own),
        tuple(bf(2, width // groups, rows) for _ in range(groups)),
        [VM] * 5 + [HB],
        [
            pltpu.VMEM((peers * (per + GAP), LANES), F32),
            rows_scratch(nbase * nblk * (share + GAP), width),
            pltpu.VMEM((width, rows), F32),
            tables,
            dma((groups,)),
        ],
        limit=20,
    )(returned.reshape(peers * per, LANES), w_out, act, pg, self_weight, far(table))

    last = each // nz
    out = call(
        x_body,
        bf(nz, last + lot, width),
        [VM] * NX,
        [pltpu.VMEM((NX, lot, width), F32)],
        limit=4,
    )(*ins)
    out = lax.all_to_all(out, "z", split_axis=0, concat_axis=0, tiled=True)
    grads = exchange("basis", grads)
    cols = width // groups
    entity_grad, activation = call(
        functools.partial(join_body, nblk),
        (bf(cols, ent_dev), bf(cols, ent_dev)),
        [VM] * groups,
        [pltpu.VMEM((groups, 2, cols, rows), F32)],
        limit=4,
    )(*grads)
    out, _ = lax.optimization_barrier((out, entity_grad))
    basis_grad, coef_grad = call(
        functools.partial(z_body, own),
        (jax.ShapeDtypeStruct((own, width // peers, width), F32), jax.ShapeDtypeStruct((own, relations), F32)),
        [VM],
        limit=4,
    )(out)
    return (activation.T, basis_grad, coef_grad.T, entity_grad.T)


def solution(mesh):
    nz = mesh.devices.shape[0] // (NX * NC)
    fine = Mesh(mesh.devices.reshape(nz, NX, NC, mesh.devices.shape[1]), (*ENT, "basis"))
    placed = (
        P(ENT, None),
        P(),
        P("basis", None, None),
        P(None, "basis"),
        P(ENT, None, None),
        P(ENT, None, None),
        P(None, ENT, None),
        P(None, ENT, None),
        P(ENT, None),
    )
    return jax.shard_map(
        local,
        mesh=fine,
        in_specs=placed,
        out_specs=(P(ENT, "basis"), P("basis", ENT, None), P(None, "basis"), P(ENT, "basis")),
        check_vma=False,
    )
```
